512 devices in a mesh: gx: 4 (over x), gy: 8 (over y), gz: 16 (over z, core).
Axes of the slice: x: 4, y: 8, z: 8, core: 2. Of those that a mesh axis runs over, the one named last changes fastest.
Arguments:
- source: float32 [32, 128, 2048], P('gx', 'gy', 'gz'), may hold values from -6 to 6
- state: float32 [32, 128, 2048], P('gx', 'gy', 'gz'), may hold values from -6 to 6
- log_coef: float32 [32, 128, 2048], P('gx', 'gy', 'gz'), may hold values from -1 to 1
- lateral: float32 [32, 128], P('gx', 'gy'), may hold values from -0.5 to 0.5
- owners: int32 [4, 8, 16], P('gx', 'gy'), may hold values from 0 to 15, as said below
Outputs:
- adjoint_field: float32 [32, 128, 2048], P('gx', 'gy', 'gz')
- lateral_gradient: float32 [32, 128], P('gx', ('gy', 'gz'))
The draws below stay inside these ranges and needn't reach their ends.
Inputs may be any that keep to these rules, and one draw needn't show every extreme that they name: Along each line, the devices with equal owners entries form a contiguous run of at most 4 devices, and every line has a run of exactly 4; the entry names the device that solves that run's level-2 system, which need not belong to the run; different runs of a line name different devices.
All inputs are finite; a program needn't handle non-finite values.
Results may differ from the reference program's by a relative error of at most 0.0003.
Values sent between devices are 32-bit elements; how exact they have to be, the bound alone decides.
No kernel may reach another device: no remote copies, remote signals or barrier semaphores. Data moves between devices by JAX's collectives and lax.ppermute only.
A program may use at most 64 MiB of HBM per device.

```python
import math
import jax
import jax.numpy as jnp
from jax import lax

CX = 8
CY = 16
CZ = 128
SWEEPS = 3
RUN = 4
ANISO = 200
NX = 32
NY = 128
NZ = 2048
N_GX = 4
N_GY = 8
N_GZ = 16


def draw_source(key, part):
    coord_y = jnp.arange(NY).astype(jnp.float32)[None, :, None] / NY
    base = jnp.clip(jax.random.normal(key, (NX, NY, NZ), jnp.float32), -5.0, 5.0)
    return base + 0.4 + 0.3 * jnp.cos(2.0 * math.pi * coord_y)


def draw_owners(key, part):
    first_key = jax.random.fold_in(key, 11)
    second_key = jax.random.fold_in(key, 12)
    lead = jax.random.randint(first_key, (N_GX, N_GY, 1), 0, min(N_GZ - RUN, RUN) + 1, dtype=jnp.int32)
    others = jax.random.randint(second_key, (N_GX, N_GY, N_GZ), 1, RUN + 1, dtype=jnp.int32)
    fixed_run = jnp.full((N_GX, N_GY, 1), RUN, jnp.int32)
    lengths = jnp.concatenate([lead, fixed_run, others[:, :, :N_GZ - 2]], axis=2)
    starts = jnp.concatenate([jnp.zeros((N_GX, N_GY, 1), jnp.int32), jnp.cumsum(lengths, axis=2)[:, :, :-1]], axis=2)
    places = jnp.arange(N_GZ).astype(jnp.int32)
    starts_wide = starts[:, :, None, :]
    before = starts_wide <= places[:, None]
    run_start = jnp.max(jnp.where(before, starts_wide, 0), axis=3).astype(jnp.int32)
    run_end = jnp.min(jnp.where(before, N_GZ, jnp.minimum(starts_wide, N_GZ)), axis=3).astype(jnp.int32)
    line_x = jnp.arange(N_GX).astype(jnp.int32)[:, None, None]
    line_y = jnp.arange(N_GY).astype(jnp.int32)[None, :, None]
    pattern = (line_x + line_y) % 3
    head_far = (run_start + N_GZ // 2) % N_GZ
    head_next = run_end % N_GZ
    head_prev = (run_start + N_GZ - 1) % N_GZ
    chosen = jnp.where(pattern == 0, head_far, jnp.where(pattern == 1, head_next, head_prev))
    return chosen.astype(jnp.int32)


def shard_levels(stream_key, extent, pieces, smallest, largest):
    factor_of = 1.0
    for axis_at, blocks in pieces:
        steps = jax.random.uniform(jax.random.fold_in(jax.random.fold_in(stream_key, 6), axis_at), (blocks,), jnp.float32, smallest / len(pieces), largest / len(pieces))
        factor_of = factor_of * jnp.repeat(jnp.exp(steps), extent[axis_at] // blocks).reshape((-1,) + (1,) * (len(extent) - 1 - axis_at))
    return factor_of


def bell_draw(rng, dims, scale, most, pieces=(), kind=jnp.bfloat16):
    gain = shard_levels(rng, dims, pieces, -0.22, 0.18) if pieces else 1.0
    values = jax.random.normal(rng, dims, jnp.float32) * scale * gain
    return jnp.minimum(jnp.maximum(values, -most), most).astype(kind)


def setup_inputs(seed: int = 0) -> dict:
    key_list = jax.random.split(jax.random.key(seed), 6)
    return {
        "source": draw_source(jax.random.fold_in(key_list[5], 71), 0),
        "state": bell_draw(key_list[1], (NX, NY, NZ), 1.0, 6.0, ((0, 4), (1, 8), (2, 16)), jnp.float32),
        "log_coef": jnp.clip(jax.random.uniform(key_list[2], (NX, NY, NZ), jnp.float32, -1.0, 1.0) * shard_levels(key_list[2], (NX, NY, NZ), ((0, 4), (1, 8), (2, 16)), -0.4, 0.0), -1.0, 1.0),
        "lateral": jnp.clip(jax.random.uniform(key_list[3], (NX, NY), jnp.float32, -0.5, 0.5) * shard_levels(key_list[3], (NX, NY), ((0, 4), (1, 8)), -0.4, 0.0), -0.5, 0.5),
        "owners": draw_owners(jax.random.fold_in(key_list[5], 71), 0),
    }


omega_relax = 0.8
neighbour_offsets = ((2, 1, 1), (0, 1, 1), (1, 2, 1), (1, 0, 1), (1, 1, 2), (1, 1, 0))

def neighbour(padded, offset, shape):
    return padded[offset[0]:offset[0] + shape[0], offset[1]:offset[1] + shape[1], offset[2]:offset[2] + shape[2]]

def face_scale(scale, order_index):
    if order_index >= 4:
        return scale * ANISO
    return scale

def level_weights(coef, scale):
    padded = jnp.pad(coef, 1, mode='edge')
    weights = []
    for order_index, offset in enumerate(neighbour_offsets):
        weights.append(face_scale(scale, order_index) * (0.5 * (coef + neighbour(padded, offset, coef.shape))))
    total = weights[0]
    for extra in weights[1:]:
        total = total + extra
    return (weights, total)

def operate(field, weights, total):
    padded = jnp.pad(field, 1)
    result = total * field
    for order_index, offset in enumerate(neighbour_offsets):
        result = result - weights[order_index] * neighbour(padded, offset, field.shape)
    return result

def smooth(field, rhs, weights, total, from_zero):
    remaining = SWEEPS
    if from_zero:
        field = omega_relax * rhs / total
        remaining = SWEEPS - 1
    for repeat in range(remaining):
        field = field + omega_relax * (rhs - operate(field, weights, total)) / total
    return field

def restrict(field):
    shape = field.shape
    return field.reshape(shape[0] // 2, 2, shape[1] // 2, 2, shape[2] // 2, 2).mean(axis=(1, 3, 5))

def prolong(field):
    shape = field.shape
    spread = jnp.broadcast_to(field[:, None, :, None, :, None], (shape[0], 2, shape[1], 2, shape[2], 2))
    return spread.reshape(2 * shape[0], 2 * shape[1], 2 * shape[2])

def line_solve(rhs, total, lower):
    upper = jnp.concatenate([lower[..., 1:], jnp.zeros_like(lower[..., :1])], axis=-1)
    solved = lax.linalg.tridiagonal_solve(-lower, total, -upper, rhs[..., None])
    return solved[..., 0]

def reference(source, state, log_coef, lateral, owners):
    coef = jnp.exp(log_coef + lateral[:, :, None])
    fine_weights, fine_total = level_weights(coef, 1.0)
    mid_coef = restrict(coef)
    mid_weights, mid_total = level_weights(mid_coef, 0.25)
    low_coef = restrict(mid_coef)
    low_weights, low_total = level_weights(low_coef, 0.0625)
    zeros_fine = jnp.zeros_like(source)
    adjoint = smooth(zeros_fine, source, fine_weights, fine_total, True)
    mid_rhs = restrict(source - operate(adjoint, fine_weights, fine_total))
    mid_field = smooth(jnp.zeros_like(mid_rhs), mid_rhs, mid_weights, mid_total, True)
    low_rhs = restrict(mid_rhs - operate(mid_field, mid_weights, mid_total))
    depth = jnp.arange(NZ // 4).astype(jnp.int32)
    block = (depth // (CZ // 4)).astype(jnp.int32)
    first = depth % (CZ // 4) == 0
    rows_line = (jnp.arange(NX // 4) // (CX // 4)).astype(jnp.int32)
    cols_line = (jnp.arange(NY // 4) // (CY // 4)).astype(jnp.int32)
    owner_cell = owners[rows_line[:, None, None], cols_line[None, :, None], block[None, None, :]]
    previous = jnp.maximum(block - 1, 0).astype(jnp.int32)
    owner_prev = owners[rows_line[:, None, None], cols_line[None, :, None], previous[None, None, :]]
    cut = first[None, None, :] & ((block == 0)[None, None, :] | (owner_cell != owner_prev))
    lower = jnp.where(cut, jnp.zeros_like(low_weights[5]), low_weights[5])
    correction = line_solve(low_rhs, low_total, lower)
    mid_field = smooth(mid_field + prolong(correction), mid_rhs, mid_weights, mid_total, False)
    adjoint = smooth(adjoint + prolong(mid_field), source, fine_weights, fine_total, False)
    adjoint_pad = jnp.pad(adjoint, 1)
    state_pad = jnp.pad(state, 1)
    inside_pad = jnp.pad(jnp.ones_like(adjoint), 1)
    grad_terms = jnp.zeros_like(adjoint)
    for offset in neighbour_offsets:
        raw = neighbour(inside_pad, offset, adjoint.shape)
        factor = jnp.where(raw == 0.0, 1.0, 0.5)
        grad_terms = grad_terms + factor * (adjoint - neighbour(adjoint_pad, offset, adjoint.shape)) * (state - neighbour(state_pad, offset, state.shape))
    summed = lax.optimization_barrier(jnp.sum(coef * grad_terms, axis=2))
    return (adjoint, summed * (-1.0 / math.sqrt(NZ)))
```

```python
import math

import jax
import jax.numpy as jnp
from jax import lax
from jax.experimental import pallas as pl
from jax.experimental.pallas import tpu as pltpu
from jax.sharding import PartitionSpec as P

CX, CY, CZ = 8, 16, 128
ANISO = 200.0
OMEGA = 0.8
HY = 12
HZ = 18
YE = CY + 2 * HY
ZE = 2 * CZ
YM = 24
ZM = CZ
XW = CX + 8
YW = CY + 8
HIGHEST = lax.Precision.HIGHEST


def iota(shape, dim):
    return lax.broadcasted_iota(jnp.int32, shape, dim)


def mm(a, b):
    return jnp.dot(a, b, precision=HIGHEST, preferred_element_type=jnp.float32)


def nxt(v, axis):
    return pltpu.roll(v, v.shape[axis] - 1, axis)


def prv(v, axis):
    return pltpu.roll(v, 1, axis)


def face(a, b):
    both = a + b
    return jnp.where(jnp.minimum(a, b) == 0.0, both, 0.5 * both)


def make_weights(c, wx, wy, wz, inv, planes, scale):
    wx[0] = scale * face(c[0], c[1])

    def step(x, carry):
        here = c[x + 1]
        fx = scale * face(here, c[x + 2])
        fy = scale * face(here, nxt(here, 0))
        fz = (scale * ANISO) * face(here, nxt(here, 1))
        wx[x + 1] = fx
        wy[x] = fy
        wz[x] = fz
        total = fx + wx[x] + fy + prv(fy, 0) + fz + prv(fz, 1)
        inv[x] = jnp.where(here > 0.0, OMEGA / total, 0.0)
        return carry

    lax.fori_loop(0, planes, step, 0)


def residual(v, b, wx, wy, wz, x, before):
    here = v[x + 1]
    fx = wx[x + 1] * (here - v[x + 2])
    fy = wy[x] * (here - nxt(here, 0))
    fz = wz[x] * (here - nxt(here, 1))
    flow = (fx - before) + (fy - prv(fy, 0)) + (fz - prv(fz, 1))
    return here, b[x] - flow, fx


def sweep(v, out, b, wx, wy, wz, inv, planes):
    def step(x, before):
        here, rest, fx = residual(v, b, wx, wy, wz, x, before)
        out[x + 1] = here + inv[x] * rest
        return fx

    lax.fori_loop(0, planes, step, wx[0] * (0.0 - v[1]))


def pack_z_kernel(line, src, c, state, down, up):
    gz = lax.axis_index("gz")
    cut = (line[gz] != line[jnp.minimum(gz + 1, 15)]).astype(jnp.float32)
    lane = iota((CX, CY, CZ), 2)
    s, k = src[...], pltpu.roll(c[...], 64, 2)
    t = pltpu.roll(state[...], 32, 2)
    zero = jnp.zeros_like(s)
    far = CZ - HZ
    coef = jnp.where((lane >= 64) & (lane < 64 + HZ), k, zero)
    down[...] = jnp.where(lane < HZ, s, jnp.where(lane == 32, t, coef))
    coef = jnp.where((lane >= far - 64) & (lane < 64), k, zero)
    coef = jnp.where(lane == 20, cut, coef)
    up[...] = jnp.where(lane >= far, s, jnp.where(lane == 31, t, coef))


def pack_y_kernel(g, state, up, down):
    row = iota((24, CZ), 0)

    def put(at, one, two):
        zero = jnp.zeros((8, CZ), jnp.float32)
        one = jnp.concatenate([one, zero], 0)
        two = jnp.concatenate([two, zero], 0)
        up[at] = jnp.where(row < HY, pltpu.roll(one, 20, 0), pltpu.roll(two, 8, 0))
        down[at] = jnp.where(row < HY, one, pltpu.roll(two, 12, 0))

    for s in range(4):
        for k in range(12):
            put(12 * s + k, g[s, 2 * k], g[s, 2 * k + 1])
    for k in range(4):
        put(48 + k, state[2 * k], state[2 * k + 1])


def rows_of(yp, own, yn, odd):
    row = iota((YE, CZ), 0)
    zero16 = jnp.zeros((16, CZ), jnp.float32)
    zero24 = jnp.zeros((24, CZ), jnp.float32)
    low = jnp.concatenate([yp, zero16], 0)
    high = jnp.concatenate([yn, zero16], 0)
    mid = pltpu.roll(jnp.concatenate([own, zero24], 0), HY, 0)
    if odd:
        low = pltpu.roll(low, YE - HY, 0)
        high = pltpu.roll(high, HY + CY - HY, 0)
    else:
        high = pltpu.roll(high, HY + CY, 0)
    return jnp.where(row < HY, low, jnp.where(row < HY + CY, mid, high))


def first_kernel(
    g, yp, yn, state,
    src_w, pre_w, c_w, se, mid_pre_o, mid_rhs_o, mid_c_o, low_o,
    c, wx, wy, wz, inv, b, va, vb, t, mc, mwx, mwy, mwz, minv, mb, mva, mvb, lc,
):
    gx, gz = lax.axis_index("gx"), lax.axis_index("gz")
    zero = jnp.zeros((YE, ZE), jnp.float32)
    nx = 4 * CX
    for ref in (c, va, vb):
        ref[0] = zero
        ref[nx + 1] = zero
    lane = iota((YE, CZ), 1)
    edge = (lane < HZ) | (lane >= CZ - HZ)

    for s in range(4):
        for i in range(0, CX, 2):
            for odd in (0, 1):
                x = CX * s + i + odd
                near = [
                    rows_of(yp[12 * s + (a * CX + i) // 2], g[s, a * CX + i + odd],
                            yn[12 * s + (a * CX + i) // 2], odd)
                    for a in range(3)
                ]
                halo = near[2]
                b[x] = jnp.concatenate([near[0], jnp.where(edge, halo, 0.0)], 1)
                other = pltpu.roll(halo, 64, 1)
                c[x + 1] = jnp.concatenate([near[1], jnp.where(edge, other, 0.0)], 1)

    make_weights(c, wx, wy, wz, inv, nx, 1.0)

    def start(x, carry):
        va[x + 1] = inv[x] * b[x]
        return carry

    lax.fori_loop(0, nx, start, 0)
    sweep(va, vb, b, wx, wy, wz, inv, nx)
    sweep(vb, va, b, wx, wy, wz, inv, nx)

    fold_y = (iota((YM, YE), 1) // 2 + 2 == iota((YM, YE), 0)).astype(jnp.float32)
    fold_z = (iota((ZE, ZM), 0) // 2 == iota((ZE, ZM), 1)).astype(jnp.float32) * 0.125

    def coarse(m, before):
        x = 2 * m
        _, one, fx = residual(va, b, wx, wy, wz, x, before)
        _, two, fx = residual(va, b, wx, wy, wz, x + 1, fx)
        t[m] = mm(fold_y, one + two)
        t[m + 16] = mm(fold_y, c[x + 1] + c[x + 2])
        return fx

    lax.fori_loop(0, 16, coarse, wx[0] * (0.0 - va[1]))
    both = mm(t[...].reshape(32 * YM, ZE), fold_z).reshape(32, YM, ZM)
    mb[...] = both[:16]
    mid_rhs_o[...] = both[:16]
    mid_zero = jnp.zeros((YM, ZM), jnp.float32)
    for ref in (mc, mva, mvb):
        ref[0] = mid_zero
        ref[17] = mid_zero
    mc[1:17] = both[16:]
    mid_c_o[...] = both[16:]

    def keep(w, carry):
        x = CX * gx - 4 + w
        inside = (x >= 0) & (x < nx)
        x = jnp.clip(x, 0, nx - 1)
        src_w[w] = jnp.where(inside, b[x, 8:32], 0.0)
        pre_w[w] = jnp.where(inside, va[x + 1, 8:32], 0.0)
        c_w[w] = jnp.where(inside, c[x + 1, 8:32], 0.0)
        return carry

    lax.fori_loop(0, XW, keep, 0)

    zero8 = jnp.zeros((8, CZ), jnp.float32)
    wide = jnp.zeros((YW, CZ), jnp.float32)
    row = iota((YW, CZ), 0)
    lane = iota((YW, CZ), 1)
    left = g[jnp.maximum(gx - 1, 0), 25]
    right = g[jnp.minimum(gx + 1, 3), 24]
    left = jnp.where(gx > 0, left, 0.0)
    right = jnp.where(gx < 3, right, 0.0)
    for at, plane in ((0, left), (9, right)):
        mid = pltpu.roll(jnp.concatenate([plane, zero8], 0), 4, 0)
        se[at] = jnp.concatenate([mid, wide], 1)
    for i in range(CX):
        mid = pltpu.roll(jnp.concatenate([state[i], zero8], 0), 4, 0)
        low, high = yp[48 + i // 2], yn[48 + i // 2]
        low = pltpu.roll(low, (3 - 11 - 12 * (i % 2)) % 24, 0)
        high = pltpu.roll(high, (20 - 12 * (i % 2)) % 24, 0)
        mid = jnp.where(row == 3, low, jnp.where(row == 20, high, mid))
        halo = pltpu.roll(jnp.concatenate([g[gx, 16 + i], zero8], 0), 4, 0)
        halo = pltpu.roll(halo, CZ - 32, 1)
        halo = jnp.where((lane == 0) | (lane == CZ - 1), halo, 0.0)
        se[i + 1] = jnp.concatenate([mid, halo], 1)

    make_weights(mc, mwx, mwy, mwz, minv, 16, 0.25)
    mva[1:17] = minv[...] * mb[...]
    sweep(mva, mvb, mb, mwx, mwy, mwz, minv, 16)
    sweep(mvb, mva, mb, mwx, mwy, mwz, minv, 16)

    def rest(x, before):
        _, r, fx = residual(mva, mb, mwx, mwy, mwz, x, before)
        mvb[x + 1] = r
        mid_pre_o[x] = mva[x + 1, 8:16]
        return fx

    lax.fori_loop(0, 16, rest, mwx[0] * (0.0 - mva[1]))

    shape = (64, 16 * YM)
    to, frm = iota(shape, 0), iota(shape, 1)
    m, r = frm // YM, frm % YM
    fold = ((m // 2 == to // 8) & (r // 2 - 2 == to % 8)).astype(jnp.float32) * 0.125
    m, l = iota((ZM, CZ), 0), iota((ZM, CZ), 1)
    m = jnp.where(m < 96, m, m - 128)
    squeeze = ((m + 8) // 2 == l).astype(jnp.float32)
    rhs = mm(mm(fold, mvb[1:17].reshape(16 * YM, ZM)), squeeze).reshape(8, 8, CZ)
    low_c = mm(mm(fold, mc[1:17].reshape(16 * YM, ZM)), squeeze).reshape(8, 8, CZ)
    lc[0] = jnp.zeros((8, CZ), jnp.float32)
    lc[9] = jnp.zeros((8, CZ), jnp.float32)
    lc[1:9] = low_c
    scale = 0.0625
    fx0 = scale * face(lc[0:8], low_c)
    fx1 = scale * face(low_c, lc[2:10])
    fy = scale * face(low_c, nxt(low_c, 1))
    fz = (scale * ANISO) * face(low_c, nxt(low_c, 2))
    lower = prv(fz, 2)
    total = fx1 + fx0 + fy + prv(fy, 1) + fz + lower
    flags = [pltpu.roll(g[s, 16, 0:8], CZ - 16, 1) for s in range(4)]
    flags = jnp.stack([flags[x // 2] for x in range(8)])
    lane = iota((8, 8, CZ), 2)
    lower = jnp.where((lane == 4) & ((flags > 0.0) | (gz == 0)), 0.0, lower)
    packed = jnp.where(
        lane < 32, pltpu.roll(rhs, CZ - 4, 2),
        jnp.where(lane < 64, pltpu.roll(total, 28, 2), pltpu.roll(lower, 60, 2)),
    )
    packed = jnp.where(lane < 96, packed, 0.0).reshape(64, CZ)
    to, frm = iota((32, 64), 0), iota((32, 64), 1)
    pick = ((to // 4 == frm // 8) & (to % 4 + 2 == frm % 8)).astype(jnp.float32)
    packed = mm(pick, packed)
    for p in range(16):
        low_o[p] = packed


def solve_kernel(rec, mid_pre, out):
    gz = lax.axis_index("gz")
    lane = iota((32, CZ), 1)
    parts = [[], [], []]
    for tile in range(4):
        pieces = [jnp.zeros((32, CZ), jnp.float32)] * 3
        for j in range(4):
            block = rec[4 * tile + j]
            here = (lane >= 32 * j) & (lane < 32 * j + 32)
            for a in range(3):
                shift = (32 * (j - a)) % CZ
                moved = pltpu.roll(block, shift, 1) if shift else block
                pieces[a] = jnp.where(here, moved, pieces[a])
        for a in range(3):
            parts[a].append(pieces[a])
    r, d, e = [jnp.concatenate(p, 1) for p in parts]
    for k in range(7):
        s = 1 << k
        back = 4 * CZ - s
        inv = 1.0 / d
        t = e * inv
        alpha = e * pltpu.roll(inv, s, 1)
        d = d - alpha * e - pltpu.roll(t * e, back, 1)
        r = r + alpha * pltpu.roll(r, s, 1) + pltpu.roll(t * r, back, 1)
        e = alpha * pltpu.roll(e, s, 1)
    x = r / d
    k, m = iota((4 * CZ, ZM), 0), iota((4 * CZ, ZM), 1)
    m = jnp.where(m < 96, m, m - 128)
    spread_z = (k == 32 * gz + ((m + 64) // 2 - 32)).astype(jnp.float32)
    to, frm = iota((128, 32), 0), iota((128, 32), 1)
    spread = ((to // 16 == frm // 4) & ((to % 8) // 2 == frm % 4)).astype(jnp.float32)
    out[...] = mid_pre[...] + mm(spread, mm(x, spread_z)).reshape(16, 8, ZM)


def second_kernel(
    mid, mid_p, mid_n, mid_rhs, mid_c, src_w, pre_w, c_w, se,
    adj, grad,
    mc, mwx, mwy, mwz, minv, mva, mvb, sp, c, wx, wy, wz, inv, va, vb,
):
    gx = lax.axis_index("gx")
    mid_zero = jnp.zeros((YM, ZM), jnp.float32)
    mc[0] = mid_zero
    mc[17] = mid_zero
    mc[1:17] = mid_c[...]
    make_weights(mc, mwx, mwy, mwz, minv, 16, 0.25)
    for ref in (mva, mvb):
        for at in (0, 1, 18, 19):
            ref[at] = mid_zero
    for x in range(16):
        mva[x + 2] = jnp.concatenate([mid_p[x], mid[x], mid_n[x]], 0)
    a, o = mva.at[1:19], mvb.at[1:19]
    sweep(a, o, mid_rhs, mwx, mwy, mwz, minv, 16)
    sweep(o, a, mid_rhs, mwx, mwy, mwz, minv, 16)
    sweep(a, o, mid_rhs, mwx, mwy, mwz, minv, 16)

    zero = jnp.zeros((YW, ZE), jnp.float32)
    for ref in (c, va, vb):
        ref[0] = zero
        ref[XW + 1] = zero
    c[1 : XW + 1] = c_w[...]
    make_weights(c, wx, wy, wz, inv, XW, 1.0)
    spread_z = (iota((ZM, ZE), 1) // 2 == iota((ZM, ZE), 0)).astype(jnp.float32)
    spread_y = ((iota((YW, YM), 0) + 12) // 2 == iota((YW, YM), 1)).astype(jnp.float32)
    near = mvb[pl.ds(4 * gx, 8)]
    sp[...] = mm(near.reshape(8 * YM, ZM), spread_z).reshape(8, YM, ZE)
    for m in range(8):
        more = mm(spread_y, sp[m])
        for x in (2 * m, 2 * m + 1):
            va[x + 1] = pre_w[x] + more
    sweep(va, vb, src_w, wx, wy, wz, inv, XW)
    sweep(vb, va, src_w, wx, wy, wz, inv, XW)
    sweep(va, vb, src_w, wx, wy, wz, inv, XW)

    def product(f, one, two, sone, stwo):
        return f * (one - two) * (sone - stwo)

    def half(one, two):
        return jnp.where(jnp.minimum(one, two) == 0.0, 1.0, 0.5)

    lane = iota((YW, CZ), 1)

    def terms(i, carry):
        before, acc = carry
        v, k, s = vb[i + 5], c[i + 5], se[i + 1]
        px = product(half(k, c[i + 6]), v, vb[i + 6], s, se[i + 2])
        py = product(half(k, nxt(k, 0)), v, nxt(v, 0), s, nxt(s, 0))
        pz = product(half(k, nxt(k, 1)), v, nxt(v, 1), s, nxt(s, 1))
        both = k * (px + before + py + prv(py, 0) + pz + prv(pz, 1))
        part = jnp.sum(both[:, :CZ], axis=1, keepdims=True)
        acc = jnp.where(lane == i, part, acc)
        adj[i] = pltpu.roll(v, YW - 4, 0)[:CY, :CZ]
        return px, acc

    first = product(half(c[4], c[5]), vb[4], vb[5], se[0], se[1])
    _, acc = lax.fori_loop(0, CX, terms, (first, jnp.zeros((YW, CZ), jnp.float32)))
    grad[...] = pltpu.roll(acc, YW - 4, 0)[:CY]


def f32(*shape):
    return jax.ShapeDtypeStruct(shape, jnp.float32)


def vm(*shape):
    return pltpu.VMEM(shape, jnp.float32)


def params():
    return pltpu.CompilerParams(vmem_limit_bytes=48 << 20)


def both_ways(up, down, axis):
    count = lax.axis_size(axis)
    higher = [(i, i + 1) for i in range(count - 1)]
    lower = [(j, i) for i, j in higher]
    return lax.ppermute(up, axis, higher), lax.ppermute(down, axis, lower)


def per_device(source, state, log_coef, lateral, owners):
    coef = jnp.exp(log_coef + lateral[:, :, None])
    block = f32(CX, CY, CZ)
    smem = pl.BlockSpec(memory_space=pltpu.SMEM)
    vmem = pl.BlockSpec(memory_space=pltpu.VMEM)
    down, up = pl.pallas_call(
        pack_z_kernel,
        out_shape=(block, block),
        in_specs=[smem, vmem, vmem, vmem],
        name="pack_z",
    )(owners[0, 0], source, coef, state)
    before, after = both_ways(up, down, "gz")
    mine = jnp.concatenate([source, coef, before + after, state[:1], state[CX - 1 :]], 0)
    g = lax.all_gather(mine, "gx")
    pair = f32(52, 24, CZ)
    up, down = pl.pallas_call(
        pack_y_kernel, out_shape=(pair, pair), compiler_params=params(), name="pack_y"
    )(g, state)
    yp, yn = both_ways(up, down, "gy")

    fine, fine1, fine2 = (32, YE, ZE), (33, YE, ZE), (34, YE, ZE)
    mid, mid1, mid2 = (16, YM, ZM), (17, YM, ZM), (18, YM, ZM)
    win, win1, win2 = (XW, YW, ZE), (XW + 1, YW, ZE), (XW + 2, YW, ZE)
    src_w, pre_w, c_w, se, mid_pre, mid_rhs, mid_c, low = pl.pallas_call(
        first_kernel,
        out_shape=(
            f32(*win), f32(*win), f32(*win), f32(CX + 2, YW, ZE),
            f32(16, 8, ZM), f32(*mid), f32(*mid), f32(16, 32, CZ),
        ),
        scratch_shapes=[
            vm(*fine2), vm(*fine1), vm(*fine), vm(*fine), vm(*fine), vm(*fine),
            vm(*fine2), vm(*fine2), vm(32, YM, ZE),
            vm(*mid2), vm(*mid1), vm(*mid), vm(*mid), vm(*mid), vm(*mid),
            vm(*mid2), vm(*mid2), vm(10, 8, CZ),
        ],
        compiler_params=params(),
        name="first",
    )(g, yp, yn, state)

    rec = lax.all_to_all(low, "gz", 0, 0, tiled=True)
    mid_init = pl.pallas_call(
        solve_kernel, out_shape=f32(16, 8, ZM), compiler_params=params(), name="solve"
    )(rec, mid_pre)
    mid_p, mid_n = both_ways(mid_init, mid_init, "gy")

    adj, grad = pl.pallas_call(
        second_kernel,
        out_shape=(block, f32(CY, CZ)),
        scratch_shapes=[
            vm(*mid2), vm(*mid1), vm(*mid), vm(*mid), vm(*mid),
            vm(20, YM, ZM), vm(20, YM, ZM), vm(8, YM, ZE),
            vm(*win2), vm(*win1), vm(*win), vm(*win), vm(*win), vm(*win2), vm(*win2),
        ],
        compiler_params=params(),
        name="second",
    )(mid_init, mid_p, mid_n, mid_rhs, mid_c, src_w, pre_w, c_w, se)
    sums = lax.all_to_all(grad, "gz", 0, 0, tiled=True)
    total = jnp.sum(sums[:, :CX], axis=0)[:, None]
    return adj, total * (-1.0 / math.sqrt(source.shape[2] * lax.axis_size("gz")))


def solution(mesh):
    placed = (
        P("gx", "gy", "gz"),
        P("gx", "gy", "gz"),
        P("gx", "gy", "gz"),
        P("gx", "gy"),
        P("gx", "gy", None),
    )
    return jax.shard_map(
        per_device,
        mesh=mesh,
        in_specs=placed,
        out_specs=(P("gx", "gy", "gz"), P("gx", ("gy", "gz"))),
        check_vma=False,
    )
```

```python
import math

import jax
import jax.numpy as jnp
from jax import lax
from jax.experimental import pallas as pl
from jax.experimental.pallas import tpu as pltpu
from jax.sharding import PartitionSpec as P

CX, CY, CZ = 8, 16, 128
ANISO = 200.0
OMEGA = 0.8
HY = 12
HZ = 18
YE = CY + 2 * HY
ZE = 2 * CZ
YM = 24
ZM = CZ
XW = CX + 8
YW = CY + 8
HIGHEST = lax.Precision.HIGHEST


def iota(shape, dim):
    return lax.broadcasted_iota(jnp.int32, shape, dim)


def mm(a, b):
    return jnp.dot(a, b, precision=HIGHEST, preferred_element_type=jnp.float32)


def nxt(v, axis):
    return pltpu.roll(v, v.shape[axis] - 1, axis)


def prv(v, axis):
    return pltpu.roll(v, 1, axis)


def face(a, b):
    both = a + b
    return jnp.where(jnp.minimum(a, b) == 0.0, both, 0.5 * both)


def unroll(planes):
    return 16 if planes == 16 else 8


def make_weights(c, wx, wy, wz, inv, planes, scale):
    wx[0] = scale * face(c[0], c[1])

    def step(x, carry):
        here = c[x + 1]
        fx = scale * face(here, c[x + 2])
        fy = scale * face(here, nxt(here, 0))
        fz = (scale * ANISO) * face(here, nxt(here, 1))
        wx[x + 1] = fx
        wy[x] = fy
        wz[x] = fz
        total = fx + wx[x] + fy + prv(fy, 0) + fz + prv(fz, 1)
        inv[x] = jnp.where(here > 0.0, OMEGA / total, 0.0)
        return carry

    lax.fori_loop(0, planes, step, 0, unroll=unroll(planes))


def residual(v, b, wx, wy, wz, x, before):
    here = v[x + 1]
    fx = wx[x + 1] * (here - v[x + 2])
    fy = wy[x] * (here - nxt(here, 0))
    fz = wz[x] * (here - nxt(here, 1))
    flow = (fx - before) + (fy - prv(fy, 0)) + (fz - prv(fz, 1))
    return here, b[x] - flow, fx


def sweep(v, out, b, wx, wy, wz, inv, planes):
    def step(x, before):
        here, rest, fx = residual(v, b, wx, wy, wz, x, before)
        out[x + 1] = here + inv[x] * rest
        return fx

    lax.fori_loop(0, planes, step, wx[0] * (0.0 - v[1]), unroll=unroll(planes))


def pack_z_kernel(line, src, log_coef, lateral, state, mine, down, up):
    gz = lax.axis_index("gz")
    cut = (line[gz] != line[jnp.minimum(gz + 1, 15)]).astype(jnp.float32)
    pick = (iota((CX * CY, CX), 0) // CY == iota((CX * CY, CX), 1)).astype(jnp.float32)
    rows = mm(pick, lateral[...])
    own = iota((CX * CY, CY), 0) % CY == iota((CX * CY, CY), 1)
    rows = jnp.sum(jnp.where(own, rows, 0.0), axis=1, keepdims=True)
    rows = jnp.broadcast_to(rows, (CX * CY, CZ)).reshape(CX, CY, CZ)
    c = jnp.exp(log_coef[...] + rows)
    s = src[...]
    mine[0:CX] = s
    mine[CX : 2 * CX] = c
    mine[3 * CX] = state[0]
    mine[3 * CX + 1] = state[CX - 1]
    lane = iota((CX, CY, CZ), 2)
    k = pltpu.roll(c, 64, 2)
    t = pltpu.roll(state[...], 32, 2)
    zero = jnp.zeros_like(s)
    far = CZ - HZ
    coef = jnp.where((lane >= 64) & (lane < 64 + HZ), k, zero)
    down[...] = jnp.where(lane < HZ, s, jnp.where(lane == 32, t, coef))
    coef = jnp.where((lane >= far - 64) & (lane < 64), k, zero)
    coef = jnp.where(lane == 20, cut, coef)
    up[...] = jnp.where(lane >= far, s, jnp.where(lane == 31, t, coef))


def pack_y_kernel(g, state, up, down):
    row = iota((24, CZ), 0)

    def put(at, one, two):
        zero = jnp.zeros((8, CZ), jnp.float32)
        one = jnp.concatenate([one, zero], 0)
        two = jnp.concatenate([two, zero], 0)
        up[at] = jnp.where(row < HY, pltpu.roll(one, 20, 0), pltpu.roll(two, 8, 0))
        down[at] = jnp.where(row < HY, one, pltpu.roll(two, 12, 0))

    for s in range(4):
        for k in range(12):
            put(12 * s + k, g[s, 2 * k], g[s, 2 * k + 1])
    for k in range(4):
        put(48 + k, state[2 * k], state[2 * k + 1])


def rows_of(yp, own, yn, odd):
    row = iota((YE, CZ), 0)
    zero16 = jnp.zeros((16, CZ), jnp.float32)
    zero24 = jnp.zeros((24, CZ), jnp.float32)
    low = jnp.concatenate([yp, zero16], 0)
    high = jnp.concatenate([yn, zero16], 0)
    mid = pltpu.roll(jnp.concatenate([own, zero24], 0), HY, 0)
    if odd:
        low = pltpu.roll(low, YE - HY, 0)
        high = pltpu.roll(high, HY + CY - HY, 0)
    else:
        high = pltpu.roll(high, HY + CY, 0)
    return jnp.where(row < HY, low, jnp.where(row < HY + CY, mid, high))


def first_kernel(
    g, yp, yn, state,
    src_w, pre_w, c_w, se, mid_pre_o, mid_rhs_o, mid_c_o, low_o,
    c, wx, wy, wz, inv, b, va, vb, t, mc, mwx, mwy, mwz, minv, mb, mva, mvb, lc,
):
    gx, gz = lax.axis_index("gx"), lax.axis_index("gz")
    zero = jnp.zeros((YE, ZE), jnp.float32)
    nx = 4 * CX
    for ref in (c, va, vb):
        ref[0] = zero
        ref[nx + 1] = zero
    lane = iota((YE, CZ), 1)
    edge = (lane < HZ) | (lane >= CZ - HZ)

    for s in range(4):
        for i in range(0, CX, 2):
            for odd in (0, 1):
                x = CX * s + i + odd
                near = [
                    rows_of(yp[12 * s + (a * CX + i) // 2], g[s, a * CX + i + odd],
                            yn[12 * s + (a * CX + i) // 2], odd)
                    for a in range(3)
                ]
                halo = near[2]
                b[x] = jnp.concatenate([near[0], jnp.where(edge, halo, 0.0)], 1)
                other = pltpu.roll(halo, 64, 1)
                c[x + 1] = jnp.concatenate([near[1], jnp.where(edge, other, 0.0)], 1)

    make_weights(c, wx, wy, wz, inv, nx, 1.0)

    def start(x, carry):
        va[x + 1] = inv[x] * b[x]
        return carry

    lax.fori_loop(0, nx, start, 0, unroll=4)
    sweep(va, vb, b, wx, wy, wz, inv, nx)
    sweep(vb, va, b, wx, wy, wz, inv, nx)

    fold_y = (iota((YM, YE), 1) // 2 + 2 == iota((YM, YE), 0)).astype(jnp.float32)
    fold_z = (iota((ZE, ZM), 0) // 2 == iota((ZE, ZM), 1)).astype(jnp.float32) * 0.125

    def coarse(m, before):
        x = 2 * m
        _, one, fx = residual(va, b, wx, wy, wz, x, before)
        _, two, fx = residual(va, b, wx, wy, wz, x + 1, fx)
        t[m] = mm(fold_y, one + two)
        t[m + 16] = mm(fold_y, c[x + 1] + c[x + 2])
        return fx

    lax.fori_loop(0, 16, coarse, wx[0] * (0.0 - va[1]), unroll=8)
    both = mm(t[...].reshape(32 * YM, ZE), fold_z).reshape(32, YM, ZM)
    mb[...] = both[:16]
    mid_rhs_o[...] = both[:16]
    mid_zero = jnp.zeros((YM, ZM), jnp.float32)
    for ref in (mc, mva, mvb):
        ref[0] = mid_zero
        ref[17] = mid_zero
    mc[1:17] = both[16:]
    mid_c_o[...] = both[16:]

    def keep(w, carry):
        x = CX * gx - 4 + w
        inside = (x >= 0) & (x < nx)
        x = jnp.clip(x, 0, nx - 1)
        src_w[w] = jnp.where(inside, b[x, 8:32], 0.0)
        pre_w[w] = jnp.where(inside, va[x + 1, 8:32], 0.0)
        c_w[w] = jnp.where(inside, c[x + 1, 8:32], 0.0)
        return carry

    lax.fori_loop(0, XW, keep, 0, unroll=4)

    zero8 = jnp.zeros((8, CZ), jnp.float32)
    wide = jnp.zeros((YW, CZ), jnp.float32)
    row = iota((YW, CZ), 0)
    lane = iota((YW, CZ), 1)
    left = g[jnp.maximum(gx - 1, 0), 25]
    right = g[jnp.minimum(gx + 1, 3), 24]
    left = jnp.where(gx > 0, left, 0.0)
    right = jnp.where(gx < 3, right, 0.0)
    for at, plane in ((0, left), (9, right)):
        mid = pltpu.roll(jnp.concatenate([plane, zero8], 0), 4, 0)
        se[at] = jnp.concatenate([mid, wide], 1)
    for i in range(CX):
        mid = pltpu.roll(jnp.concatenate([state[i], zero8], 0), 4, 0)
        low, high = yp[48 + i // 2], yn[48 + i // 2]
        low = pltpu.roll(low, (3 - 11 - 12 * (i % 2)) % 24, 0)
        high = pltpu.roll(high, (20 - 12 * (i % 2)) % 24, 0)
        mid = jnp.where(row == 3, low, jnp.where(row == 20, high, mid))
        halo = pltpu.roll(jnp.concatenate([g[gx, 16 + i], zero8], 0), 4, 0)
        halo = pltpu.roll(halo, CZ - 32, 1)
        halo = jnp.where((lane == 0) | (lane == CZ - 1), halo, 0.0)
        se[i + 1] = jnp.concatenate([mid, halo], 1)

    make_weights(mc, mwx, mwy, mwz, minv, 16, 0.25)
    mva[1:17] = minv[...] * mb[...]
    sweep(mva, mvb, mb, mwx, mwy, mwz, minv, 16)
    sweep(mvb, mva, mb, mwx, mwy, mwz, minv, 16)

    def rest(x, before):
        _, r, fx = residual(mva, mb, mwx, mwy, mwz, x, before)
        mvb[x + 1] = r
        mid_pre_o[x] = mva[x + 1, 8:16]
        return fx

    lax.fori_loop(0, 16, rest, mwx[0] * (0.0 - mva[1]), unroll=16)

    shape = (64, 16 * YM)
    to, frm = iota(shape, 0), iota(shape, 1)
    m, r = frm // YM, frm % YM
    fold = ((m // 2 == to // 8) & (r // 2 - 2 == to % 8)).astype(jnp.float32) * 0.125
    m, l = iota((ZM, CZ), 0), iota((ZM, CZ), 1)
    m = jnp.where(m < 96, m, m - 128)
    squeeze = ((m + 8) // 2 == l).astype(jnp.float32)
    rhs = mm(mm(fold, mvb[1:17].reshape(16 * YM, ZM)), squeeze).reshape(8, 8, CZ)
    low_c = mm(mm(fold, mc[1:17].reshape(16 * YM, ZM)), squeeze).reshape(8, 8, CZ)
    lc[0] = jnp.zeros((8, CZ), jnp.float32)
    lc[9] = jnp.zeros((8, CZ), jnp.float32)
    lc[1:9] = low_c
    scale = 0.0625
    fx0 = scale * face(lc[0:8], low_c)
    fx1 = scale * face(low_c, lc[2:10])
    fy = scale * face(low_c, nxt(low_c, 1))
    fz = (scale * ANISO) * face(low_c, nxt(low_c, 2))
    lower = prv(fz, 2)
    total = fx1 + fx0 + fy + prv(fy, 1) + fz + lower
    flags = [pltpu.roll(g[s, 16, 0:8], CZ - 16, 1) for s in range(4)]
    flags = jnp.stack([flags[x // 2] for x in range(8)])
    lane = iota((8, 8, CZ), 2)
    lower = jnp.where((lane == 4) & ((flags > 0.0) | (gz == 0)), 0.0, lower)
    packed = jnp.where(
        lane < 32, pltpu.roll(rhs, CZ - 4, 2),
        jnp.where(lane < 64, pltpu.roll(total, 28, 2), pltpu.roll(lower, 60, 2)),
    )
    packed = jnp.where(lane < 96, packed, 0.0).reshape(64, CZ)
    to, frm = iota((32, 64), 0), iota((32, 64), 1)
    pick = ((to // 4 == frm // 8) & (to % 4 + 2 == frm % 8)).astype(jnp.float32)
    packed = mm(pick, packed)
    for p in range(16):
        low_o[p] = packed


def solve_kernel(rec, mid_pre, out):
    gz = lax.axis_index("gz")
    lane = iota((32, CZ), 1)
    parts = [[], [], []]
    for tile in range(4):
        pieces = [jnp.zeros((32, CZ), jnp.float32)] * 3
        for j in range(4):
            block = rec[4 * tile + j]
            here = (lane >= 32 * j) & (lane < 32 * j + 32)
            for a in range(3):
                shift = (32 * (j - a)) % CZ
                moved = pltpu.roll(block, shift, 1) if shift else block
                pieces[a] = jnp.where(here, moved, pieces[a])
        for a in range(3):
            parts[a].append(pieces[a])
    r, d, e = [jnp.concatenate(p, 1) for p in parts]
    for k in range(7):
        s = 1 << k
        back = 4 * CZ - s
        inv = 1.0 / d
        t = e * inv
        alpha = e * pltpu.roll(inv, s, 1)
        d = d - alpha * e - pltpu.roll(t * e, back, 1)
        r = r + alpha * pltpu.roll(r, s, 1) + pltpu.roll(t * r, back, 1)
        e = alpha * pltpu.roll(e, s, 1)
    x = r / d
    k, m = iota((4 * CZ, ZM), 0), iota((4 * CZ, ZM), 1)
    m = jnp.where(m < 96, m, m - 128)
    spread_z = (k == 32 * gz + ((m + 64) // 2 - 32)).astype(jnp.float32)
    to, frm = iota((128, 32), 0), iota((128, 32), 1)
    spread = ((to // 16 == frm // 4) & ((to % 8) // 2 == frm % 4)).astype(jnp.float32)
    out[...] = mid_pre[...] + mm(spread, mm(x, spread_z)).reshape(16, 8, ZM)


def second_kernel(
    mid, mid_p, mid_n, mid_rhs, mid_c, src_w, pre_w, c_w, se,
    adj, grad,
    mc, mwx, mwy, mwz, minv, mva, mvb, sp, c, wx, wy, wz, inv, va, vb,
):
    gx = lax.axis_index("gx")
    mid_zero = jnp.zeros((YM, ZM), jnp.float32)
    mc[0] = mid_zero
    mc[17] = mid_zero
    mc[1:17] = mid_c[...]
    make_weights(mc, mwx, mwy, mwz, minv, 16, 0.25)
    for ref in (mva, mvb):
        for at in (0, 1, 18, 19):
            ref[at] = mid_zero
    for x in range(16):
        mva[x + 2] = jnp.concatenate([mid_p[x], mid[x], mid_n[x]], 0)
    a, o = mva.at[1:19], mvb.at[1:19]
    sweep(a, o, mid_rhs, mwx, mwy, mwz, minv, 16)
    sweep(o, a, mid_rhs, mwx, mwy, mwz, minv, 16)
    sweep(a, o, mid_rhs, mwx, mwy, mwz, minv, 16)

    zero = jnp.zeros((YW, ZE), jnp.float32)
    for ref in (c, va, vb):
        ref[0] = zero
        ref[XW + 1] = zero
    c[1 : XW + 1] = c_w[...]
    make_weights(c, wx, wy, wz, inv, XW, 1.0)
    spread_z = (iota((ZM, ZE), 1) // 2 == iota((ZM, ZE), 0)).astype(jnp.float32)
    spread_y = ((iota((YW, YM), 0) + 12) // 2 == iota((YW, YM), 1)).astype(jnp.float32)
    near = mvb[pl.ds(4 * gx, 8)]
    sp[...] = mm(near.reshape(8 * YM, ZM), spread_z).reshape(8, YM, ZE)
    for m in range(8):
        more = mm(spread_y, sp[m])
        for x in (2 * m, 2 * m + 1):
            va[x + 1] = pre_w[x] + more
    sweep(va, vb, src_w, wx, wy, wz, inv, XW)
    sweep(vb, va, src_w, wx, wy, wz, inv, XW)
    sweep(va, vb, src_w, wx, wy, wz, inv, XW)

    def product(f, one, two, sone, stwo):
        return f * (one - two) * (sone - stwo)

    def half(one, two):
        return jnp.where(jnp.minimum(one, two) == 0.0, 1.0, 0.5)

    lane = iota((YW, CZ), 1)

    def terms(i, carry):
        before, acc = carry
        v, k, s = vb[i + 5], c[i + 5], se[i + 1]
        px = product(half(k, c[i + 6]), v, vb[i + 6], s, se[i + 2])
        py = product(half(k, nxt(k, 0)), v, nxt(v, 0), s, nxt(s, 0))
        pz = product(half(k, nxt(k, 1)), v, nxt(v, 1), s, nxt(s, 1))
        both = k * (px + before + py + prv(py, 0) + pz + prv(pz, 1))
        part = jnp.sum(both[:, :CZ], axis=1, keepdims=True)
        acc = jnp.where(lane == i, part, acc)
        adj[i] = pltpu.roll(v, YW - 4, 0)[:CY, :CZ]
        return px, acc

    first = product(half(c[4], c[5]), vb[4], vb[5], se[0], se[1])
    _, acc = lax.fori_loop(
        0, CX, terms, (first, jnp.zeros((YW, CZ), jnp.float32)), unroll=8
    )
    grad[...] = pltpu.roll(acc, YW - 4, 0)[:CY]


def f32(*shape):
    return jax.ShapeDtypeStruct(shape, jnp.float32)


def vm(*shape):
    return pltpu.VMEM(shape, jnp.float32)


def params():
    return pltpu.CompilerParams(vmem_limit_bytes=48 << 20)


def both_ways(up, down, axis):
    count = lax.axis_size(axis)
    higher = [(i, i + 1) for i in range(count - 1)]
    lower = [(j, i) for i, j in higher]
    return lax.ppermute(up, axis, higher), lax.ppermute(down, axis, lower)


def per_device(source, state, log_coef, lateral, owners):
    block = f32(CX, CY, CZ)
    smem = pl.BlockSpec(memory_space=pltpu.SMEM)
    vmem = pl.BlockSpec(memory_space=pltpu.VMEM)
    mine, down, up = pl.pallas_call(
        pack_z_kernel,
        out_shape=(f32(3 * CX + 2, CY, CZ), block, block),
        in_specs=[smem, vmem, vmem, vmem, vmem],
        name="pack_z",
    )(owners[0, 0], source, log_coef, lateral, state)
    gz, count = lax.axis_index("gz"), lax.axis_size("gz")
    before = lax.ppermute(up, "gz", [(i, (i + 1) % count) for i in range(count)])
    after = lax.ppermute(down, "gz", [(i, (i - 1) % count) for i in range(count)])
    halo = jnp.where(gz > 0, before, 0.0) + jnp.where(gz < count - 1, after, 0.0)
    mine = lax.dynamic_update_slice(mine, halo, (2 * CX, 0, 0))
    g = lax.all_gather(mine, "gx")
    pair = f32(52, 24, CZ)
    up, down = pl.pallas_call(
        pack_y_kernel, out_shape=(pair, pair), compiler_params=params(), name="pack_y"
    )(g, state)
    yp, yn = both_ways(up, down, "gy")

    fine, fine1, fine2 = (32, YE, ZE), (33, YE, ZE), (34, YE, ZE)
    mid, mid1, mid2 = (16, YM, ZM), (17, YM, ZM), (18, YM, ZM)
    win, win1, win2 = (XW, YW, ZE), (XW + 1, YW, ZE), (XW + 2, YW, ZE)
    src_w, pre_w, c_w, se, mid_pre, mid_rhs, mid_c, low = pl.pallas_call(
        first_kernel,
        out_shape=(
            f32(*win), f32(*win), f32(*win), f32(CX + 2, YW, ZE),
            f32(16, 8, ZM), f32(*mid), f32(*mid), f32(16, 32, CZ),
        ),
        scratch_shapes=[
            vm(*fine2), vm(*fine1), vm(*fine), vm(*fine), vm(*fine), vm(*fine),
            vm(*fine2), vm(*fine2), vm(32, YM, ZE),
            vm(*mid2), vm(*mid1), vm(*mid), vm(*mid), vm(*mid), vm(*mid),
            vm(*mid2), vm(*mid2), vm(10, 8, CZ),
        ],
        compiler_params=params(),
        name="first",
    )(g, yp, yn, state)

    rec = lax.all_to_all(low, "gz", 0, 0, tiled=True)
    mid_init = pl.pallas_call(
        solve_kernel, out_shape=f32(16, 8, ZM), compiler_params=params(), name="solve"
    )(rec, mid_pre)
    mid_p, mid_n = both_ways(mid_init, mid_init, "gy")

    adj, grad = pl.pallas_call(
        second_kernel,
        out_shape=(block, f32(CY, CZ)),
        scratch_shapes=[
            vm(*mid2), vm(*mid1), vm(*mid), vm(*mid), vm(*mid),
            vm(20, YM, ZM), vm(20, YM, ZM), vm(8, YM, ZE),
            vm(*win2), vm(*win1), vm(*win), vm(*win), vm(*win), vm(*win2), vm(*win2),
        ],
        compiler_params=params(),
        name="second",
    )(mid_init, mid_p, mid_n, mid_rhs, mid_c, src_w, pre_w, c_w, se)
    sums = lax.all_to_all(grad, "gz", 0, 0, tiled=True)
    total = jnp.sum(sums[:, :CX], axis=0)[:, None]
    return adj, total * (-1.0 / math.sqrt(source.shape[2] * lax.axis_size("gz")))


def solution(mesh):
    placed = (
        P("gx", "gy", "gz"),
        P("gx", "gy", "gz"),
        P("gx", "gy", "gz"),
        P("gx", "gy"),
        P("gx", "gy", None),
    )
    return jax.shard_map(
        per_device,
        mesh=mesh,
        in_specs=placed,
        out_specs=(P("gx", "gy", "gz"), P("gx", ("gy", "gz"))),
        check_vma=False,
    )
```

```python
import math

import jax
import jax.numpy as jnp
from jax import lax
from jax.experimental import pallas as pl
from jax.experimental.pallas import tpu as pltpu
from jax.sharding import PartitionSpec as P

CX, CY, CZ = 8, 16, 128
ANISO = 200.0
OMEGA = 0.8
HY = 12
HZ = 18
YE = CY + 2 * HY
ZE = 2 * CZ
YM = 24
ZM = CZ
XW = CX + 8
YW = CY + 8
HIGHEST = lax.Precision.HIGHEST


def iota(shape, dim):
    return lax.broadcasted_iota(jnp.int32, shape, dim)


def mm(a, b):
    return jnp.dot(a, b, precision=HIGHEST, preferred_element_type=jnp.float32)


def nxt(v, axis):
    return pltpu.roll(v, v.shape[axis] - 1, axis)


def prv(v, axis):
    return pltpu.roll(v, 1, axis)


def face(a, b):
    both = a + b
    return jnp.where(jnp.minimum(a, b) == 0.0, both, 0.5 * both)


def unroll(planes):
    return 16 if planes == 16 else 8


def make_weights(c, wx, wy, wz, inv, planes, scale):
    wx[0] = scale * face(c[0], c[1])

    def step(x, carry):
        here = c[x + 1]
        fx = scale * face(here, c[x + 2])
        fy = scale * face(here, nxt(here, 0))
        fz = (scale * ANISO) * face(here, nxt(here, 1))
        wx[x + 1] = fx
        wy[x] = fy
        wz[x] = fz
        total = fx + wx[x] + fy + prv(fy, 0) + fz + prv(fz, 1)
        inv[x] = jnp.where(here > 0.0, OMEGA / total, 0.0)
        return carry

    lax.fori_loop(0, planes, step, 0, unroll=unroll(planes))


def residual(v, b, wx, wy, wz, x, before):
    here = v[x + 1]
    fx = wx[x + 1] * (here - v[x + 2])
    fy = wy[x] * (here - nxt(here, 0))
    fz = wz[x] * (here - nxt(here, 1))
    flow = (fx - before) + (fy - prv(fy, 0)) + (fz - prv(fz, 1))
    return here, b[x] - flow, fx


def sweep(v, out, b, wx, wy, wz, inv, planes):
    def step(x, before):
        here, rest, fx = residual(v, b, wx, wy, wz, x, before)
        out[x + 1] = here + inv[x] * rest
        return fx

    lax.fori_loop(0, planes, step, wx[0] * (0.0 - v[1]), unroll=unroll(planes))


def pack_z_kernel(line, src, log_coef, lateral, state, mine, down, up):
    gz = lax.axis_index("gz")
    cut = (line[gz] != line[jnp.minimum(gz + 1, 15)]).astype(jnp.float32)
    pick = (iota((CX * CY, CX), 0) // CY == iota((CX * CY, CX), 1)).astype(jnp.float32)
    rows = mm(pick, lateral[...])
    own = iota((CX * CY, CY), 0) % CY == iota((CX * CY, CY), 1)
    rows = jnp.sum(jnp.where(own, rows, 0.0), axis=1, keepdims=True)
    rows = jnp.broadcast_to(rows, (CX * CY, CZ)).reshape(CX, CY, CZ)
    c = jnp.exp(log_coef[...] + rows)
    s = src[...]
    mine[0:CX] = s
    mine[CX : 2 * CX] = c
    mine[3 * CX] = state[0]
    mine[3 * CX + 1] = state[CX - 1]
    lane = iota((CX, CY, CZ), 2)
    k = pltpu.roll(c, 64, 2)
    t = pltpu.roll(state[...], 32, 2)
    zero = jnp.zeros_like(s)
    far = CZ - HZ
    coef = jnp.where((lane >= 64) & (lane < 64 + HZ), k, zero)
    down[...] = jnp.where(lane < HZ, s, jnp.where(lane == 32, t, coef))
    coef = jnp.where((lane >= far - 64) & (lane < 64), k, zero)
    coef = jnp.where(lane == 20, cut, coef)
    up[...] = jnp.where(lane >= far, s, jnp.where(lane == 31, t, coef))


def pack_y_kernel(g, state, up, down):
    row = iota((24, CZ), 0)

    def put(at, one, two):
        zero = jnp.zeros((8, CZ), jnp.float32)
        one = jnp.concatenate([one, zero], 0)
        two = jnp.concatenate([two, zero], 0)
        up[at] = jnp.where(row < HY, pltpu.roll(one, 20, 0), pltpu.roll(two, 8, 0))
        down[at] = jnp.where(row < HY, one, pltpu.roll(two, 12, 0))

    for s in range(4):
        for k in range(12):
            put(12 * s + k, g[s, 2 * k], g[s, 2 * k + 1])
    for k in range(4):
        put(48 + k, state[2 * k], state[2 * k + 1])


def rows_of(yp, own, yn, odd):
    row = iota((YE, CZ), 0)
    zero16 = jnp.zeros((16, CZ), jnp.float32)
    zero24 = jnp.zeros((24, CZ), jnp.float32)
    low = jnp.concatenate([yp, zero16], 0)
    high = jnp.concatenate([yn, zero16], 0)
    mid = pltpu.roll(jnp.concatenate([own, zero24], 0), HY, 0)
    if odd:
        low = pltpu.roll(low, YE - HY, 0)
        high = pltpu.roll(high, HY + CY - HY, 0)
    else:
        high = pltpu.roll(high, HY + CY, 0)
    return jnp.where(row < HY, low, jnp.where(row < HY + CY, mid, high))


def first_kernel(
    g, yp, yn, state,
    src_w, pre_w, c_w, se, mid_pre_o, mid_rhs_o, mid_c_o, low_o, block_o,
    c, wx, wy, wz, inv, b, va, vb, t, mc, mwx, mwy, mwz, minv, mb, mva, mvb,
):
    gx, gz = lax.axis_index("gx"), lax.axis_index("gz")
    zero = jnp.zeros((YE, ZE), jnp.float32)
    nx = 4 * CX
    for ref in (c, va, vb):
        ref[0] = zero
        ref[nx + 1] = zero
    lane = iota((YE, CZ), 1)
    edge = (lane < HZ) | (lane >= CZ - HZ)

    for s in range(4):
        for i in range(0, CX, 2):
            for odd in (0, 1):
                x = CX * s + i + odd
                near = [
                    rows_of(yp[12 * s + (a * CX + i) // 2], g[s, a * CX + i + odd],
                            yn[12 * s + (a * CX + i) // 2], odd)
                    for a in range(3)
                ]
                halo = near[2]
                b[x] = jnp.concatenate([near[0], jnp.where(edge, halo, 0.0)], 1)
                other = pltpu.roll(halo, 64, 1)
                c[x + 1] = jnp.concatenate([near[1], jnp.where(edge, other, 0.0)], 1)

    make_weights(c, wx, wy, wz, inv, nx, 1.0)

    def start(x, carry):
        va[x + 1] = inv[x] * b[x]
        return carry

    lax.fori_loop(0, nx, start, 0, unroll=4)
    sweep(va, vb, b, wx, wy, wz, inv, nx)
    sweep(vb, va, b, wx, wy, wz, inv, nx)

    fold_y = (iota((YM, YE), 1) // 2 + 2 == iota((YM, YE), 0)).astype(jnp.float32)
    fold_z = (iota((ZE, ZM), 0) // 2 == iota((ZE, ZM), 1)).astype(jnp.float32) * 0.125

    def coarse(m, before):
        x = 2 * m
        _, one, fx = residual(va, b, wx, wy, wz, x, before)
        _, two, fx = residual(va, b, wx, wy, wz, x + 1, fx)
        t[m] = mm(fold_y, one + two)
        t[m + 16] = mm(fold_y, c[x + 1] + c[x + 2])
        return fx

    lax.fori_loop(0, 16, coarse, wx[0] * (0.0 - va[1]), unroll=8)
    both = mm(t[...].reshape(32 * YM, ZE), fold_z).reshape(32, YM, ZM)
    mb[...] = both[:16]
    mid_rhs_o[...] = both[:16]
    mid_zero = jnp.zeros((YM, ZM), jnp.float32)
    for ref in (mc, mva, mvb):
        ref[0] = mid_zero
        ref[17] = mid_zero
    mc[1:17] = both[16:]
    mid_c_o[...] = both[16:]

    def keep(w, carry):
        x = CX * gx - 4 + w
        inside = (x >= 0) & (x < nx)
        x = jnp.clip(x, 0, nx - 1)
        src_w[w] = jnp.where(inside, b[x, 8:32], 0.0)
        pre_w[w] = jnp.where(inside, va[x + 1, 8:32], 0.0)
        c_w[w] = jnp.where(inside, c[x + 1, 8:32], 0.0)
        return carry

    lax.fori_loop(0, XW, keep, 0, unroll=4)

    zero8 = jnp.zeros((8, CZ), jnp.float32)
    wide = jnp.zeros((YW, CZ), jnp.float32)
    row = iota((YW, CZ), 0)
    lane = iota((YW, CZ), 1)
    left = g[jnp.maximum(gx - 1, 0), 25]
    right = g[jnp.minimum(gx + 1, 3), 24]
    left = jnp.where(gx > 0, left, 0.0)
    right = jnp.where(gx < 3, right, 0.0)
    for at, plane in ((0, left), (9, right)):
        mid = pltpu.roll(jnp.concatenate([plane, zero8], 0), 4, 0)
        se[at] = jnp.concatenate([mid, wide], 1)
    for i in range(CX):
        mid = pltpu.roll(jnp.concatenate([state[i], zero8], 0), 4, 0)
        low, high = yp[48 + i // 2], yn[48 + i // 2]
        low = pltpu.roll(low, (3 - 11 - 12 * (i % 2)) % 24, 0)
        high = pltpu.roll(high, (20 - 12 * (i % 2)) % 24, 0)
        mid = jnp.where(row == 3, low, jnp.where(row == 20, high, mid))
        halo = pltpu.roll(jnp.concatenate([g[gx, 16 + i], zero8], 0), 4, 0)
        halo = pltpu.roll(halo, CZ - 32, 1)
        halo = jnp.where((lane == 0) | (lane == CZ - 1), halo, 0.0)
        se[i + 1] = jnp.concatenate([mid, halo], 1)

    make_weights(mc, mwx, mwy, mwz, minv, 16, 0.25)
    mva[1:17] = minv[...] * mb[...]
    sweep(mva, mvb, mb, mwx, mwy, mwz, minv, 16)
    sweep(mvb, mva, mb, mwx, mwy, mwz, minv, 16)

    def rest(x, before):
        _, r, fx = residual(mva, mb, mwx, mwy, mwz, x, before)
        mvb[x + 1] = r
        mid_pre_o[x] = mva[x + 1, 8:16]
        return fx

    lax.fori_loop(0, 16, rest, mwx[0] * (0.0 - mva[1]), unroll=16)

    shape = (48, 16 * YM)
    to, frm = iota(shape, 0), iota(shape, 1)
    m, r = frm // YM, frm % YM
    fold = ((m // 2 == to % 8) & (r // 2 - 3 == to // 8)).astype(jnp.float32) * 0.125
    m, l = iota((ZM, CZ), 0), iota((ZM, CZ), 1)
    m = jnp.where(m < 96, m, m - 128)
    squeeze = ((m + 8) // 2 == l).astype(jnp.float32)
    rhs = mm(mm(fold[8:40], mvb[1:17].reshape(16 * YM, ZM)), squeeze).reshape(4, 8, CZ)
    low_c = mm(mm(fold, mc[1:17].reshape(16 * YM, ZM)), squeeze).reshape(6, 8, CZ)
    here = low_c[1:5]
    row = iota((4, 8, CZ), 1)
    scale = 0.0625
    fx1 = scale * face(here, jnp.where(row < 7, nxt(here, 1), 0.0))
    fx0 = scale * face(here, jnp.where(row > 0, prv(here, 1), 0.0))
    fy1 = scale * face(here, low_c[2:6])
    fy0 = scale * face(here, low_c[0:4])
    fz = (scale * ANISO) * face(here, nxt(here, 2))
    lower = prv(fz, 2)
    total = fx1 + fx0 + fy1 + fy0 + fz + lower

    lane = iota((8, CZ), 1)
    depth = lane % 32

    def gather(v):
        out = pltpu.roll(v[0], CZ - 4, 1)
        for y in range(1, 4):
            out = jnp.where(lane >= 32 * y, pltpu.roll(v[y], 32 * y - 4, 1), out)
        return out

    flag = pltpu.roll(g[3, 16, 0:8], CZ - 20, 1)
    row = iota((8, CZ), 0)
    for s in range(2, -1, -1):
        flag = jnp.where(row < 2 * s + 2, pltpu.roll(g[s, 16, 0:8], CZ - 20, 1), flag)
    flag = jnp.broadcast_to(flag[:, 0:1], (8, CZ))
    r, d, e = gather(rhs), gather(total), gather(lower)
    top = depth == 0
    edge = jnp.where(top & (flag == 0.0) & (gz > 0), e, 0.0)
    e = jnp.where(top, 0.0, e)
    v = jnp.where(top, 1.0, 0.0)
    w = jnp.where(depth == 31, 1.0, 0.0)
    for k in range(5):
        s = 1 << k
        back = CZ - s
        inv = 1.0 / d
        t = e * inv
        alpha = e * pltpu.roll(inv, s, 1)
        r, v, w = [
            q + alpha * pltpu.roll(q, s, 1) + pltpu.roll(t * q, back, 1) for q in (r, v, w)
        ]
        d = d - alpha * e - pltpu.roll(t * e, back, 1)
        e = alpha * pltpu.roll(e, s, 1)
    inv = 1.0 / d
    r, v, w = r * inv, v * inv, w * inv
    block_o[0] = r
    block_o[1] = v
    block_o[2] = w
    packed = jnp.where((depth < 3) | (depth >= 29), r, 0.0)
    packed = jnp.where((depth >= 3) & (depth < 6), pltpu.roll(v, 3, 1), packed)
    packed = jnp.where((depth >= 26) & (depth < 29), pltpu.roll(v, CZ - 3, 1), packed)
    packed = jnp.where((depth >= 6) & (depth < 9), pltpu.roll(w, 6, 1), packed)
    packed = jnp.where((depth >= 23) & (depth < 26), pltpu.roll(w, CZ - 6, 1), packed)
    packed = jnp.where(depth == 9, pltpu.roll(edge, 9, 1), packed)
    for p in range(16):
        low_o[p] = packed


def solve_kernel(rec, block, mid_pre, out):
    gz = lax.axis_index("gz")
    lane = iota((8, CZ), 1)
    depth = lane % 32

    def take(v, at):
        return pltpu.roll(v, (CZ - at) % CZ, 1) if at else v

    def parts(offset):
        p = gz + offset
        v = rec[jnp.clip(p, 0, 15)]
        low = take(v, 0), take(v, 3), take(v, 6)
        high = take(v, 31), take(v, 28), take(v, 25)
        return v, low, high, jnp.where((p >= 0) & (p <= 15), take(v, 9), 0.0)

    every = {k: parts(k) for k in range(-4, 5)}
    zero = jnp.zeros((8, CZ), jnp.float32)

    a, b = {-5: zero}, {-5: zero}
    f, g = {}, {}
    for k in range(-4, 1):
        _, (y0, v0, w0), (y1, v1, w1), e = every[k]
        left, more = e * a[k - 1], e * e * b[k - 1]
        den = 1.0 / (1.0 - v0 * more)
        f[k] = (y0 + v0 * left) * den
        g[k] = w0 * den
        a[k] = y1 + v1 * (left + more * f[k])
        b[k] = w1 + v1 * (more * g[k])
    ra, rb = {5: zero}, {5: zero}
    rf, rg = {}, {}
    e_next = zero
    for k in range(4, 0, -1):
        _, (y0, v0, w0), (y1, v1, w1), e = every[k]
        right, more = e_next * ra[k + 1], e_next * e_next * rb[k + 1]
        den = 1.0 / (1.0 - w1 * more)
        rf[k] = (y1 + w1 * right) * den
        rg[k] = v1 * den
        ra[k] = y0 + w0 * (right + more * rf[k])
        rb[k] = v0 + w0 * (more * rg[k])
        e_next = e
    e0, e1 = every[0][3], every[1][3]
    last = (a[0] + b[0] * e1 * ra[1]) / (1.0 - b[0] * e1 * e1 * rb[1])
    right = e1 * (ra[1] + rb[1] * (e1 * last))
    first = f[0] + g[0] * right
    left = e0 * (a[-1] + b[-1] * (e0 * first))
    before = f[-1] + g[-1] * (e0 * first)
    em = every[-1][3]
    left_m, right_m = em * (a[-2] + b[-2] * (em * before)), e0 * first
    after = rf[1] + rg[1] * (e1 * last)
    ep = every[2][3]
    left_p, right_p = e1 * last, ep * (ra[2] + rb[2] * (ep * after))

    ends = jnp.concatenate([left, right, left_m, right_m, left_p, right_p], 0)
    ends = jnp.where(iota((48, CZ), 1) % 32 == 0, ends, 0.0)
    copy = (iota((CZ, CZ), 1) // 32 * 32 == iota((CZ, CZ), 0)).astype(jnp.float32)
    ends = mm(ends, copy).reshape(6, 8, CZ)
    own = block[0] + block[1] * ends[0] + block[2] * ends[1]
    v = every[-1][0]
    low = v + pltpu.roll(v, 3, 1) * ends[2] + pltpu.roll(v, 6, 1) * ends[3]
    low = jnp.where((depth >= 29) & (gz > 0), low, 0.0)
    v = every[1][0]
    high = v + pltpu.roll(v, CZ - 3, 1) * ends[4] + pltpu.roll(v, CZ - 6, 1) * ends[5]
    high = jnp.where((depth < 3) & (gz < 15), high, 0.0)

    rows = []
    for y in range(4):
        part = jnp.where(lane < 32, take(own, 32 * y), 0.0)
        part = jnp.where((lane >= 32) & (lane < 64), take(high, (32 * y - 32) % CZ), part)
        part = jnp.where(lane >= 96, take(low, (32 * y + 32) % CZ), part)
        rows.append(part)
    rows = jnp.concatenate(rows, 0)
    k, m = iota((CZ, ZM), 0), iota((CZ, ZM), 1)
    spread_z = (k == jnp.where(m < 96, m // 2, m // 2 + 64)).astype(jnp.float32)
    to, frm = iota((128, 32), 0), iota((128, 32), 1)
    spread = ((to // 16 == frm % 8) & ((to % 8) // 2 == frm // 8)).astype(jnp.float32)
    out[...] = mid_pre[...] + mm(spread, mm(rows, spread_z)).reshape(16, 8, ZM)


def second_kernel(
    mid, mid_p, mid_n, mid_rhs, mid_c, src_w, pre_w, c_w, se,
    adj, grad,
    mc, mwx, mwy, mwz, minv, mva, mvb, sp, c, wx, wy, wz, inv, va, vb,
):
    gx = lax.axis_index("gx")
    mid_zero = jnp.zeros((YM, ZM), jnp.float32)
    mc[0] = mid_zero
    mc[17] = mid_zero
    mc[1:17] = mid_c[...]
    make_weights(mc, mwx, mwy, mwz, minv, 16, 0.25)
    for ref in (mva, mvb):
        for at in (0, 1, 18, 19):
            ref[at] = mid_zero
    for x in range(16):
        mva[x + 2] = jnp.concatenate([mid_p[x], mid[x], mid_n[x]], 0)
    a, o = mva.at[1:19], mvb.at[1:19]
    sweep(a, o, mid_rhs, mwx, mwy, mwz, minv, 16)
    sweep(o, a, mid_rhs, mwx, mwy, mwz, minv, 16)
    sweep(a, o, mid_rhs, mwx, mwy, mwz, minv, 16)

    zero = jnp.zeros((YW, ZE), jnp.float32)
    for ref in (c, va, vb):
        ref[0] = zero
        ref[XW + 1] = zero
    c[1 : XW + 1] = c_w[...]
    make_weights(c, wx, wy, wz, inv, XW, 1.0)
    spread_z = (iota((ZM, ZE), 1) // 2 == iota((ZM, ZE), 0)).astype(jnp.float32)
    spread_y = ((iota((YW, YM), 0) + 12) // 2 == iota((YW, YM), 1)).astype(jnp.float32)
    near = mvb[pl.ds(4 * gx, 8)]
    sp[...] = mm(near.reshape(8 * YM, ZM), spread_z).reshape(8, YM, ZE)
    for m in range(8):
        more = mm(spread_y, sp[m])
        for x in (2 * m, 2 * m + 1):
            va[x + 1] = pre_w[x] + more
    sweep(va, vb, src_w, wx, wy, wz, inv, XW)
    sweep(vb, va, src_w, wx, wy, wz, inv, XW)
    sweep(va, vb, src_w, wx, wy, wz, inv, XW)

    def product(f, one, two, sone, stwo):
        return f * (one - two) * (sone - stwo)

    def half(one, two):
        return jnp.where(jnp.minimum(one, two) == 0.0, 1.0, 0.5)

    lane = iota((YW, CZ), 1)

    def terms(i, carry):
        before, acc = carry
        v, k, s = vb[i + 5], c[i + 5], se[i + 1]
        px = product(half(k, c[i + 6]), v, vb[i + 6], s, se[i + 2])
        py = product(half(k, nxt(k, 0)), v, nxt(v, 0), s, nxt(s, 0))
        pz = product(half(k, nxt(k, 1)), v, nxt(v, 1), s, nxt(s, 1))
        both = k * (px + before + py + prv(py, 0) + pz + prv(pz, 1))
        part = jnp.sum(both[:, :CZ], axis=1, keepdims=True)
        acc = jnp.where(lane == i, part, acc)
        adj[i] = pltpu.roll(v, YW - 4, 0)[:CY, :CZ]
        return px, acc

    first = product(half(c[4], c[5]), vb[4], vb[5], se[0], se[1])
    _, acc = lax.fori_loop(
        0, CX, terms, (first, jnp.zeros((YW, CZ), jnp.float32)), unroll=8
    )
    grad[...] = pltpu.roll(acc, YW - 4, 0)[:CY]


def f32(*shape):
    return jax.ShapeDtypeStruct(shape, jnp.float32)


def vm(*shape):
    return pltpu.VMEM(shape, jnp.float32)


def params():
    return pltpu.CompilerParams(vmem_limit_bytes=48 << 20)


def both_ways(up, down, axis):
    count = lax.axis_size(axis)
    higher = [(i, i + 1) for i in range(count - 1)]
    lower = [(j, i) for i, j in higher]
    return lax.ppermute(up, axis, higher), lax.ppermute(down, axis, lower)


def per_device(source, state, log_coef, lateral, owners):
    block = f32(CX, CY, CZ)
    smem = pl.BlockSpec(memory_space=pltpu.SMEM)
    vmem = pl.BlockSpec(memory_space=pltpu.VMEM)
    mine, down, up = pl.pallas_call(
        pack_z_kernel,
        out_shape=(f32(3 * CX + 2, CY, CZ), block, block),
        in_specs=[smem, vmem, vmem, vmem, vmem],
        name="pack_z",
    )(owners[0, 0], source, log_coef, lateral, state)
    gz, count = lax.axis_index("gz"), lax.axis_size("gz")
    before = lax.ppermute(up, "gz", [(i, (i + 1) % count) for i in range(count)])
    after = lax.ppermute(down, "gz", [(i, (i - 1) % count) for i in range(count)])
    halo = jnp.where(gz > 0, before, 0.0) + jnp.where(gz < count - 1, after, 0.0)
    mine = lax.dynamic_update_slice(mine, halo, (2 * CX, 0, 0))
    g = lax.all_gather(mine, "gx")
    pair = f32(52, 24, CZ)
    up, down = pl.pallas_call(
        pack_y_kernel, out_shape=(pair, pair), compiler_params=params(), name="pack_y"
    )(g, state)
    yp, yn = both_ways(up, down, "gy")

    fine, fine1, fine2 = (32, YE, ZE), (33, YE, ZE), (34, YE, ZE)
    mid, mid1, mid2 = (16, YM, ZM), (17, YM, ZM), (18, YM, ZM)
    win, win1, win2 = (XW, YW, ZE), (XW + 1, YW, ZE), (XW + 2, YW, ZE)
    src_w, pre_w, c_w, se, mid_pre, mid_rhs, mid_c, low, block_s = pl.pallas_call(
        first_kernel,
        out_shape=(
            f32(*win), f32(*win), f32(*win), f32(CX + 2, YW, ZE),
            f32(16, 8, ZM), f32(*mid), f32(*mid), f32(16, 8, CZ), f32(3, 8, CZ),
        ),
        scratch_shapes=[
            vm(*fine2), vm(*fine1), vm(*fine), vm(*fine), vm(*fine), vm(*fine),
            vm(*fine2), vm(*fine2), vm(32, YM, ZE),
            vm(*mid2), vm(*mid1), vm(*mid), vm(*mid), vm(*mid), vm(*mid),
            vm(*mid2), vm(*mid2),
        ],
        compiler_params=params(),
        name="first",
    )(g, yp, yn, state)

    rec = lax.all_to_all(low, "gz", 0, 0, tiled=True)
    mid_init = pl.pallas_call(
        solve_kernel, out_shape=f32(16, 8, ZM), compiler_params=params(), name="solve"
    )(rec, block_s, mid_pre)
    mid_p, mid_n = both_ways(mid_init, mid_init, "gy")

    adj, grad = pl.pallas_call(
        second_kernel,
        out_shape=(block, f32(CY, CZ)),
        scratch_shapes=[
            vm(*mid2), vm(*mid1), vm(*mid), vm(*mid), vm(*mid),
            vm(20, YM, ZM), vm(20, YM, ZM), vm(8, YM, ZE),
            vm(*win2), vm(*win1), vm(*win), vm(*win), vm(*win), vm(*win2), vm(*win2),
        ],
        compiler_params=params(),
        name="second",
    )(mid_init, mid_p, mid_n, mid_rhs, mid_c, src_w, pre_w, c_w, se)
    sums = lax.all_to_all(grad, "gz", 0, 0, tiled=True)
    total = jnp.sum(sums[:, :CX], axis=0)[:, None]
    return adj, total * (-1.0 / math.sqrt(source.shape[2] * lax.axis_size("gz")))


def solution(mesh):
    placed = (
        P("gx", "gy", "gz"),
        P("gx", "gy", "gz"),
        P("gx", "gy", "gz"),
        P("gx", "gy"),
        P("gx", "gy", None),
    )
    return jax.shard_map(
        per_device,
        mesh=mesh,
        in_specs=placed,
        out_specs=(P("gx", "gy", "gz"), P("gx", ("gy", "gz"))),
        check_vma=False,
    )
```

```python
import math

import jax
import jax.numpy as jnp
from jax import lax
from jax.experimental import pallas as pl
from jax.experimental.pallas import tpu as pltpu
from jax.sharding import PartitionSpec as P

CX, CY, CZ = 8, 16, 128
ANISO = 200.0
OMEGA = 0.8
HY = 10
Y0 = 12
HZ = 18
YE = CY + 2 * Y0
ZE = 2 * CZ
YM = 24
ZM = CZ
XW = CX + 8
YW = CY + 8
HIGHEST = lax.Precision.HIGHEST


def iota(shape, dim):
    return lax.broadcasted_iota(jnp.int32, shape, dim)


def mm(a, b):
    return jnp.dot(a, b, precision=HIGHEST, preferred_element_type=jnp.float32)


def nxt(v, axis):
    return pltpu.roll(v, v.shape[axis] - 1, axis)


def prv(v, axis):
    return pltpu.roll(v, 1, axis)


def face(a, b):
    both = a + b
    return jnp.where(jnp.minimum(a, b) == 0.0, both, 0.5 * both)


def unroll(planes):
    return 16 if planes == 16 else 8


def make_weights(c, wx, wy, wz, inv, planes, scale):
    wx[0] = scale * face(c[0], c[1])

    def step(x, carry):
        here = c[x + 1]
        fx = scale * face(here, c[x + 2])
        fy = scale * face(here, nxt(here, 0))
        fz = (scale * ANISO) * face(here, nxt(here, 1))
        wx[x + 1] = fx
        wy[x] = fy
        wz[x] = fz
        total = fx + wx[x] + fy + prv(fy, 0) + fz + prv(fz, 1)
        inv[x] = jnp.where(here > 0.0, OMEGA / total, 0.0)
        return carry

    lax.fori_loop(0, planes, step, 0, unroll=unroll(planes))


def residual(v, b, wx, wy, wz, x, before):
    here = v[x + 1]
    fx = wx[x + 1] * (here - v[x + 2])
    fy = wy[x] * (here - nxt(here, 0))
    fz = wz[x] * (here - nxt(here, 1))
    flow = (fx - before) + (fy - prv(fy, 0)) + (fz - prv(fz, 1))
    return here, b[x] - flow, fx


def sweep(v, out, b, wx, wy, wz, inv, planes):
    def step(x, before):
        here, rest, fx = residual(v, b, wx, wy, wz, x, before)
        out[x + 1] = here + inv[x] * rest
        return fx

    lax.fori_loop(0, planes, step, wx[0] * (0.0 - v[1]), unroll=unroll(planes))


def pack_z_kernel(line, src, log_coef, lateral, state, mine, down, up):
    gz = lax.axis_index("gz")
    cut = (line[gz] != line[jnp.minimum(gz + 1, 15)]).astype(jnp.float32)
    pick = (iota((CX * CY, CX), 0) // CY == iota((CX * CY, CX), 1)).astype(jnp.float32)
    rows = mm(pick, lateral[...])
    own = iota((CX * CY, CY), 0) % CY == iota((CX * CY, CY), 1)
    rows = jnp.sum(jnp.where(own, rows, 0.0), axis=1, keepdims=True)
    rows = jnp.broadcast_to(rows, (CX * CY, CZ)).reshape(CX, CY, CZ)
    c = jnp.exp(log_coef[...] + rows)
    s = src[...]
    mine[0:CX] = s
    mine[CX : 2 * CX] = c
    mine[3 * CX] = state[0]
    mine[3 * CX + 1] = state[CX - 1]
    lane = iota((CX, CY, CZ), 2)
    k = pltpu.roll(c, 64, 2)
    t = pltpu.roll(state[...], 32, 2)
    zero = jnp.zeros_like(s)
    far = CZ - HZ
    coef = jnp.where((lane >= 64) & (lane < 64 + HZ), k, zero)
    down[...] = jnp.where(lane < HZ, s, jnp.where(lane == 32, t, coef))
    coef = jnp.where((lane >= far - 64) & (lane < 64), k, zero)
    coef = jnp.where(lane == 20, cut, coef)
    up[...] = jnp.where(lane >= far, s, jnp.where(lane == 31, t, coef))


def pack_y_kernel(g, state, c_up, c_down, s_up, s_down):
    def put(up, down, n, plane):
        at = pl.ds(HY * (n % 4), HY)
        up[n // 4, at] = plane[CY - HY :]
        down[n // 4, at] = plane[:HY]

    for s in range(4):
        for i in range(2 * CX):
            put(c_up, c_down, 2 * CX * s + i, g[s, CX + i])
        for i in range(CX):
            put(s_up, s_down, CX * s + i, g[s, i])
    for i in range(CX):
        put(s_up, s_down, 4 * CX + i, state[i])


def place(out, lanes, n, low, own, high, change):
    at = pl.ds(HY * (n % 4), HY)
    out[Y0 - HY : Y0, lanes] = change(low[n // 4, at])
    out[Y0 : Y0 + CY, lanes] = change(own)
    out[Y0 + CY : Y0 + CY + HY, lanes] = change(high[n // 4, at])


def edge_lanes(v):
    lane = iota(v.shape, 1)
    return jnp.where((lane < HZ) | (lane >= CZ - HZ), v, 0.0)


LOW, HIGH = slice(0, CZ), slice(CZ, ZE)


def window(gx, pairs, planes):
    nx = 4 * CX

    def keep(w, carry):
        for out, ref, shift, first in pairs:
            x = CX * gx - 4 + w - first
            inside = (x >= -first) & (x < nx)
            at = jnp.clip(x, -first, nx - 1) + shift
            out[w] = jnp.where(inside, ref[at, 8:32], 0.0)
        return carry

    lax.fori_loop(0, planes, keep, 0, unroll=4)


def fold_y():
    return (iota((YM, YE), 1) // 2 + 2 == iota((YM, YE), 0)).astype(jnp.float32)


def fold_z():
    return (iota((ZE, ZM), 0) // 2 == iota((ZE, ZM), 1)).astype(jnp.float32) * 0.125


def fold_low(first, count):
    shape = (8 * count, 16 * YM)
    to, frm = iota(shape, 0), iota(shape, 1)
    m, r = frm // YM, frm % YM
    return ((m // 2 == to % 8) & (r // 2 - 4 == to // 8 + first)).astype(jnp.float32) * 0.125


def squeeze():
    m, l = iota((ZM, CZ), 0), iota((ZM, CZ), 1)
    m = jnp.where(m < 96, m, m - 128)
    return ((m + 8) // 2 == l).astype(jnp.float32)


def gather(v):
    lane = iota((8, CZ), 1)
    out = pltpu.roll(v[0], CZ - 4, 1)
    for y in range(1, 4):
        out = jnp.where(lane >= 32 * y, pltpu.roll(v[y], 32 * y - 4, 1), out)
    return out


def coef_kernel(
    g, yp, yn,
    wx, wy, wz, inv, c_w, wx_w, wy_w, wz_w, inv_w, mwx, mwy, mwz, minv, low_o,
    c, t, mc,
):
    gx, gz = lax.axis_index("gx"), lax.axis_index("gz")
    zero = jnp.zeros((YE, ZE), jnp.float32)
    nx = 4 * CX
    c[0] = zero
    c[nx + 1] = zero
    none = jnp.zeros((8, ZE), jnp.float32)
    for s in range(4):
        for i in range(CX):
            out = c.at[CX * s + i + 1]
            out[0:8] = none
            out[YE - 8 :] = none
            n = 2 * CX * s + i
            place(out, LOW, n, yp, g[s, CX + i], yn, lambda v: v)
            place(
                out, HIGH, n + CX, yp, g[s, 2 * CX + i], yn,
                lambda v: edge_lanes(pltpu.roll(v, 64, 1)),
            )
    make_weights(c, wx, wy, wz, inv, nx, 1.0)
    rows = fold_y()

    def coarse(m, carry):
        t[m] = mm(rows, c[2 * m + 1] + c[2 * m + 2])
        return carry

    lax.fori_loop(0, 16, coarse, 0, unroll=8)
    mid_zero = jnp.zeros((YM, ZM), jnp.float32)
    mc[0] = mid_zero
    mc[17] = mid_zero
    mc[1:17] = mm(t[...].reshape(16 * YM, ZE), fold_z()).reshape(16, YM, ZM)
    make_weights(mc, mwx, mwy, mwz, minv, 16, 0.25)
    window(gx, [(c_w, c, 1, 0), (wy_w, wy, 0, 0), (wz_w, wz, 0, 0), (inv_w, inv, 0, 0)], XW)
    window(gx, [(wx_w, wx, 1, 1)], XW + 1)

    low_c = mm(mm(fold_low(-1, 6), mc[1:17].reshape(16 * YM, ZM)), squeeze())
    low_c = low_c.reshape(6, 8, CZ)
    here = low_c[1:5]
    row = iota((4, 8, CZ), 1)
    scale = 0.0625
    fx1 = scale * face(here, jnp.where(row < 7, nxt(here, 1), 0.0))
    fx0 = scale * face(here, jnp.where(row > 0, prv(here, 1), 0.0))
    fy1 = scale * face(here, low_c[2:6])
    fy0 = scale * face(here, low_c[0:4])
    fz = (scale * ANISO) * face(here, nxt(here, 2))
    lower = prv(fz, 2)
    total = fx1 + fx0 + fy1 + fy0 + fz + lower

    flag = pltpu.roll(g[3, 16, 0:8], CZ - 20, 1)
    row = iota((8, CZ), 0)
    for s in range(2, -1, -1):
        flag = jnp.where(row < 2 * s + 2, pltpu.roll(g[s, 16, 0:8], CZ - 20, 1), flag)
    flag = jnp.broadcast_to(flag[:, 0:1], (8, CZ))
    e = gather(lower)
    top = iota((8, CZ), 1) % 32 == 0
    low_o[0] = gather(total)
    low_o[1] = jnp.where(top, 0.0, e)
    low_o[2] = jnp.where(top & (flag == 0.0) & (gz > 0), e, 0.0)


def first_kernel(
    g, cp, cn, yp, yn, state, wx, wy, wz, inv, mwx, mwy, mwz, minv, low,
    src_w, pre_w, se, mid_pre_o, mb, low_o, block_o,
    b, va, vb, t, mva, mvb,
):
    gx = lax.axis_index("gx")
    zero = jnp.zeros((YE, ZE), jnp.float32)
    nx = 4 * CX
    for ref in (va, vb):
        ref[0] = zero
        ref[nx + 1] = zero
    none = jnp.zeros((8, ZE), jnp.float32)
    for s in range(4):
        for i in range(CX):
            out = b.at[CX * s + i]
            out[0:8] = none
            out[YE - 8 :] = none
            place(out, LOW, CX * s + i, yp, g[s, i], yn, lambda v: v)
            place(out, HIGH, 2 * CX * s + CX + i, cp, g[s, 2 * CX + i], cn, edge_lanes)

    def start(x, carry):
        va[x + 1] = inv[x] * b[x]
        return carry

    lax.fori_loop(0, nx, start, 0, unroll=4)
    sweep(va, vb, b, wx, wy, wz, inv, nx)
    sweep(vb, va, b, wx, wy, wz, inv, nx)

    rows = fold_y()

    def coarse(m, before):
        x = 2 * m
        _, one, fx = residual(va, b, wx, wy, wz, x, before)
        _, two, fx = residual(va, b, wx, wy, wz, x + 1, fx)
        t[m] = mm(rows, one + two)
        return fx

    lax.fori_loop(0, 16, coarse, wx[0] * (0.0 - va[1]), unroll=8)
    mb[...] = mm(t[...].reshape(16 * YM, ZE), fold_z()).reshape(16, YM, ZM)
    mid_zero = jnp.zeros((YM, ZM), jnp.float32)
    for ref in (mva, mvb):
        ref[0] = mid_zero
        ref[17] = mid_zero

    window(gx, [(src_w, b, 0, 0), (pre_w, va, 1, 0)], XW)

    zero8 = jnp.zeros((8, CZ), jnp.float32)
    wide = jnp.zeros((YW, CZ), jnp.float32)
    row = iota((YW, CZ), 0)
    lane = iota((YW, CZ), 1)
    left = g[jnp.maximum(gx - 1, 0), 25]
    right = g[jnp.minimum(gx + 1, 3), 24]
    left = jnp.where(gx > 0, left, 0.0)
    right = jnp.where(gx < 3, right, 0.0)
    for at, plane in ((0, left), (9, right)):
        mid = pltpu.roll(jnp.concatenate([plane, zero8], 0), 4, 0)
        se[at] = jnp.concatenate([mid, wide], 1)
    for i in range(CX):
        mid = pltpu.roll(jnp.concatenate([state[i], zero8], 0), 4, 0)
        n = 4 * CX + i
        at = HY * (n % 4)
        under, over = yp[n // 4, at + HY - 1 : at + HY], yn[n // 4, at : at + 1]
        mid = jnp.where(row == 3, under, jnp.where(row == 20, over, mid))
        halo = pltpu.roll(jnp.concatenate([g[gx, 16 + i], zero8], 0), 4, 0)
        halo = pltpu.roll(halo, CZ - 32, 1)
        halo = jnp.where((lane == 0) | (lane == CZ - 1), halo, 0.0)
        se[i + 1] = jnp.concatenate([mid, halo], 1)

    mva[1:17] = minv[...] * mb[...]
    sweep(mva, mvb, mb, mwx, mwy, mwz, minv, 16)
    sweep(mvb, mva, mb, mwx, mwy, mwz, minv, 16)

    def rest(x, before):
        _, r, fx = residual(mva, mb, mwx, mwy, mwz, x, before)
        mvb[x + 1] = r
        mid_pre_o[x] = mva[x + 1, 8:16]
        return fx

    lax.fori_loop(0, 16, rest, mwx[0] * (0.0 - mva[1]), unroll=16)

    rhs = mm(mm(fold_low(0, 4), mvb[1:17].reshape(16 * YM, ZM)), squeeze()).reshape(4, 8, CZ)
    depth = iota((8, CZ), 1) % 32
    top = depth == 0
    r, d, e, edge = gather(rhs), low[0], low[1], low[2]
    v = jnp.where(top, 1.0, 0.0)
    w = jnp.where(depth == 31, 1.0, 0.0)
    for k in range(5):
        s = 1 << k
        back = CZ - s
        inv = 1.0 / d
        t = e * inv
        alpha = e * pltpu.roll(inv, s, 1)
        r, v, w = [
            q + alpha * pltpu.roll(q, s, 1) + pltpu.roll(t * q, back, 1) for q in (r, v, w)
        ]
        d = d - alpha * e - pltpu.roll(t * e, back, 1)
        e = alpha * pltpu.roll(e, s, 1)
    inv = 1.0 / d
    r, v, w = r * inv, v * inv, w * inv
    block_o[0] = r
    block_o[1] = v
    block_o[2] = w
    packed = jnp.where((depth < 3) | (depth >= 29), r, 0.0)
    packed = jnp.where((depth >= 3) & (depth < 6), pltpu.roll(v, 3, 1), packed)
    packed = jnp.where((depth >= 26) & (depth < 29), pltpu.roll(v, CZ - 3, 1), packed)
    packed = jnp.where((depth >= 6) & (depth < 9), pltpu.roll(w, 6, 1), packed)
    packed = jnp.where((depth >= 23) & (depth < 26), pltpu.roll(w, CZ - 6, 1), packed)
    packed = jnp.where(depth == 9, pltpu.roll(edge, 9, 1), packed)
    for p in range(16):
        low_o[p] = packed


def solve_kernel(rec, block, mid_pre, mid_rhs, out, up, down):
    gz = lax.axis_index("gz")
    lane = iota((8, CZ), 1)
    depth = lane % 32

    def take(v, at):
        return pltpu.roll(v, (CZ - at) % CZ, 1) if at else v

    def parts(offset):
        p = gz + offset
        v = rec[jnp.clip(p, 0, 15)]
        low = take(v, 0), take(v, 3), take(v, 6)
        high = take(v, 31), take(v, 28), take(v, 25)
        return v, low, high, jnp.where((p >= 0) & (p <= 15), take(v, 9), 0.0)

    every = {k: parts(k) for k in range(-4, 5)}
    zero = jnp.zeros((8, CZ), jnp.float32)

    a, b = {-5: zero}, {-5: zero}
    f, g = {}, {}
    for k in range(-4, 1):
        _, (y0, v0, w0), (y1, v1, w1), e = every[k]
        left, more = e * a[k - 1], e * e * b[k - 1]
        den = 1.0 / (1.0 - v0 * more)
        f[k] = (y0 + v0 * left) * den
        g[k] = w0 * den
        a[k] = y1 + v1 * (left + more * f[k])
        b[k] = w1 + v1 * (more * g[k])
    ra, rb = {5: zero}, {5: zero}
    rf, rg = {}, {}
    e_next = zero
    for k in range(4, 0, -1):
        _, (y0, v0, w0), (y1, v1, w1), e = every[k]
        right, more = e_next * ra[k + 1], e_next * e_next * rb[k + 1]
        den = 1.0 / (1.0 - w1 * more)
        rf[k] = (y1 + w1 * right) * den
        rg[k] = v1 * den
        ra[k] = y0 + w0 * (right + more * rf[k])
        rb[k] = v0 + w0 * (more * rg[k])
        e_next = e
    e0, e1 = every[0][3], every[1][3]
    last = (a[0] + b[0] * e1 * ra[1]) / (1.0 - b[0] * e1 * e1 * rb[1])
    right = e1 * (ra[1] + rb[1] * (e1 * last))
    first = f[0] + g[0] * right
    left = e0 * (a[-1] + b[-1] * (e0 * first))
    before = f[-1] + g[-1] * (e0 * first)
    em = every[-1][3]
    left_m, right_m = em * (a[-2] + b[-2] * (em * before)), e0 * first
    after = rf[1] + rg[1] * (e1 * last)
    ep = every[2][3]
    left_p, right_p = e1 * last, ep * (ra[2] + rb[2] * (ep * after))

    ends = jnp.concatenate([left, right, left_m, right_m, left_p, right_p], 0)
    ends = jnp.where(iota((48, CZ), 1) % 32 == 0, ends, 0.0)
    copy = (iota((CZ, CZ), 1) // 32 * 32 == iota((CZ, CZ), 0)).astype(jnp.float32)
    ends = mm(ends, copy).reshape(6, 8, CZ)
    own = block[0] + block[1] * ends[0] + block[2] * ends[1]
    v = every[-1][0]
    low = v + pltpu.roll(v, 3, 1) * ends[2] + pltpu.roll(v, 6, 1) * ends[3]
    low = jnp.where((depth >= 29) & (gz > 0), low, 0.0)
    v = every[1][0]
    high = v + pltpu.roll(v, CZ - 3, 1) * ends[4] + pltpu.roll(v, CZ - 6, 1) * ends[5]
    high = jnp.where((depth < 3) & (gz < 15), high, 0.0)

    rows = []
    for y in range(4):
        part = jnp.where(lane < 32, take(own, 32 * y), 0.0)
        part = jnp.where((lane >= 32) & (lane < 64), take(high, (32 * y - 32) % CZ), part)
        part = jnp.where(lane >= 96, take(low, (32 * y + 32) % CZ), part)
        rows.append(part)
    rows = jnp.concatenate(rows, 0)
    k, m = iota((CZ, ZM), 0), iota((CZ, ZM), 1)
    spread_z = (k == jnp.where(m < 96, m // 2, m // 2 + 64)).astype(jnp.float32)
    to, frm = iota((128, 32), 0), iota((128, 32), 1)
    spread = ((to // 16 == frm % 8) & ((to % 8) // 2 == frm // 8)).astype(jnp.float32)
    mid = mid_pre[...] + mm(spread, mm(rows, spread_z)).reshape(16, 8, ZM)
    out[...] = mid
    row = iota((16, 8, ZM), 1)
    rest = pltpu.roll(mid_rhs[:, 8:16], 4, 1)
    up[...] = jnp.where(row == 0, rest, mid)
    down[...] = jnp.where(row == 7, rest, mid)


def second_kernel(
    mid, mid_p, mid_n, mid_rhs, mwx, mwy, mwz, minv, src_w, pre_w, c, wx, wy, wz, inv, se,
    adj, grad,
    mb, mva, mvb, sp, va, vb,
):
    gx = lax.axis_index("gx")
    mid_zero = jnp.zeros((YM, ZM), jnp.float32)
    row = iota((YM, ZM), 0)
    for x in range(16):
        out = jnp.concatenate([pltpu.roll(v, 4, 0) for v in (mid_p[x], mid[x], mid_n[x])], 0)
        mb[x] = jnp.where((row == 4) | (row == 19), out, mid_rhs[x])
    for ref in (mva, mvb):
        for at in (0, 1, 18, 19):
            ref[at] = mid_zero
    for x in range(16):
        mva[x + 2] = jnp.concatenate([mid_p[x], mid[x], mid_n[x]], 0)
    a, o = mva.at[1:19], mvb.at[1:19]
    sweep(a, o, mb, mwx, mwy, mwz, minv, 16)
    sweep(o, a, mb, mwx, mwy, mwz, minv, 16)
    sweep(a, o, mb, mwx, mwy, mwz, minv, 16)

    zero = jnp.zeros((YW, ZE), jnp.float32)
    for ref in (va, vb):
        ref[0] = zero
        ref[XW + 1] = zero
    spread_z = (iota((ZM, ZE), 1) // 2 == iota((ZM, ZE), 0)).astype(jnp.float32)
    spread_y = ((iota((YW, YM), 0) + 12) // 2 == iota((YW, YM), 1)).astype(jnp.float32)
    near = mvb[pl.ds(4 * gx, 8)]
    sp[...] = mm(near.reshape(8 * YM, ZM), spread_z).reshape(8, YM, ZE)
    for m in range(8):
        more = mm(spread_y, sp[m])
        for x in (2 * m, 2 * m + 1):
            va[x + 1] = pre_w[x] + more
    sweep(va, vb, src_w, wx, wy, wz, inv, XW)
    sweep(vb, va, src_w, wx, wy, wz, inv, XW)
    sweep(va, vb, src_w, wx, wy, wz, inv, XW)

    def product(f, one, two, sone, stwo):
        return f * (one - two) * (sone - stwo)

    def half(one, two):
        return jnp.where(jnp.minimum(one, two) == 0.0, 1.0, 0.5)

    lane = iota((YW, CZ), 1)

    def terms(i, carry):
        before, acc = carry
        v, k, s = vb[i + 5], c[i + 4], se[i + 1]
        px = product(half(k, c[i + 5]), v, vb[i + 6], s, se[i + 2])
        py = product(half(k, nxt(k, 0)), v, nxt(v, 0), s, nxt(s, 0))
        pz = product(half(k, nxt(k, 1)), v, nxt(v, 1), s, nxt(s, 1))
        both = k * (px + before + py + prv(py, 0) + pz + prv(pz, 1))
        part = jnp.sum(both[:, :CZ], axis=1, keepdims=True)
        acc = jnp.where(lane == i, part, acc)
        adj[i] = pltpu.roll(v, YW - 4, 0)[:CY, :CZ]
        return px, acc

    first = product(half(c[3], c[4]), vb[4], vb[5], se[0], se[1])
    _, acc = lax.fori_loop(
        0, CX, terms, (first, jnp.zeros((YW, CZ), jnp.float32)), unroll=8
    )
    grad[...] = pltpu.roll(acc, YW - 4, 0)[:CY]


def f32(*shape):
    return jax.ShapeDtypeStruct(shape, jnp.float32)


def vm(*shape):
    return pltpu.VMEM(shape, jnp.float32)


def params():
    return pltpu.CompilerParams(vmem_limit_bytes=20 << 20)


def both_ways(up, down, axis):
    count = lax.axis_size(axis)
    higher = [(i, i + 1) for i in range(count - 1)]
    lower = [(j, i) for i, j in higher]
    return lax.ppermute(up, axis, higher), lax.ppermute(down, axis, lower)


def per_device(source, state, log_coef, lateral, owners):
    block = f32(CX, CY, CZ)
    smem = pl.BlockSpec(memory_space=pltpu.SMEM)
    vmem = pl.BlockSpec(memory_space=pltpu.VMEM)
    mine, down, up = pl.pallas_call(
        pack_z_kernel,
        out_shape=(f32(3 * CX + 2, CY, CZ), block, block),
        in_specs=[smem, vmem, vmem, vmem, vmem],
        name="pack_z",
    )(owners[0, 0], source, log_coef, lateral, state)
    gz, count = lax.axis_index("gz"), lax.axis_size("gz")
    before = lax.ppermute(up, "gz", [(i, (i + 1) % count) for i in range(count)])
    after = lax.ppermute(down, "gz", [(i, (i - 1) % count) for i in range(count)])
    halo = jnp.where(gz > 0, before, 0.0) + jnp.where(gz < count - 1, after, 0.0)
    mine = lax.dynamic_update_slice(mine, halo, (2 * CX, 0, 0))
    g = lax.all_gather(mine, "gx")
    fine, fine1, fine2 = (32, YE, ZE), (33, YE, ZE), (34, YE, ZE)
    mid, mid1, mid2 = (16, YM, ZM), (17, YM, ZM), (18, YM, ZM)
    win, win1, win2 = (XW, YW, ZE), (XW + 1, YW, ZE), (XW + 2, YW, ZE)
    c_rows, s_rows = f32(16, 4 * HY, CZ), f32(10, 4 * HY, CZ)
    c_up, c_down, s_up, s_down = pl.pallas_call(
        pack_y_kernel,
        out_shape=(c_rows, c_rows, s_rows, s_rows),
        compiler_params=params(),
        name="pack_y",
    )(g, state)
    cp, cn = both_ways(c_up, c_down, "gy")
    sp, sn = both_ways(s_up, s_down, "gy")
    wx, wy, wz, inv, c_w, wx_w, wy_w, wz_w, inv_w, mwx, mwy, mwz, minv, low = pl.pallas_call(
        coef_kernel,
        out_shape=(
            f32(*fine1), f32(*fine), f32(*fine), f32(*fine),
            f32(*win), f32(*win1), f32(*win), f32(*win), f32(*win),
            f32(*mid1), f32(*mid), f32(*mid), f32(*mid), f32(3, 8, CZ),
        ),
        scratch_shapes=[vm(*fine2), vm(16, YM, ZE), vm(*mid2)],
        compiler_params=params(),
        name="coef",
    )(g, cp, cn)
    src_w, pre_w, se, mid_pre, mid_rhs, ends, block_s = pl.pallas_call(
        first_kernel,
        out_shape=(
            f32(*win), f32(*win), f32(CX + 2, YW, ZE),
            f32(16, 8, ZM), f32(*mid), f32(16, 8, CZ), f32(3, 8, CZ),
        ),
        scratch_shapes=[
            vm(*fine), vm(*fine2), vm(*fine2), vm(16, YM, ZE), vm(*mid2), vm(*mid2),
        ],
        compiler_params=params(),
        name="first",
    )(g, cp, cn, sp, sn, state, wx, wy, wz, inv, mwx, mwy, mwz, minv, low)

    rec = lax.all_to_all(ends, "gz", 0, 0, tiled=True)
    tile = f32(16, 8, ZM)
    mid_init, up, down = pl.pallas_call(
        solve_kernel, out_shape=(tile, tile, tile), compiler_params=params(), name="solve"
    )(rec, block_s, mid_pre, mid_rhs)
    mid_p, mid_n = both_ways(up, down, "gy")

    adj, grad = pl.pallas_call(
        second_kernel,
        out_shape=(block, f32(CY, CZ)),
        scratch_shapes=[
            vm(*mid), vm(20, YM, ZM), vm(20, YM, ZM), vm(8, YM, ZE), vm(*win2), vm(*win2),
        ],
        compiler_params=params(),
        name="second",
    )(mid_init, mid_p, mid_n, mid_rhs, mwx, mwy, mwz, minv,
      src_w, pre_w, c_w, wx_w, wy_w, wz_w, inv_w, se)
    sums = lax.all_to_all(grad, "gz", 0, 0, tiled=True)
    total = jnp.sum(sums[:, :CX], axis=0)[:, None]
    return adj, total * (-1.0 / math.sqrt(source.shape[2] * lax.axis_size("gz")))


def solution(mesh):
    placed = (
        P("gx", "gy", "gz"),
        P("gx", "gy", "gz"),
        P("gx", "gy", "gz"),
        P("gx", "gy"),
        P("gx", "gy", None),
    )
    return jax.shard_map(
        per_device,
        mesh=mesh,
        in_specs=placed,
        out_specs=(P("gx", "gy", "gz"), P("gx", ("gy", "gz"))),
        check_vma=False,
    )
```

```python
import math

import jax
import jax.numpy as jnp
from jax import lax
from jax.experimental import pallas as pl
from jax.experimental.pallas import tpu as pltpu
from jax.sharding import PartitionSpec as P

CX, CY, CZ = 8, 16, 128
ANISO = 200.0
OMEGA = 0.8
HY = 10
Y0 = 12
HZ = 18
YE = CY + 2 * Y0
ZE = 2 * CZ
TILES = 11
YM = 24
ZM = CZ
XW = CX + 8
YW = CY + 8
HIGHEST = lax.Precision.HIGHEST


def iota(shape, dim):
    return lax.broadcasted_iota(jnp.int32, shape, dim)


def mm(a, b):
    return jnp.dot(a, b, precision=HIGHEST, preferred_element_type=jnp.float32)


def split(v, axis):
    high = v.astype(jnp.bfloat16)
    v = v - high.astype(jnp.float32)
    mid = v.astype(jnp.bfloat16)
    low = (v - mid.astype(jnp.float32)).astype(jnp.bfloat16)
    return jnp.concatenate([high, mid, low], axis)


def pick_rows(sel, v):
    out = jnp.dot(sel.astype(jnp.bfloat16), split(v, 1), preferred_element_type=jnp.float32)
    n = v.shape[1]
    return out[:, :n] + (out[:, n : 2 * n] + out[:, 2 * n :])


def pick_lanes(v, sel):
    out = jnp.dot(split(v, 0), sel.astype(jnp.bfloat16), preferred_element_type=jnp.float32)
    n = v.shape[0]
    return out[:n] + (out[n : 2 * n] + out[2 * n :])


def nxt(v, axis):
    return pltpu.roll(v, v.shape[axis] - 1, axis)


def prv(v, axis):
    return pltpu.roll(v, 1, axis)


def face(a, b):
    both = a + b
    return jnp.where(jnp.minimum(a, b) == 0.0, both, 0.5 * both)


def unroll(planes):
    return 16 if planes == 16 else 8


def make_weights(c, wx, wy, wz, inv, planes, scale):
    wx[0] = scale * face(c[0], c[1])

    def step(x, carry):
        here = c[x + 1]
        fx = scale * face(here, c[x + 2])
        fy = scale * face(here, nxt(here, 0))
        fz = (scale * ANISO) * face(here, nxt(here, 1))
        wx[x + 1] = fx
        wy[x] = fy
        wz[x] = fz
        total = fx + wx[x] + fy + prv(fy, 0) + fz + prv(fz, 1)
        inv[x] = jnp.where(here > 0.0, OMEGA / total, 0.0)
        return carry

    lax.fori_loop(0, planes, step, 0, unroll=unroll(planes))


def residual(v, b, wx, wy, wz, x, before):
    here = v[x + 1]
    fx = wx[x + 1] * (here - v[x + 2])
    fy = wy[x] * (here - nxt(here, 0))
    fz = wz[x] * (here - nxt(here, 1))
    flow = (fx - before) + (fy - prv(fy, 0)) + (fz - prv(fz, 1))
    return here, b[x] - flow, fx


def sweep(v, out, b, wx, wy, wz, inv, planes):
    def step(x, before):
        here, rest, fx = residual(v, b, wx, wy, wz, x, before)
        out[x + 1] = here + inv[x] * rest
        return fx

    lax.fori_loop(0, planes, step, wx[0] * (0.0 - v[1]), unroll=unroll(planes))


def first_sweeps(out, b, wx, wy, wz, inv, planes):
    def step(x, carry):
        before, here = carry
        after = inv[jnp.minimum(x + 1, planes - 1)] * b[x + 1]
        fx = wx[x + 1] * (here - after)
        fy = wy[x] * (here - nxt(here, 0))
        fz = wz[x] * (here - nxt(here, 1))
        flow = (fx - before) + (fy - prv(fy, 0)) + (fz - prv(fz, 1))
        out[x + 1] = here + inv[x] * (b[x] - flow)
        return fx, after

    here = inv[0] * b[0]
    lax.fori_loop(0, planes, step, (wx[0] * (0.0 - here), here), unroll=unroll(planes))


def pack_z_kernel(line, src, log_coef, lateral, state, mine, down, up):
    gz = lax.axis_index("gz")
    cut = (line[gz] != line[jnp.minimum(gz + 1, 15)]).astype(jnp.float32)
    pick = (iota((CX * CY, CX), 0) // CY == iota((CX * CY, CX), 1)).astype(jnp.float32)
    rows = mm(pick, lateral[...])
    own = iota((CX * CY, CY), 0) % CY == iota((CX * CY, CY), 1)
    rows = jnp.sum(jnp.where(own, rows, 0.0), axis=1, keepdims=True)
    rows = jnp.broadcast_to(rows, (CX * CY, CZ)).reshape(CX, CY, CZ)
    c = jnp.exp(log_coef[...] + rows)
    s = src[...]
    mine[0:CX] = s
    mine[CX : 2 * CX] = c
    mine[3 * CX] = state[0]
    mine[3 * CX + 1] = state[CX - 1]
    lane = iota((CX, CY, CZ), 2)
    k = pltpu.roll(c, 64, 2)
    t = pltpu.roll(state[...], 32, 2)
    zero = jnp.zeros_like(s)
    far = CZ - HZ
    coef = jnp.where((lane >= 64) & (lane < 64 + HZ), k, zero)
    down[...] = jnp.where(lane < HZ, s, jnp.where(lane == 32, t, coef))
    coef = jnp.where((lane >= far - 64) & (lane < 64), k, zero)
    coef = jnp.where(lane == 20, cut, coef)
    up[...] = jnp.where(lane >= far, s, jnp.where(lane == 31, t, coef))


def pack_y_kernel(g, state, c_up, c_down, s_up, s_down):
    lane = iota((CY, CZ), 1)
    none = jnp.zeros((HY, CZ), jnp.float32)

    def put(refs, n, low, high):
        at = pl.ds(HY * (n % 4), HY)
        refs[0][n // 4, at] = high
        refs[1][n // 4, at] = low

    for coef, refs in ((1, (c_up, c_down)), (0, (s_up, s_down))):
        for s in range(4):
            for i in range(CX):
                plane = g[s, CX * coef + i]
                put(refs, CX * s + i, plane[:HY], plane[CY - HY :])
        for t in range(TILES):
            plane = jnp.zeros((CY, CZ), jnp.float32)
            for x in range(3 * t, min(3 * t + 3, 4 * CX)):
                off = 2 * HZ * (x % 3)
                move = off - 46 if coef else off + HZ
                halo = pltpu.roll(g[x // CX, 2 * CX + x % CX], move % CZ, 1)
                plane = jnp.where(lane >= off, halo, plane)
            put(refs, 4 * CX + t, plane[:HY], plane[CY - HY :])
    for i in range(CX):
        put((c_up, c_down), 4 * CX + TILES + i, state[i, :HY], state[i, CY - HY :])
    put((s_up, s_down), 4 * CX + TILES, none, none)
    put((c_up, c_down), 5 * CX + TILES, none, none)


def rows_at(ref, n):
    return ref[n // 4, HY * (n % 4) : HY * (n % 4) + HY]


def place(out, lanes, low, own, high):
    out[Y0 - HY : Y0, lanes] = low
    out[Y0 : Y0 + CY, lanes] = own
    out[Y0 + CY : Y0 + CY + HY, lanes] = high


def edge_lanes(v, move):
    v = pltpu.roll(v, move % CZ, 1) if move % CZ else v
    lane = iota(v.shape, 1)
    return jnp.where((lane < HZ) | (lane >= CZ - HZ), v, 0.0)


def fill(out, g, yp, yn, x, coef):
    s, i = x // CX, x % CX
    none = jnp.zeros((8, ZE), jnp.float32)
    out[0:8] = none
    out[YE - 8 :] = none
    place(out, LOW, rows_at(yp, x), g[s, CX * coef + i], rows_at(yn, x))
    n, move = 4 * CX + x // 3, CZ - HZ - 2 * HZ * (x % 3)
    place(
        out, HIGH, edge_lanes(rows_at(yp, n), move),
        edge_lanes(g[s, 2 * CX + i], 64 * coef), edge_lanes(rows_at(yn, n), move),
    )


LOW, HIGH = slice(0, CZ), slice(CZ, ZE)


def window(gx, pairs, planes):
    nx = 4 * CX

    def keep(w, carry):
        for out, ref, shift, first in pairs:
            x = CX * gx - 4 + w - first
            inside = (x >= -first) & (x < nx)
            at = jnp.clip(x, -first, nx - 1) + shift
            out[w] = jnp.where(inside, ref[at, 8:32], 0.0)
        return carry

    lax.fori_loop(0, planes, keep, 0, unroll=4)


def fold_y():
    return (iota((YM, YE), 1) // 2 + 2 == iota((YM, YE), 0)).astype(jnp.float32)


def fold_z():
    return (iota((ZE, ZM), 0) // 2 == iota((ZE, ZM), 1)).astype(jnp.float32) * 0.125


def fold_low(first, count):
    shape = (8 * count, 16 * YM)
    to, frm = iota(shape, 0), iota(shape, 1)
    m, r = frm // YM, frm % YM
    return ((m // 2 == to % 8) & (r // 2 - 4 == to // 8 + first)).astype(jnp.float32) * 0.125


def squeeze():
    m, l = iota((ZM, CZ), 0), iota((ZM, CZ), 1)
    m = jnp.where(m < 96, m, m - 128)
    return ((m + 8) // 2 == l).astype(jnp.float32)


def gather(v):
    lane = iota((8, CZ), 1)
    out = pltpu.roll(v[0], CZ - 4, 1)
    for y in range(1, 4):
        out = jnp.where(lane >= 32 * y, pltpu.roll(v[y], 32 * y - 4, 1), out)
    return out


def coef_kernel(
    g, yp, yn,
    wx, wy, wz, inv, c_w, wx_w, wy_w, wz_w, inv_w, mwx, mwy, mwz, minv, low_o,
    c, t, mc,
):
    gx, gz = lax.axis_index("gx"), lax.axis_index("gz")
    zero = jnp.zeros((YE, ZE), jnp.float32)
    nx = 4 * CX
    c[0] = zero
    c[nx + 1] = zero
    for x in range(nx):
        fill(c.at[x + 1], g, yp, yn, x, 1)
    make_weights(c, wx, wy, wz, inv, nx, 1.0)
    rows = fold_y()

    def coarse(m, carry):
        t[m] = pick_rows(rows, c[2 * m + 1] + c[2 * m + 2])
        return carry

    lax.fori_loop(0, 16, coarse, 0, unroll=8)
    mid_zero = jnp.zeros((YM, ZM), jnp.float32)
    mc[0] = mid_zero
    mc[17] = mid_zero
    mc[1:17] = pick_lanes(t[...].reshape(16 * YM, ZE), fold_z()).reshape(16, YM, ZM)
    make_weights(mc, mwx, mwy, mwz, minv, 16, 0.25)
    window(gx, [(c_w, c, 1, 0), (wy_w, wy, 0, 0), (wz_w, wz, 0, 0), (inv_w, inv, 0, 0)], XW)
    window(gx, [(wx_w, wx, 1, 1)], XW + 1)

    low_c = pick_lanes(pick_rows(fold_low(-1, 6), mc[1:17].reshape(16 * YM, ZM)), squeeze())
    low_c = low_c.reshape(6, 8, CZ)
    here = low_c[1:5]
    row = iota((4, 8, CZ), 1)
    scale = 0.0625
    fx1 = scale * face(here, jnp.where(row < 7, nxt(here, 1), 0.0))
    fx0 = scale * face(here, jnp.where(row > 0, prv(here, 1), 0.0))
    fy1 = scale * face(here, low_c[2:6])
    fy0 = scale * face(here, low_c[0:4])
    fz = (scale * ANISO) * face(here, nxt(here, 2))
    lower = prv(fz, 2)
    total = fx1 + fx0 + fy1 + fy0 + fz + lower

    flag = pltpu.roll(g[3, 16, 0:8], CZ - 20, 1)
    row = iota((8, CZ), 0)
    for s in range(2, -1, -1):
        flag = jnp.where(row < 2 * s + 2, pltpu.roll(g[s, 16, 0:8], CZ - 20, 1), flag)
    flag = jnp.broadcast_to(flag[:, 0:1], (8, CZ))
    e = gather(lower)
    top = iota((8, CZ), 1) % 32 == 0
    low_o[0] = gather(total)
    low_o[1] = jnp.where(top, 0.0, e)
    low_o[2] = jnp.where(top & (flag == 0.0) & (gz > 0), e, 0.0)


def first_kernel(
    g, cp, cn, yp, yn, state, wx, wy, wz, inv, mwx, mwy, mwz, minv, low,
    src_w, pre_w, se, mid_pre_o, mb, low_o, block_o,
    b, va, vb, t, mva, mvb,
):
    gx = lax.axis_index("gx")
    zero = jnp.zeros((YE, ZE), jnp.float32)
    nx = 4 * CX
    for ref in (va, vb):
        ref[0] = zero
        ref[nx + 1] = zero
    for x in range(nx):
        fill(b.at[x], g, yp, yn, x, 0)
    b[nx] = zero
    first_sweeps(va, b, wx, wy, wz, inv, nx)
    sweep(va, vb, b, wx, wy, wz, inv, nx)

    rows = fold_y()

    def coarse(m, before):
        x = 2 * m
        _, one, fx = residual(vb, b, wx, wy, wz, x, before)
        _, two, fx = residual(vb, b, wx, wy, wz, x + 1, fx)
        t[m] = pick_rows(rows, one + two)
        return fx

    lax.fori_loop(0, 16, coarse, wx[0] * (0.0 - vb[1]), unroll=8)
    mb[...] = pick_lanes(t[...].reshape(16 * YM, ZE), fold_z()).reshape(16, YM, ZM)
    mid_zero = jnp.zeros((YM, ZM), jnp.float32)
    for ref in (mva, mvb):
        ref[0] = mid_zero
        ref[17] = mid_zero

    window(gx, [(src_w, b, 0, 0), (pre_w, vb, 1, 0)], XW)

    zero8 = jnp.zeros((8, CZ), jnp.float32)
    wide = jnp.zeros((YW, CZ), jnp.float32)
    row = iota((YW, CZ), 0)
    lane = iota((YW, CZ), 1)
    left = g[jnp.maximum(gx - 1, 0), 25]
    right = g[jnp.minimum(gx + 1, 3), 24]
    left = jnp.where(gx > 0, left, 0.0)
    right = jnp.where(gx < 3, right, 0.0)
    for at, plane in ((0, left), (9, right)):
        mid = pltpu.roll(jnp.concatenate([plane, zero8], 0), 4, 0)
        se[at] = jnp.concatenate([mid, wide], 1)
    for i in range(CX):
        mid = pltpu.roll(jnp.concatenate([state[i], zero8], 0), 4, 0)
        n = 4 * CX + TILES + i
        at = HY * (n % 4)
        under, over = cp[n // 4, at + HY - 1 : at + HY], cn[n // 4, at : at + 1]
        mid = jnp.where(row == 3, under, jnp.where(row == 20, over, mid))
        halo = pltpu.roll(jnp.concatenate([g[gx, 16 + i], zero8], 0), 4, 0)
        halo = pltpu.roll(halo, CZ - 32, 1)
        halo = jnp.where((lane == 0) | (lane == CZ - 1), halo, 0.0)
        se[i + 1] = jnp.concatenate([mid, halo], 1)

    mva[1:17] = minv[...] * mb[...]
    sweep(mva, mvb, mb, mwx, mwy, mwz, minv, 16)
    sweep(mvb, mva, mb, mwx, mwy, mwz, minv, 16)

    def rest(x, before):
        _, r, fx = residual(mva, mb, mwx, mwy, mwz, x, before)
        mvb[x + 1] = r
        mid_pre_o[x] = mva[x + 1, 8:16]
        return fx

    lax.fori_loop(0, 16, rest, mwx[0] * (0.0 - mva[1]), unroll=16)

    rhs = pick_lanes(pick_rows(fold_low(0, 4), mvb[1:17].reshape(16 * YM, ZM)), squeeze()).reshape(4, 8, CZ)
    depth = iota((8, CZ), 1) % 32
    top = depth == 0
    r, d, e, edge = gather(rhs), low[0], low[1], low[2]
    v = jnp.where(top, 1.0, 0.0)
    w = jnp.where(depth == 31, 1.0, 0.0)
    for k in range(5):
        s = 1 << k
        back = CZ - s
        inv = 1.0 / d
        t = e * inv
        alpha = e * pltpu.roll(inv, s, 1)
        r, v, w = [
            q + alpha * pltpu.roll(q, s, 1) + pltpu.roll(t * q, back, 1) for q in (r, v, w)
        ]
        d = d - alpha * e - pltpu.roll(t * e, back, 1)
        e = alpha * pltpu.roll(e, s, 1)
    inv = 1.0 / d
    r, v, w = r * inv, v * inv, w * inv
    block_o[0] = r
    block_o[1] = v
    block_o[2] = w
    packed = jnp.where((depth < 3) | (depth >= 29), r, 0.0)
    packed = jnp.where((depth >= 3) & (depth < 6), pltpu.roll(v, 3, 1), packed)
    packed = jnp.where((depth >= 26) & (depth < 29), pltpu.roll(v, CZ - 3, 1), packed)
    packed = jnp.where((depth >= 6) & (depth < 9), pltpu.roll(w, 6, 1), packed)
    packed = jnp.where((depth >= 23) & (depth < 26), pltpu.roll(w, CZ - 6, 1), packed)
    packed = jnp.where(depth == 9, pltpu.roll(edge, 9, 1), packed)
    for p in range(16):
        low_o[p] = packed


def solve_kernel(rec, block, mid_pre, mid_rhs, out, up, down):
    gz = lax.axis_index("gz")
    lane = iota((8, CZ), 1)
    depth = lane % 32

    def take(v, at):
        return pltpu.roll(v, (CZ - at) % CZ, 1) if at else v

    def parts(offset):
        p = gz + offset
        v = rec[jnp.clip(p, 0, 15)]
        low = take(v, 0), take(v, 3), take(v, 6)
        high = take(v, 31), take(v, 28), take(v, 25)
        return v, low, high, jnp.where((p >= 0) & (p <= 15), take(v, 9), 0.0)

    every = {k: parts(k) for k in range(-4, 5)}
    zero = jnp.zeros((8, CZ), jnp.float32)

    a, b = {-5: zero}, {-5: zero}
    f, g = {}, {}
    for k in range(-4, 1):
        _, (y0, v0, w0), (y1, v1, w1), e = every[k]
        left, more = e * a[k - 1], e * e * b[k - 1]
        den = 1.0 / (1.0 - v0 * more)
        f[k] = (y0 + v0 * left) * den
        g[k] = w0 * den
        a[k] = y1 + v1 * (left + more * f[k])
        b[k] = w1 + v1 * (more * g[k])
    ra, rb = {5: zero}, {5: zero}
    rf, rg = {}, {}
    e_next = zero
    for k in range(4, 0, -1):
        _, (y0, v0, w0), (y1, v1, w1), e = every[k]
        right, more = e_next * ra[k + 1], e_next * e_next * rb[k + 1]
        den = 1.0 / (1.0 - w1 * more)
        rf[k] = (y1 + w1 * right) * den
        rg[k] = v1 * den
        ra[k] = y0 + w0 * (right + more * rf[k])
        rb[k] = v0 + w0 * (more * rg[k])
        e_next = e
    e0, e1 = every[0][3], every[1][3]
    last = (a[0] + b[0] * e1 * ra[1]) / (1.0 - b[0] * e1 * e1 * rb[1])
    right = e1 * (ra[1] + rb[1] * (e1 * last))
    first = f[0] + g[0] * right
    left = e0 * (a[-1] + b[-1] * (e0 * first))
    before = f[-1] + g[-1] * (e0 * first)
    em = every[-1][3]
    left_m, right_m = em * (a[-2] + b[-2] * (em * before)), e0 * first
    after = rf[1] + rg[1] * (e1 * last)
    ep = every[2][3]
    left_p, right_p = e1 * last, ep * (ra[2] + rb[2] * (ep * after))

    ends = jnp.concatenate([left, right, left_m, right_m, left_p, right_p], 0)
    ends = jnp.where(iota((48, CZ), 1) % 32 == 0, ends, 0.0)
    copy = (iota((CZ, CZ), 1) // 32 * 32 == iota((CZ, CZ), 0)).astype(jnp.float32)
    ends = pick_lanes(ends, copy).reshape(6, 8, CZ)
    own = block[0] + block[1] * ends[0] + block[2] * ends[1]
    v = every[-1][0]
    low = v + pltpu.roll(v, 3, 1) * ends[2] + pltpu.roll(v, 6, 1) * ends[3]
    low = jnp.where((depth >= 29) & (gz > 0), low, 0.0)
    v = every[1][0]
    high = v + pltpu.roll(v, CZ - 3, 1) * ends[4] + pltpu.roll(v, CZ - 6, 1) * ends[5]
    high = jnp.where((depth < 3) & (gz < 15), high, 0.0)

    rows = []
    for y in range(4):
        part = jnp.where(lane < 32, take(own, 32 * y), 0.0)
        part = jnp.where((lane >= 32) & (lane < 64), take(high, (32 * y - 32) % CZ), part)
        part = jnp.where(lane >= 96, take(low, (32 * y + 32) % CZ), part)
        rows.append(part)
    rows = jnp.concatenate(rows, 0)
    k, m = iota((CZ, ZM), 0), iota((CZ, ZM), 1)
    spread_z = (k == jnp.where(m < 96, m // 2, m // 2 + 64)).astype(jnp.float32)
    to, frm = iota((128, 32), 0), iota((128, 32), 1)
    spread = ((to // 16 == frm % 8) & ((to % 8) // 2 == frm // 8)).astype(jnp.float32)
    mid = mid_pre[...] + pick_rows(spread, pick_lanes(rows, spread_z)).reshape(16, 8, ZM)
    out[...] = mid
    row = iota((16, 8, ZM), 1)
    rest = pltpu.roll(mid_rhs[:, 8:16], 4, 1)
    up[...] = jnp.where(row == 0, rest, mid)
    down[...] = jnp.where(row == 7, rest, mid)


def second_kernel(
    mid, mid_p, mid_n, mid_rhs, mwx, mwy, mwz, minv, src_w, pre_w, c, wx, wy, wz, inv, se,
    adj, grad,
    mb, mva, mvb, sp, va, vb,
):
    gx = lax.axis_index("gx")
    mid_zero = jnp.zeros((YM, ZM), jnp.float32)
    row = iota((YM, ZM), 0)
    for x in range(16):
        out = jnp.concatenate([pltpu.roll(v, 4, 0) for v in (mid_p[x], mid[x], mid_n[x])], 0)
        mb[x] = jnp.where((row == 4) | (row == 19), out, mid_rhs[x])
    for ref in (mva, mvb):
        for at in (0, 1, 18, 19):
            ref[at] = mid_zero
    for x in range(16):
        mva[x + 2] = jnp.concatenate([mid_p[x], mid[x], mid_n[x]], 0)
    a, o = mva.at[1:19], mvb.at[1:19]
    sweep(a, o, mb, mwx, mwy, mwz, minv, 16)
    sweep(o, a, mb, mwx, mwy, mwz, minv, 16)
    sweep(a, o, mb, mwx, mwy, mwz, minv, 16)

    zero = jnp.zeros((YW, ZE), jnp.float32)
    for ref in (va, vb):
        ref[0] = zero
        ref[XW + 1] = zero
    spread_z = (iota((ZM, ZE), 1) // 2 == iota((ZM, ZE), 0)).astype(jnp.float32)
    spread_y = ((iota((YW, YM), 0) + 12) // 2 == iota((YW, YM), 1)).astype(jnp.float32)
    near = mvb[pl.ds(4 * gx, 8)]
    sp[...] = pick_lanes(near.reshape(8 * YM, ZM), spread_z).reshape(8, YM, ZE)
    for m in range(8):
        more = pick_rows(spread_y, sp[m])
        for x in (2 * m, 2 * m + 1):
            va[x + 1] = pre_w[x] + more
    sweep(va, vb, src_w, wx, wy, wz, inv, XW)
    sweep(vb, va, src_w, wx, wy, wz, inv, XW)
    sweep(va, vb, src_w, wx, wy, wz, inv, XW)

    def product(f, one, two, sone, stwo):
        return f * (one - two) * (sone - stwo)

    def half(one, two):
        return jnp.where(jnp.minimum(one, two) == 0.0, 1.0, 0.5)

    lane = iota((YW, CZ), 1)

    def terms(i, carry):
        before, acc = carry
        v, k, s = vb[i + 5], c[i + 4], se[i + 1]
        px = product(half(k, c[i + 5]), v, vb[i + 6], s, se[i + 2])
        py = product(half(k, nxt(k, 0)), v, nxt(v, 0), s, nxt(s, 0))
        pz = product(half(k, nxt(k, 1)), v, nxt(v, 1), s, nxt(s, 1))
        both = k * (px + before + py + prv(py, 0) + pz + prv(pz, 1))
        part = jnp.sum(both[:, :CZ], axis=1, keepdims=True)
        acc = jnp.where(lane == i, part, acc)
        adj[i] = pltpu.roll(v, YW - 4, 0)[:CY, :CZ]
        return px, acc

    first = product(half(c[3], c[4]), vb[4], vb[5], se[0], se[1])
    _, acc = lax.fori_loop(
        0, CX, terms, (first, jnp.zeros((YW, CZ), jnp.float32)), unroll=8
    )
    grad[...] = pltpu.roll(acc, YW - 4, 0)[:CY]


def f32(*shape):
    return jax.ShapeDtypeStruct(shape, jnp.float32)


def vm(*shape):
    return pltpu.VMEM(shape, jnp.float32)


def params():
    return pltpu.CompilerParams(vmem_limit_bytes=20 << 20)


def both_ways(up, down, axis):
    count = lax.axis_size(axis)
    higher = [(i, i + 1) for i in range(count - 1)]
    lower = [(j, i) for i, j in higher]
    return lax.ppermute(up, axis, higher), lax.ppermute(down, axis, lower)


def per_device(source, state, log_coef, lateral, owners):
    block = f32(CX, CY, CZ)
    smem = pl.BlockSpec(memory_space=pltpu.SMEM)
    vmem = pl.BlockSpec(memory_space=pltpu.VMEM)
    mine, down, up = pl.pallas_call(
        pack_z_kernel,
        out_shape=(f32(3 * CX + 2, CY, CZ), block, block),
        in_specs=[smem, vmem, vmem, vmem, vmem],
        name="pack_z",
    )(owners[0, 0], source, log_coef, lateral, state)
    gz, count = lax.axis_index("gz"), lax.axis_size("gz")
    before = lax.ppermute(up, "gz", [(i, (i + 1) % count) for i in range(count)])
    after = lax.ppermute(down, "gz", [(i, (i - 1) % count) for i in range(count)])
    halo = jnp.where(gz > 0, before, 0.0) + jnp.where(gz < count - 1, after, 0.0)
    mine = lax.dynamic_update_slice(mine, halo, (2 * CX, 0, 0))
    g = lax.all_gather(mine, "gx")
    fine, fine1, fine2 = (32, YE, ZE), (33, YE, ZE), (34, YE, ZE)
    mid, mid1, mid2 = (16, YM, ZM), (17, YM, ZM), (18, YM, ZM)
    win, win1, win2 = (XW, YW, ZE), (XW + 1, YW, ZE), (XW + 2, YW, ZE)
    c_rows, s_rows = f32(13, 4 * HY, CZ), f32(11, 4 * HY, CZ)
    c_up, c_down, s_up, s_down = pl.pallas_call(
        pack_y_kernel,
        out_shape=(c_rows, c_rows, s_rows, s_rows),
        compiler_params=params(),
        name="pack_y",
    )(g, state)
    cp, cn = both_ways(c_up, c_down, "gy")
    yp, yn = both_ways(s_up, s_down, "gy")
    wx, wy, wz, inv, c_w, wx_w, wy_w, wz_w, inv_w, mwx, mwy, mwz, minv, low = pl.pallas_call(
        coef_kernel,
        out_shape=(
            f32(*fine1), f32(*fine), f32(*fine), f32(*fine),
            f32(*win), f32(*win1), f32(*win), f32(*win), f32(*win),
            f32(*mid1), f32(*mid), f32(*mid), f32(*mid), f32(3, 8, CZ),
        ),
        scratch_shapes=[vm(*fine2), vm(16, YM, ZE), vm(*mid2)],
        compiler_params=params(),
        name="coef",
    )(g, cp, cn)
    src_w, pre_w, se, mid_pre, mid_rhs, ends, block_s = pl.pallas_call(
        first_kernel,
        out_shape=(
            f32(*win), f32(*win), f32(CX + 2, YW, ZE),
            f32(16, 8, ZM), f32(*mid), f32(16, 8, CZ), f32(3, 8, CZ),
        ),
        scratch_shapes=[
            vm(*fine1), vm(*fine2), vm(*fine2), vm(16, YM, ZE), vm(*mid2), vm(*mid2),
        ],
        compiler_params=params(),
        name="first",
    )(g, cp, cn, yp, yn, state, wx, wy, wz, inv, mwx, mwy, mwz, minv, low)

    rec = lax.all_to_all(ends, "gz", 0, 0, tiled=True)
    tile = f32(16, 8, ZM)
    mid_init, up, down = pl.pallas_call(
        solve_kernel, out_shape=(tile, tile, tile), compiler_params=params(), name="solve"
    )(rec, block_s, mid_pre, mid_rhs)
    mid_p, mid_n = both_ways(up, down, "gy")

    adj, grad = pl.pallas_call(
        second_kernel,
        out_shape=(block, f32(CY, CZ)),
        scratch_shapes=[
            vm(*mid), vm(20, YM, ZM), vm(20, YM, ZM), vm(8, YM, ZE), vm(*win2), vm(*win2),
        ],
        compiler_params=params(),
        name="second",
    )(mid_init, mid_p, mid_n, mid_rhs, mwx, mwy, mwz, minv,
      src_w, pre_w, c_w, wx_w, wy_w, wz_w, inv_w, se)
    sums = lax.all_to_all(grad, "gz", 0, 0, tiled=True)
    total = jnp.sum(sums[:, :CX], axis=0)[:, None]
    return adj, total * (-1.0 / math.sqrt(source.shape[2] * lax.axis_size("gz")))


def solution(mesh):
    placed = (
        P("gx", "gy", "gz"),
        P("gx", "gy", "gz"),
        P("gx", "gy", "gz"),
        P("gx", "gy"),
        P("gx", "gy", None),
    )
    return jax.shard_map(
        per_device,
        mesh=mesh,
        in_specs=placed,
        out_specs=(P("gx", "gy", "gz"), P("gx", ("gy", "gz"))),
        check_vma=False,
    )
```

```python
import functools
import math

import jax
import jax.numpy as jnp
from jax import lax
from jax.experimental import pallas as pl
from jax.experimental.pallas import tpu as pltpu
from jax.sharding import PartitionSpec as P

CX, CY, CZ = 8, 16, 128
ANISO = 200.0
OMEGA = 0.8
HC, HS = 10, 9
Y0 = 12
HZ = 18
YE = CY + 2 * Y0
ZE = 2 * CZ
TILES = 11
YM = 24
ZM = CZ
XW = CX + 8
YW = CY + 8
HIGHEST = lax.Precision.HIGHEST


def iota(shape, dim):
    return lax.broadcasted_iota(jnp.int32, shape, dim)


def mm(a, b):
    return jnp.dot(a, b, precision=HIGHEST, preferred_element_type=jnp.float32)


def split(v, axis):
    high = v.astype(jnp.bfloat16)
    v = v - high.astype(jnp.float32)
    mid = v.astype(jnp.bfloat16)
    low = (v - mid.astype(jnp.float32)).astype(jnp.bfloat16)
    return jnp.concatenate([high, mid, low], axis)


def pick_rows(sel, v):
    out = jnp.dot(sel.astype(jnp.bfloat16), split(v, 1), preferred_element_type=jnp.float32)
    n = v.shape[1]
    return out[:, :n] + (out[:, n : 2 * n] + out[:, 2 * n :])


def pick_lanes(v, sel):
    out = jnp.dot(split(v, 0), sel.astype(jnp.bfloat16), preferred_element_type=jnp.float32)
    n = v.shape[0]
    return out[:n] + (out[n : 2 * n] + out[2 * n :])


def nxt(v, axis):
    return pltpu.roll(v, v.shape[axis] - 1, axis)


def prv(v, axis):
    return pltpu.roll(v, 1, axis)


def face(a, b):
    both = a + b
    return jnp.where(jnp.minimum(a, b) == 0.0, both, 0.5 * both)


def unroll(planes):
    return 16 if planes == 16 else 8


def make_weights(c, wx, wy, wz, inv, planes, scale):
    wx[0] = scale * face(c[0], c[1])

    def step(x, carry):
        here = c[x + 1]
        fx = scale * face(here, c[x + 2])
        fy = scale * face(here, nxt(here, 0))
        fz = (scale * ANISO) * face(here, nxt(here, 1))
        wx[x + 1] = fx
        wy[x] = fy
        wz[x] = fz
        total = fx + wx[x] + fy + prv(fy, 0) + fz + prv(fz, 1)
        inv[x] = jnp.where(here > 0.0, OMEGA / total, 0.0)
        return carry

    lax.fori_loop(0, planes, step, 0, unroll=unroll(planes))


def residual(v, b, wx, wy, wz, x, before):
    here = v[x + 1]
    fx = wx[x + 1] * (here - v[x + 2])
    fy = wy[x] * (here - nxt(here, 0))
    fz = wz[x] * (here - nxt(here, 1))
    flow = (fx - before) + (fy - prv(fy, 0)) + (fz - prv(fz, 1))
    return here, b[x] - flow, fx


def sweep(v, out, b, wx, wy, wz, inv, planes):
    def step(x, before):
        here, rest, fx = residual(v, b, wx, wy, wz, x, before)
        out[x + 1] = here + inv[x] * rest
        return fx

    lax.fori_loop(0, planes, step, wx[0] * (0.0 - v[1]), unroll=unroll(planes))


def first_sweeps(out, b, wx, wy, wz, inv, planes):
    def step(x, carry):
        before, here = carry
        after = inv[jnp.minimum(x + 1, planes - 1)] * b[x + 1]
        fx = wx[x + 1] * (here - after)
        fy = wy[x] * (here - nxt(here, 0))
        fz = wz[x] * (here - nxt(here, 1))
        flow = (fx - before) + (fy - prv(fy, 0)) + (fz - prv(fz, 1))
        out[x + 1] = here + inv[x] * (b[x] - flow)
        return fx, after

    here = inv[0] * b[0]
    lax.fori_loop(0, planes, step, (wx[0] * (0.0 - here), here), unroll=unroll(planes))


def pack_z_kernel(
    line_far, src_far, log_coef_far, lateral_far, state_far, mine, down, up,
    line, src, log_coef, lateral, state, sems,
):
    copies = [
        pltpu.make_async_copy(far, near, sems.at[i])
        for i, (far, near) in enumerate(
            (
                (lateral_far, lateral), (log_coef_far, log_coef), (src_far, src),
                (state_far, state), (line_far, line),
            )
        )
    ]
    for copy in copies:
        copy.start()
    for copy in copies:
        copy.wait()
    gz = lax.axis_index("gz")
    cut = (line[0, 0, gz] != line[0, 0, jnp.minimum(gz + 1, 15)]).astype(jnp.float32)
    pick = (iota((CX * CY, CX), 0) // CY == iota((CX * CY, CX), 1)).astype(jnp.float32)
    rows = mm(pick, lateral[...])
    own = iota((CX * CY, CY), 0) % CY == iota((CX * CY, CY), 1)
    rows = jnp.sum(jnp.where(own, rows, 0.0), axis=1, keepdims=True)
    rows = jnp.broadcast_to(rows, (CX * CY, CZ)).reshape(CX, CY, CZ)
    c = jnp.exp(log_coef[...] + rows)
    s = src[...]
    mine[0:CX] = s
    mine[CX : 2 * CX] = c
    mine[3 * CX] = state[0]
    mine[3 * CX + 1] = state[CX - 1]
    lane = iota((CX, CY, CZ), 2)
    k = pltpu.roll(c, 64, 2)
    t = pltpu.roll(state[...], 32, 2)
    zero = jnp.zeros_like(s)
    far = CZ - HZ
    coef = jnp.where((lane >= 64) & (lane < 64 + HZ), k, zero)
    down[...] = jnp.where(lane < HZ, s, jnp.where(lane == 32, t, coef))
    coef = jnp.where((lane >= far - 64) & (lane < 64), k, zero)
    coef = jnp.where(lane == 20, cut, coef)
    up[...] = jnp.where(lane >= far, s, jnp.where(lane == 31, t, coef))


def pack_y_kernel(g, state, c_up, c_down, s_up, s_down):
    lane = iota((CY, CZ), 1)
    planes = 4 * CX + TILES
    for coef, h, up, down in ((1, HC, c_up, c_down), (0, HS, s_up, s_down)):

        def put(n, plane):
            up[h * n : h * n + h] = plane[CY - h :]
            down[h * n : h * n + h] = plane[:h]

        for s in range(4):
            for i in range(CX):
                put(CX * s + i, g[s, CX * coef + i])
        for t in range(TILES):
            plane = jnp.zeros((CY, CZ), jnp.float32)
            for x in range(3 * t, min(3 * t + 3, 4 * CX)):
                off = 2 * HZ * (x % 3)
                move = off - 46 if coef else off + HZ
                halo = pltpu.roll(g[x // CX, 2 * CX + x % CX], move % CZ, 1)
                plane = jnp.where(lane >= off, halo, plane)
            put(4 * CX + t, plane)
        end = h * planes
        if coef:
            for i in range(CX):
                up[end + i : end + i + 1] = state[i, CY - 1 :]
                down[end + i : end + i + 1] = state[i, :1]
            end += CX
        none = jnp.zeros((up.shape[0] - end, CZ), jnp.float32)
        up[end:] = none
        down[end:] = none


def place(out, lanes, low, own, high):
    h = low.shape[0]
    out[Y0 - h : Y0, lanes] = low
    out[Y0 : Y0 + CY, lanes] = own
    out[Y0 + CY : Y0 + CY + h, lanes] = high


def edge_lanes(v, move):
    v = pltpu.roll(v, move % CZ, 1) if move % CZ else v
    lane = iota(v.shape, 1)
    return jnp.where((lane < HZ) | (lane >= CZ - HZ), v, 0.0)


def fill(out, g, yp, yn, x, coef):
    s, i = x // CX, x % CX
    none = jnp.zeros((8, ZE), jnp.float32)
    out[0:8] = none
    out[YE - 8 :] = none
    h = HC if coef else HS
    at = slice(h * x, h * x + h)
    place(out, LOW, yp[at], g[s, CX * coef + i], yn[at])
    n, move = 4 * CX + x // 3, CZ - HZ - 2 * HZ * (x % 3)
    at = slice(h * n, h * n + h)
    place(
        out, HIGH, edge_lanes(yp[at], move),
        edge_lanes(g[s, 2 * CX + i], 64 * coef), edge_lanes(yn[at], move),
    )


LOW, HIGH = slice(0, CZ), slice(CZ, ZE)


def window(gx, pairs, planes):
    nx = 4 * CX

    def keep(w, carry):
        for out, ref, shift, first in pairs:
            x = CX * gx - 4 + w - first
            inside = (x >= -first) & (x < nx)
            at = jnp.clip(x, -first, nx - 1) + shift
            out[w] = jnp.where(inside, ref[at, 8:32], 0.0)
        return carry

    lax.fori_loop(0, planes, keep, 0, unroll=4)


def fold_y():
    return (iota((YM, YE), 1) // 2 + 2 == iota((YM, YE), 0)).astype(jnp.float32)


def fold_z():
    return (iota((ZE, ZM), 0) // 2 == iota((ZE, ZM), 1)).astype(jnp.float32) * 0.125


def fold_low(first, count):
    shape = (8 * count, 16 * YM)
    to, frm = iota(shape, 0), iota(shape, 1)
    m, r = frm // YM, frm % YM
    return ((m // 2 == to % 8) & (r // 2 - 4 == to // 8 + first)).astype(jnp.float32) * 0.125


def squeeze():
    m, l = iota((ZM, CZ), 0), iota((ZM, CZ), 1)
    m = jnp.where(m < 96, m, m - 128)
    return ((m + 8) // 2 == l).astype(jnp.float32)


def gather(v):
    lane = iota((8, CZ), 1)
    out = pltpu.roll(v[0], CZ - 4, 1)
    for y in range(1, 4):
        out = jnp.where(lane >= 32 * y, pltpu.roll(v[y], 32 * y - 4, 1), out)
    return out


def coef_kernel(
    g, yp, yn,
    wx, wy, wz, inv, c_w, wx_w, wy_w, wz_w, inv_w, mwx, mwy, mwz, minv, low_o,
    c, t, mc,
):
    gx, gz = lax.axis_index("gx"), lax.axis_index("gz")
    zero = jnp.zeros((YE, ZE), jnp.float32)
    nx = 4 * CX
    c[0] = zero
    c[nx + 1] = zero
    for x in range(nx):
        fill(c.at[x + 1], g, yp, yn, x, 1)
    make_weights(c, wx, wy, wz, inv, nx, 1.0)
    rows = fold_y()

    def coarse(m, carry):
        t[m] = pick_rows(rows, c[2 * m + 1] + c[2 * m + 2])
        return carry

    lax.fori_loop(0, 16, coarse, 0, unroll=8)
    mid_zero = jnp.zeros((YM, ZM), jnp.float32)
    mc[0] = mid_zero
    mc[17] = mid_zero
    mc[1:17] = pick_lanes(t[...].reshape(16 * YM, ZE), fold_z()).reshape(16, YM, ZM)
    make_weights(mc, mwx, mwy, mwz, minv, 16, 0.25)
    window(gx, [(c_w, c, 1, 0), (wy_w, wy, 0, 0), (wz_w, wz, 0, 0), (inv_w, inv, 0, 0)], XW)
    window(gx, [(wx_w, wx, 1, 1)], XW + 1)

    low_c = pick_lanes(pick_rows(fold_low(-1, 6), mc[1:17].reshape(16 * YM, ZM)), squeeze())
    low_c = low_c.reshape(6, 8, CZ)
    here = low_c[1:5]
    row = iota((4, 8, CZ), 1)
    scale = 0.0625
    fx1 = scale * face(here, jnp.where(row < 7, nxt(here, 1), 0.0))
    fx0 = scale * face(here, jnp.where(row > 0, prv(here, 1), 0.0))
    fy1 = scale * face(here, low_c[2:6])
    fy0 = scale * face(here, low_c[0:4])
    fz = (scale * ANISO) * face(here, nxt(here, 2))
    lower = prv(fz, 2)
    total = fx1 + fx0 + fy1 + fy0 + fz + lower

    flag = pltpu.roll(g[3, 16, 0:8], CZ - 20, 1)
    row = iota((8, CZ), 0)
    for s in range(2, -1, -1):
        flag = jnp.where(row < 2 * s + 2, pltpu.roll(g[s, 16, 0:8], CZ - 20, 1), flag)
    flag = jnp.broadcast_to(flag[:, 0:1], (8, CZ))
    e = gather(lower)
    top = iota((8, CZ), 1) % 32 == 0
    low_o[0] = gather(total)
    low_o[1] = jnp.where(top, 0.0, e)
    low_o[2] = jnp.where(top & (flag == 0.0) & (gz > 0), e, 0.0)


def first_kernel(
    g, cp, cn, yp, yn, state, wx, wy, wz, inv, mwx, mwy, mwz, minv, low,
    src_w, pre_w, se, mid_pre_o, mb, low_o, block_o,
    b, va, vb, t, mva, mvb,
):
    gx = lax.axis_index("gx")
    zero = jnp.zeros((YE, ZE), jnp.float32)
    nx = 4 * CX
    for ref in (va, vb):
        ref[0] = zero
        ref[nx + 1] = zero
    for x in range(nx):
        fill(b.at[x], g, yp, yn, x, 0)
    b[nx] = zero
    first_sweeps(va, b, wx, wy, wz, inv, nx)
    sweep(va, vb, b, wx, wy, wz, inv, nx)

    rows = fold_y()

    def coarse(m, before):
        x = 2 * m
        _, one, fx = residual(vb, b, wx, wy, wz, x, before)
        _, two, fx = residual(vb, b, wx, wy, wz, x + 1, fx)
        t[m] = pick_rows(rows, one + two)
        return fx

    lax.fori_loop(0, 16, coarse, wx[0] * (0.0 - vb[1]), unroll=8)
    mb[...] = pick_lanes(t[...].reshape(16 * YM, ZE), fold_z()).reshape(16, YM, ZM)
    mid_zero = jnp.zeros((YM, ZM), jnp.float32)
    for ref in (mva, mvb):
        ref[0] = mid_zero
        ref[17] = mid_zero

    window(gx, [(src_w, b, 0, 0), (pre_w, vb, 1, 0)], XW)

    zero8 = jnp.zeros((8, CZ), jnp.float32)
    wide = jnp.zeros((YW, CZ), jnp.float32)
    row = iota((YW, CZ), 0)
    lane = iota((YW, CZ), 1)
    left = g[jnp.maximum(gx - 1, 0), 25]
    right = g[jnp.minimum(gx + 1, 3), 24]
    left = jnp.where(gx > 0, left, 0.0)
    right = jnp.where(gx < 3, right, 0.0)
    for at, plane in ((0, left), (9, right)):
        mid = pltpu.roll(jnp.concatenate([plane, zero8], 0), 4, 0)
        se[at] = jnp.concatenate([mid, wide], 1)
    for i in range(CX):
        mid = pltpu.roll(jnp.concatenate([state[i], zero8], 0), 4, 0)
        n = HC * (4 * CX + TILES) + i
        under, over = cp[n : n + 1], cn[n : n + 1]
        mid = jnp.where(row == 3, under, jnp.where(row == 20, over, mid))
        halo = pltpu.roll(jnp.concatenate([g[gx, 16 + i], zero8], 0), 4, 0)
        halo = pltpu.roll(halo, CZ - 32, 1)
        halo = jnp.where((lane == 0) | (lane == CZ - 1), halo, 0.0)
        se[i + 1] = jnp.concatenate([mid, halo], 1)

    mva[1:17] = minv[...] * mb[...]
    sweep(mva, mvb, mb, mwx, mwy, mwz, minv, 16)
    sweep(mvb, mva, mb, mwx, mwy, mwz, minv, 16)

    def rest(x, before):
        _, r, fx = residual(mva, mb, mwx, mwy, mwz, x, before)
        mvb[x + 1] = r
        mid_pre_o[x] = mva[x + 1, 8:16]
        return fx

    lax.fori_loop(0, 16, rest, mwx[0] * (0.0 - mva[1]), unroll=16)

    rhs = pick_lanes(pick_rows(fold_low(0, 4), mvb[1:17].reshape(16 * YM, ZM)), squeeze()).reshape(4, 8, CZ)
    depth = iota((8, CZ), 1) % 32
    top = depth == 0
    r, d, e, edge = gather(rhs), low[0], low[1], low[2]
    v = jnp.where(top, 1.0, 0.0)
    w = jnp.where(depth == 31, 1.0, 0.0)
    for k in range(5):
        s = 1 << k
        back = CZ - s
        inv = 1.0 / d
        t = e * inv
        alpha = e * pltpu.roll(inv, s, 1)
        r, v, w = [
            q + alpha * pltpu.roll(q, s, 1) + pltpu.roll(t * q, back, 1) for q in (r, v, w)
        ]
        d = d - alpha * e - pltpu.roll(t * e, back, 1)
        e = alpha * pltpu.roll(e, s, 1)
    inv = 1.0 / d
    r, v, w = r * inv, v * inv, w * inv
    block_o[0] = r
    block_o[1] = v
    block_o[2] = w
    packed = jnp.where((depth < 3) | (depth >= 29), r, 0.0)
    packed = jnp.where((depth >= 3) & (depth < 6), pltpu.roll(v, 3, 1), packed)
    packed = jnp.where((depth >= 26) & (depth < 29), pltpu.roll(v, CZ - 3, 1), packed)
    packed = jnp.where((depth >= 6) & (depth < 9), pltpu.roll(w, 6, 1), packed)
    packed = jnp.where((depth >= 23) & (depth < 26), pltpu.roll(w, CZ - 6, 1), packed)
    packed = jnp.where(depth == 9, pltpu.roll(edge, 9, 1), packed)
    for p in range(16):
        low_o[p] = packed


def solve_kernel(rec, block, mid_pre, mid_rhs, out, up, down):
    gz = lax.axis_index("gz")
    lane = iota((8, CZ), 1)
    depth = lane % 32

    def take(v, at):
        return pltpu.roll(v, (CZ - at) % CZ, 1) if at else v

    def parts(offset):
        p = gz + offset
        v = rec[jnp.clip(p, 0, 15)]
        low = take(v, 0), take(v, 3), take(v, 6)
        high = take(v, 31), take(v, 28), take(v, 25)
        return v, low, high, jnp.where((p >= 0) & (p <= 15), take(v, 9), 0.0)

    every = {k: parts(k) for k in range(-4, 5)}
    zero = jnp.zeros((8, CZ), jnp.float32)

    a, b = {-5: zero}, {-5: zero}
    f, g = {}, {}
    for k in range(-4, 1):
        _, (y0, v0, w0), (y1, v1, w1), e = every[k]
        left, more = e * a[k - 1], e * e * b[k - 1]
        den = 1.0 / (1.0 - v0 * more)
        f[k] = (y0 + v0 * left) * den
        g[k] = w0 * den
        a[k] = y1 + v1 * (left + more * f[k])
        b[k] = w1 + v1 * (more * g[k])
    ra, rb = {5: zero}, {5: zero}
    rf, rg = {}, {}
    e_next = zero
    for k in range(4, 0, -1):
        _, (y0, v0, w0), (y1, v1, w1), e = every[k]
        right, more = e_next * ra[k + 1], e_next * e_next * rb[k + 1]
        den = 1.0 / (1.0 - w1 * more)
        rf[k] = (y1 + w1 * right) * den
        rg[k] = v1 * den
        ra[k] = y0 + w0 * (right + more * rf[k])
        rb[k] = v0 + w0 * (more * rg[k])
        e_next = e
    e0, e1 = every[0][3], every[1][3]
    last = (a[0] + b[0] * e1 * ra[1]) / (1.0 - b[0] * e1 * e1 * rb[1])
    right = e1 * (ra[1] + rb[1] * (e1 * last))
    first = f[0] + g[0] * right
    left = e0 * (a[-1] + b[-1] * (e0 * first))
    before = f[-1] + g[-1] * (e0 * first)
    em = every[-1][3]
    left_m, right_m = em * (a[-2] + b[-2] * (em * before)), e0 * first
    after = rf[1] + rg[1] * (e1 * last)
    ep = every[2][3]
    left_p, right_p = e1 * last, ep * (ra[2] + rb[2] * (ep * after))

    ends = jnp.concatenate([left, right, left_m, right_m, left_p, right_p], 0)
    ends = jnp.where(iota((48, CZ), 1) % 32 == 0, ends, 0.0)
    copy = (iota((CZ, CZ), 1) // 32 * 32 == iota((CZ, CZ), 0)).astype(jnp.float32)
    ends = pick_lanes(ends, copy).reshape(6, 8, CZ)
    own = block[0] + block[1] * ends[0] + block[2] * ends[1]
    v = every[-1][0]
    low = v + pltpu.roll(v, 3, 1) * ends[2] + pltpu.roll(v, 6, 1) * ends[3]
    low = jnp.where((depth >= 29) & (gz > 0), low, 0.0)
    v = every[1][0]
    high = v + pltpu.roll(v, CZ - 3, 1) * ends[4] + pltpu.roll(v, CZ - 6, 1) * ends[5]
    high = jnp.where((depth < 3) & (gz < 15), high, 0.0)

    rows = []
    for y in range(4):
        part = jnp.where(lane < 32, take(own, 32 * y), 0.0)
        part = jnp.where((lane >= 32) & (lane < 64), take(high, (32 * y - 32) % CZ), part)
        part = jnp.where(lane >= 96, take(low, (32 * y + 32) % CZ), part)
        rows.append(part)
    rows = jnp.concatenate(rows, 0)
    k, m = iota((CZ, ZM), 0), iota((CZ, ZM), 1)
    spread_z = (k == jnp.where(m < 96, m // 2, m // 2 + 64)).astype(jnp.float32)
    to, frm = iota((128, 32), 0), iota((128, 32), 1)
    spread = ((to // 16 == frm % 8) & ((to % 8) // 2 == frm // 8)).astype(jnp.float32)
    mid = mid_pre[...] + pick_rows(spread, pick_lanes(rows, spread_z)).reshape(16, 8, ZM)
    out[...] = mid
    for x in range(16):
        up[6 * x : 6 * x + 5] = mid[x, 3:]
        up[6 * x + 5 : 6 * x + 6] = mid_rhs[x, 12:13]
        down[6 * x : 6 * x + 5] = mid[x, :5]
        down[6 * x + 5 : 6 * x + 6] = mid_rhs[x, 11:12]


def second_kernel(
    scale, mid, mid_p, mid_n, mid_rhs, mwx, mwy, mwz, minv, src_w, pre_w, c, wx, wy, wz, inv, se,
    adj, grad,
    mb, mva, mvb, sp, va, vb,
):
    gx = lax.axis_index("gx")
    mid_zero = jnp.zeros((YM, ZM), jnp.float32)
    none = jnp.zeros((8, ZM), jnp.float32)
    mb[...] = mid_rhs[...]
    for x in range(16):
        mb[x, 4:5] = mid_p[6 * x + 5 : 6 * x + 6]
        mb[x, 19:20] = mid_n[6 * x + 5 : 6 * x + 6]
    for ref in (mva, mvb):
        for at in (0, 1, 18, 19):
            ref[at] = mid_zero
    for x in range(16):
        mva[x + 2, 0:8] = none
        mva[x + 2, 16:24] = none
        mva[x + 2, 3:8] = mid_p[6 * x : 6 * x + 5]
        mva[x + 2, 8:16] = mid[x]
        mva[x + 2, 16:21] = mid_n[6 * x : 6 * x + 5]
    a, o = mva.at[1:19], mvb.at[1:19]
    sweep(a, o, mb, mwx, mwy, mwz, minv, 16)
    sweep(o, a, mb, mwx, mwy, mwz, minv, 16)
    sweep(a, o, mb, mwx, mwy, mwz, minv, 16)

    zero = jnp.zeros((YW, ZE), jnp.float32)
    for ref in (va, vb):
        ref[0] = zero
        ref[XW + 1] = zero
    spread_z = (iota((ZM, ZE), 1) // 2 == iota((ZM, ZE), 0)).astype(jnp.float32)
    spread_y = ((iota((YW, YM), 0) + 12) // 2 == iota((YW, YM), 1)).astype(jnp.float32)
    near = mvb[pl.ds(4 * gx, 8)]
    sp[...] = pick_lanes(near.reshape(8 * YM, ZM), spread_z).reshape(8, YM, ZE)
    for m in range(8):
        more = pick_rows(spread_y, sp[m])
        for x in (2 * m, 2 * m + 1):
            va[x + 1] = pre_w[x] + more
    sweep(va, vb, src_w, wx, wy, wz, inv, XW)
    sweep(vb, va, src_w, wx, wy, wz, inv, XW)
    sweep(va, vb, src_w, wx, wy, wz, inv, XW)

    def product(f, one, two, sone, stwo):
        return f * (one - two) * (sone - stwo)

    def half(one, two):
        return jnp.where(jnp.minimum(one, two) == 0.0, 1.0, 0.5)

    lane = iota((YW, CZ), 1)

    def terms(i, carry):
        before, acc = carry
        v, k, s = vb[i + 5], c[i + 4], se[i + 1]
        px = product(half(k, c[i + 5]), v, vb[i + 6], s, se[i + 2])
        py = product(half(k, nxt(k, 0)), v, nxt(v, 0), s, nxt(s, 0))
        pz = product(half(k, nxt(k, 1)), v, nxt(v, 1), s, nxt(s, 1))
        both = k * (px + before + py + prv(py, 0) + pz + prv(pz, 1))
        part = jnp.sum(both[:, :CZ], axis=1, keepdims=True)
        acc = jnp.where(lane == i, part, acc)
        adj[i] = pltpu.roll(v, YW - 4, 0)[:CY, :CZ]
        return px, acc

    first = product(half(c[3], c[4]), vb[4], vb[5], se[0], se[1])
    _, acc = lax.fori_loop(
        0, CX, terms, (first, jnp.zeros((YW, CZ), jnp.float32)), unroll=8
    )
    grad[...] = pltpu.roll(acc, YW - 4, 0)[:CY] * scale


def f32(*shape):
    return jax.ShapeDtypeStruct(shape, jnp.float32)


def vm(*shape):
    return pltpu.VMEM(shape, jnp.float32)


def params():
    return pltpu.CompilerParams(vmem_limit_bytes=16 << 20)


def both_ways(up, down, axis):
    count = lax.axis_size(axis)
    higher = [(i, i + 1) for i in range(count - 1)]
    lower = [(j, i) for i, j in higher]
    return lax.ppermute(up, axis, higher), lax.ppermute(down, axis, lower)


def per_device(source, state, log_coef, lateral, owners):
    block = f32(CX, CY, CZ)
    far = pl.BlockSpec(memory_space=pltpu.HBM)
    mine, down, up = pl.pallas_call(
        pack_z_kernel,
        out_shape=(f32(3 * CX + 2, CY, CZ), block, block),
        in_specs=[far] * 5,
        scratch_shapes=[
            pltpu.SMEM((1, 1, 16), jnp.int32),
            vm(CX, CY, CZ), vm(CX, CY, CZ), vm(CX, CY), vm(CX, CY, CZ),
            pltpu.SemaphoreType.DMA((5,)),
        ],
        compiler_params=params(),
        name="pack_z",
    )(*[
        pltpu.with_memory_space_constraint(v, pltpu.HBM)
        for v in (owners, source, log_coef, lateral, state)
    ])
    gz, count = lax.axis_index("gz"), lax.axis_size("gz")
    before = lax.ppermute(up, "gz", [(i, (i + 1) % count) for i in range(count)])
    after = lax.ppermute(down, "gz", [(i, (i - 1) % count) for i in range(count)])
    halo = jnp.where(gz > 0, before, 0.0) + jnp.where(gz < count - 1, after, 0.0)
    mine = lax.dynamic_update_slice(mine, halo, (2 * CX, 0, 0))
    g = lax.all_gather(mine, "gx")
    fine, fine1, fine2 = (32, YE, ZE), (33, YE, ZE), (34, YE, ZE)
    mid, mid1, mid2 = (16, YM, ZM), (17, YM, ZM), (18, YM, ZM)
    win, win1, win2 = (XW, YW, ZE), (XW + 1, YW, ZE), (XW + 2, YW, ZE)
    c_rows, s_rows = f32(440, CZ), f32(392, CZ)
    c_up, c_down, s_up, s_down = pl.pallas_call(
        pack_y_kernel,
        out_shape=(c_rows, c_rows, s_rows, s_rows),
        compiler_params=params(),
        name="pack_y",
    )(g, state)
    cp, cn = both_ways(c_up, c_down, "gy")
    yp, yn = both_ways(s_up, s_down, "gy")
    wx, wy, wz, inv, c_w, wx_w, wy_w, wz_w, inv_w, mwx, mwy, mwz, minv, low = pl.pallas_call(
        coef_kernel,
        out_shape=(
            f32(*fine1), f32(*fine), f32(*fine), f32(*fine),
            f32(*win), f32(*win1), f32(*win), f32(*win), f32(*win),
            f32(*mid1), f32(*mid), f32(*mid), f32(*mid), f32(3, 8, CZ),
        ),
        scratch_shapes=[vm(*fine2), vm(16, YM, ZE), vm(*mid2)],
        compiler_params=params(),
        name="coef",
    )(g, cp, cn)
    src_w, pre_w, se, mid_pre, mid_rhs, ends, block_s = pl.pallas_call(
        first_kernel,
        out_shape=(
            f32(*win), f32(*win), f32(CX + 2, YW, ZE),
            f32(16, 8, ZM), f32(*mid), f32(16, 8, CZ), f32(3, 8, CZ),
        ),
        scratch_shapes=[
            vm(*fine1), vm(*fine2), vm(*fine2), vm(16, YM, ZE), vm(*mid2), vm(*mid2),
        ],
        compiler_params=params(),
        name="first",
    )(g, cp, cn, yp, yn, state, wx, wy, wz, inv, mwx, mwy, mwz, minv, low)

    rec = lax.all_to_all(ends, "gz", 0, 0, tiled=True)
    tile = f32(16, 8, ZM)
    mid_init, up, down = pl.pallas_call(
        solve_kernel, out_shape=(tile, f32(96, ZM), f32(96, ZM)), compiler_params=params(), name="solve"
    )(rec, block_s, mid_pre, mid_rhs)
    mid_p, mid_n = both_ways(up, down, "gy")

    scale = -1.0 / math.sqrt(source.shape[2] * count)
    adj, grad = pl.pallas_call(
        functools.partial(second_kernel, scale),
        out_shape=(f32(CX, CY, CZ), f32(CY, CZ)),
        scratch_shapes=[
            vm(*mid), vm(20, YM, ZM), vm(20, YM, ZM), vm(8, YM, ZE), vm(*win2), vm(*win2),
        ],
        compiler_params=params(),
        name="second",
    )(mid_init, mid_p, mid_n, mid_rhs, mwx, mwy, mwz, minv,
      src_w, pre_w, c_w, wx_w, wy_w, wz_w, inv_w, se)
    sums = lax.all_to_all(grad, "gz", 0, 0, tiled=True)
    return adj, jnp.sum(sums[:, :CX], axis=0)[:, None]


def solution(mesh):
    placed = (
        P("gx", "gy", "gz"),
        P("gx", "gy", "gz"),
        P("gx", "gy", "gz"),
        P("gx", "gy"),
        P("gx", "gy", None),
    )
    return jax.shard_map(
        per_device,
        mesh=mesh,
        in_specs=placed,
        out_specs=(P("gx", "gy", "gz"), P("gx", ("gy", "gz"))),
        check_vma=False,
    )
```

```python
import functools
import math

import jax
import jax.numpy as jnp
from jax import lax
from jax.experimental import pallas as pl
from jax.experimental.pallas import tpu as pltpu
from jax.sharding import PartitionSpec as P

CX, CY, CZ = 8, 16, 128
ANISO = 200.0
OMEGA = 0.8
HC, HS = 10, 9
Y0 = 12
HZ = 18
YE = CY + 2 * Y0
ZE = 2 * CZ
TILES = 11
YM = 24
ZM = CZ
XW = CX + 8
YW = CY + 8
HIGHEST = lax.Precision.HIGHEST


def iota(shape, dim):
    return lax.broadcasted_iota(jnp.int32, shape, dim)


def mm(a, b):
    return jnp.dot(a, b, precision=HIGHEST, preferred_element_type=jnp.float32)


def split(v, axis):
    high = v.astype(jnp.bfloat16)
    v = v - high.astype(jnp.float32)
    mid = v.astype(jnp.bfloat16)
    low = (v - mid.astype(jnp.float32)).astype(jnp.bfloat16)
    return jnp.concatenate([high, mid, low], axis)


def pick_rows(sel, v):
    out = jnp.dot(sel.astype(jnp.bfloat16), split(v, 1), preferred_element_type=jnp.float32)
    n = v.shape[1]
    return out[:, :n] + (out[:, n : 2 * n] + out[:, 2 * n :])


def pick_lanes(v, sel):
    out = jnp.dot(split(v, 0), sel.astype(jnp.bfloat16), preferred_element_type=jnp.float32)
    n = v.shape[0]
    return out[:n] + (out[n : 2 * n] + out[2 * n :])


def nxt(v, axis):
    return pltpu.roll(v, v.shape[axis] - 1, axis)


def prv(v, axis):
    return pltpu.roll(v, 1, axis)


def face(a, b):
    both = a + b
    return jnp.where(jnp.minimum(a, b) == 0.0, both, 0.5 * both)


def unroll(planes):
    return 16 if planes == 16 else 8


def make_weights(c, wx, wy, wz, inv, planes, scale):
    wx[0] = scale * face(c[0], c[1])

    def step(x, carry):
        here = c[x + 1]
        fx = scale * face(here, c[x + 2])
        fy = scale * face(here, nxt(here, 0))
        fz = (scale * ANISO) * face(here, nxt(here, 1))
        wx[x + 1] = fx
        wy[x] = fy
        wz[x] = fz
        total = fx + wx[x] + fy + prv(fy, 0) + fz + prv(fz, 1)
        inv[x] = jnp.where(here > 0.0, OMEGA / total, 0.0)
        return carry

    lax.fori_loop(0, planes, step, 0, unroll=unroll(planes))


def residual(v, b, wx, wy, wz, x, before):
    here = v[x + 1]
    fx = wx[x + 1] * (here - v[x + 2])
    fy = wy[x] * (here - nxt(here, 0))
    fz = wz[x] * (here - nxt(here, 1))
    flow = (fx - before) + (fy - prv(fy, 0)) + (fz - prv(fz, 1))
    return here, b[x] - flow, fx


def sweep(v, out, b, wx, wy, wz, inv, planes):
    def step(x, before):
        here, rest, fx = residual(v, b, wx, wy, wz, x, before)
        out[x + 1] = here + inv[x] * rest
        return fx

    lax.fori_loop(0, planes, step, wx[0] * (0.0 - v[1]), unroll=unroll(planes))


def first_sweeps(out, b, wx, wy, wz, inv, planes):
    def step(x, carry):
        before, here = carry
        after = inv[jnp.minimum(x + 1, planes - 1)] * b[x + 1]
        fx = wx[x + 1] * (here - after)
        fy = wy[x] * (here - nxt(here, 0))
        fz = wz[x] * (here - nxt(here, 1))
        flow = (fx - before) + (fy - prv(fy, 0)) + (fz - prv(fz, 1))
        out[x + 1] = here + inv[x] * (b[x] - flow)
        return fx, after

    here = inv[0] * b[0]
    lax.fori_loop(0, planes, step, (wx[0] * (0.0 - here), here), unroll=unroll(planes))


def pack_z_kernel(
    line_far, src_far, log_coef_far, lateral_far, state_far, mine, down, up,
    line, src, log_coef, lateral, state, sems,
):
    copies = [
        pltpu.make_async_copy(far, near, sems.at[i])
        for i, (far, near) in enumerate(
            (
                (lateral_far, lateral), (log_coef_far, log_coef), (src_far, src),
                (state_far, state), (line_far, line),
            )
        )
    ]
    for copy in copies:
        copy.start()
    copies[0].wait()
    gz = lax.axis_index("gz")
    pick = (iota((CX * CY, CX), 0) // CY == iota((CX * CY, CX), 1)).astype(jnp.float32)
    rows = pick_rows(pick, lateral[...])
    own = iota((CX * CY, CY), 0) % CY == iota((CX * CY, CY), 1)
    rows = jnp.sum(jnp.where(own, rows, 0.0), axis=1, keepdims=True)
    rows = jnp.broadcast_to(rows, (CX * CY, CZ)).reshape(CX, CY, CZ)
    for copy in copies[1:]:
        copy.wait()
    cut = (line[0, 0, gz] != line[0, 0, jnp.minimum(gz + 1, 15)]).astype(jnp.float32)
    c = jnp.exp(log_coef[...] + rows)
    s = src[...]
    mine[0:CX] = s
    mine[CX : 2 * CX] = c
    mine[3 * CX] = state[0]
    mine[3 * CX + 1] = state[CX - 1]
    lane = iota((CX, CY, CZ), 2)
    k = pltpu.roll(c, 64, 2)
    t = pltpu.roll(state[...], 32, 2)
    zero = jnp.zeros_like(s)
    far = CZ - HZ
    coef = jnp.where((lane >= 64) & (lane < 64 + HZ), k, zero)
    down[...] = jnp.where(lane < HZ, s, jnp.where(lane == 32, t, coef))
    coef = jnp.where((lane >= far - 64) & (lane < 64), k, zero)
    coef = jnp.where(lane == 20, cut, coef)
    up[...] = jnp.where(lane >= far, s, jnp.where(lane == 31, t, coef))


def pack_y_kernel(g, state, c_up, c_down, s_up, s_down):
    lane = iota((CY, CZ), 1)
    planes = 4 * CX + TILES
    for coef, h, up, down in ((1, HC, c_up, c_down), (0, HS, s_up, s_down)):

        def put(n, plane):
            up[h * n : h * n + h] = plane[CY - h :]
            down[h * n : h * n + h] = plane[:h]

        for s in range(4):
            for i in range(CX):
                put(CX * s + i, g[s, CX * coef + i])
        for t in range(TILES):
            plane = jnp.zeros((CY, CZ), jnp.float32)
            for x in range(3 * t, min(3 * t + 3, 4 * CX)):
                off = 2 * HZ * (x % 3)
                move = off - 46 if coef else off + HZ
                halo = pltpu.roll(g[x // CX, 2 * CX + x % CX], move % CZ, 1)
                plane = jnp.where(lane >= off, halo, plane)
            put(4 * CX + t, plane)
        end = h * planes
        if coef:
            for i in range(CX):
                up[end + i : end + i + 1] = state[i, CY - 1 :]
                down[end + i : end + i + 1] = state[i, :1]
            end += CX
        none = jnp.zeros((up.shape[0] - end, CZ), jnp.float32)
        up[end:] = none
        down[end:] = none


def place(out, lanes, low, own, high):
    h = low.shape[0]
    out[Y0 - h : Y0, lanes] = low
    out[Y0 : Y0 + CY, lanes] = own
    out[Y0 + CY : Y0 + CY + h, lanes] = high


def edge_lanes(v, move):
    v = pltpu.roll(v, move % CZ, 1) if move % CZ else v
    lane = iota(v.shape, 1)
    return jnp.where((lane < HZ) | (lane >= CZ - HZ), v, 0.0)


def fill(out, g, yp, yn, x, coef):
    s, i = x // CX, x % CX
    none = jnp.zeros((8, ZE), jnp.float32)
    out[0:8] = none
    out[YE - 8 :] = none
    h = HC if coef else HS
    at = slice(h * x, h * x + h)
    place(out, LOW, yp[at], g[s, CX * coef + i], yn[at])
    n, move = 4 * CX + x // 3, CZ - HZ - 2 * HZ * (x % 3)
    at = slice(h * n, h * n + h)
    place(
        out, HIGH, edge_lanes(yp[at], move),
        edge_lanes(g[s, 2 * CX + i], 64 * coef), edge_lanes(yn[at], move),
    )


LOW, HIGH = slice(0, CZ), slice(CZ, ZE)


def window(gx, pairs, planes):
    nx = 4 * CX

    def keep(w, carry):
        for out, ref, shift, first in pairs:
            x = CX * gx - 4 + w - first
            inside = (x >= -first) & (x < nx)
            at = jnp.clip(x, -first, nx - 1) + shift
            out[w] = jnp.where(inside, ref[at, 8:32], 0.0)
        return carry

    lax.fori_loop(0, planes, keep, 0, unroll=4)


def fold_y():
    return (iota((YM, YE), 1) // 2 + 2 == iota((YM, YE), 0)).astype(jnp.float32)


def fold_z():
    return (iota((ZE, ZM), 0) // 2 == iota((ZE, ZM), 1)).astype(jnp.float32) * 0.125


def fold_low(first, count):
    shape = (8 * count, 16 * YM)
    to, frm = iota(shape, 0), iota(shape, 1)
    m, r = frm // YM, frm % YM
    return ((m // 2 == to % 8) & (r // 2 - 4 == to // 8 + first)).astype(jnp.float32) * 0.125


def squeeze():
    m, l = iota((ZM, CZ), 0), iota((ZM, CZ), 1)
    m = jnp.where(m < 96, m, m - 128)
    return ((m + 8) // 2 == l).astype(jnp.float32)


def gather(v):
    lane = iota((8, CZ), 1)
    out = pltpu.roll(v[0], CZ - 4, 1)
    for y in range(1, 4):
        out = jnp.where(lane >= 32 * y, pltpu.roll(v[y], 32 * y - 4, 1), out)
    return out


def coef_kernel(
    g, yp, yn,
    wx, wy, wz, inv, c_w, wx_w, wy_w, wz_w, inv_w, mwx, mwy, mwz, minv, low_o,
    c, t, mc,
):
    gx, gz = lax.axis_index("gx"), lax.axis_index("gz")
    zero = jnp.zeros((YE, ZE), jnp.float32)
    nx = 4 * CX
    c[0] = zero
    c[nx + 1] = zero
    for x in range(nx):
        fill(c.at[x + 1], g, yp, yn, x, 1)
    make_weights(c, wx, wy, wz, inv, nx, 1.0)
    rows = fold_y()

    def coarse(m, carry):
        t[m] = pick_rows(rows, c[2 * m + 1] + c[2 * m + 2])
        return carry

    lax.fori_loop(0, 16, coarse, 0, unroll=16)
    mid_zero = jnp.zeros((YM, ZM), jnp.float32)
    mc[0] = mid_zero
    mc[17] = mid_zero
    mc[1:17] = pick_lanes(t[...].reshape(16 * YM, ZE), fold_z()).reshape(16, YM, ZM)
    make_weights(mc, mwx, mwy, mwz, minv, 16, 0.25)
    window(gx, [(c_w, c, 1, 0), (wy_w, wy, 0, 0), (wz_w, wz, 0, 0), (inv_w, inv, 0, 0)], XW)
    window(gx, [(wx_w, wx, 1, 1)], XW + 1)

    low_c = pick_lanes(pick_rows(fold_low(-1, 6), mc[1:17].reshape(16 * YM, ZM)), squeeze())
    low_c = low_c.reshape(6, 8, CZ)
    here = low_c[1:5]
    row = iota((4, 8, CZ), 1)
    scale = 0.0625
    fx1 = scale * face(here, jnp.where(row < 7, nxt(here, 1), 0.0))
    fx0 = scale * face(here, jnp.where(row > 0, prv(here, 1), 0.0))
    fy1 = scale * face(here, low_c[2:6])
    fy0 = scale * face(here, low_c[0:4])
    fz = (scale * ANISO) * face(here, nxt(here, 2))
    lower = prv(fz, 2)
    total = fx1 + fx0 + fy1 + fy0 + fz + lower

    flag = pltpu.roll(g[3, 16, 0:8], CZ - 20, 1)
    row = iota((8, CZ), 0)
    for s in range(2, -1, -1):
        flag = jnp.where(row < 2 * s + 2, pltpu.roll(g[s, 16, 0:8], CZ - 20, 1), flag)
    flag = jnp.broadcast_to(flag[:, 0:1], (8, CZ))
    e = gather(lower)
    top = iota((8, CZ), 1) % 32 == 0
    low_o[0] = gather(total)
    low_o[1] = jnp.where(top, 0.0, e)
    low_o[2] = jnp.where(top & (flag == 0.0) & (gz > 0), e, 0.0)


def first_kernel(
    g, cp, cn, yp, yn, state, wx, wy, wz, inv, mwx, mwy, mwz, minv, low,
    src_w, pre_w, se, mid_pre_o, mb, low_o, block_o,
    b, va, vb, t, mva, mvb,
):
    gx = lax.axis_index("gx")
    zero = jnp.zeros((YE, ZE), jnp.float32)
    nx = 4 * CX
    for ref in (va, vb):
        ref[0] = zero
        ref[nx + 1] = zero
    for x in range(nx):
        fill(b.at[x], g, yp, yn, x, 0)
    b[nx] = zero
    first_sweeps(va, b, wx, wy, wz, inv, nx)
    sweep(va, vb, b, wx, wy, wz, inv, nx)

    rows = fold_y()

    def coarse(m, before):
        x = 2 * m
        _, one, fx = residual(vb, b, wx, wy, wz, x, before)
        _, two, fx = residual(vb, b, wx, wy, wz, x + 1, fx)
        t[m] = pick_rows(rows, one + two)
        return fx

    lax.fori_loop(0, 16, coarse, wx[0] * (0.0 - vb[1]), unroll=16)
    mb[...] = pick_lanes(t[...].reshape(16 * YM, ZE), fold_z()).reshape(16, YM, ZM)
    mid_zero = jnp.zeros((YM, ZM), jnp.float32)
    for ref in (mva, mvb):
        ref[0] = mid_zero
        ref[17] = mid_zero

    window(gx, [(src_w, b, 0, 0), (pre_w, vb, 1, 0)], XW)

    zero8 = jnp.zeros((8, CZ), jnp.float32)
    wide = jnp.zeros((YW, CZ), jnp.float32)
    row = iota((YW, CZ), 0)
    lane = iota((YW, CZ), 1)
    left = g[jnp.maximum(gx - 1, 0), 25]
    right = g[jnp.minimum(gx + 1, 3), 24]
    left = jnp.where(gx > 0, left, 0.0)
    right = jnp.where(gx < 3, right, 0.0)
    for at, plane in ((0, left), (9, right)):
        mid = pltpu.roll(jnp.concatenate([plane, zero8], 0), 4, 0)
        se[at] = jnp.concatenate([mid, wide], 1)
    for i in range(CX):
        mid = pltpu.roll(jnp.concatenate([state[i], zero8], 0), 4, 0)
        n = HC * (4 * CX + TILES) + i
        under, over = cp[n : n + 1], cn[n : n + 1]
        mid = jnp.where(row == 3, under, jnp.where(row == 20, over, mid))
        halo = pltpu.roll(jnp.concatenate([g[gx, 16 + i], zero8], 0), 4, 0)
        halo = pltpu.roll(halo, CZ - 32, 1)
        halo = jnp.where((lane == 0) | (lane == CZ - 1), halo, 0.0)
        se[i + 1] = jnp.concatenate([mid, halo], 1)

    mva[1:17] = minv[...] * mb[...]
    sweep(mva, mvb, mb, mwx, mwy, mwz, minv, 16)
    sweep(mvb, mva, mb, mwx, mwy, mwz, minv, 16)

    def rest(x, before):
        _, r, fx = residual(mva, mb, mwx, mwy, mwz, x, before)
        mvb[x + 1] = r
        mid_pre_o[x] = mva[x + 1, 8:16]
        return fx

    lax.fori_loop(0, 16, rest, mwx[0] * (0.0 - mva[1]), unroll=16)

    rhs = pick_lanes(pick_rows(fold_low(0, 4), mvb[1:17].reshape(16 * YM, ZM)), squeeze()).reshape(4, 8, CZ)
    depth = iota((8, CZ), 1) % 32
    top = depth == 0
    r, d, e, edge = gather(rhs), low[0], low[1], low[2]
    v = jnp.where(top, 1.0, 0.0)
    w = jnp.where(depth == 31, 1.0, 0.0)
    for k in range(5):
        s = 1 << k
        back = CZ - s
        inv = 1.0 / d
        t = e * inv
        alpha = e * pltpu.roll(inv, s, 1)
        r, v, w = [
            q + alpha * pltpu.roll(q, s, 1) + pltpu.roll(t * q, back, 1) for q in (r, v, w)
        ]
        d = d - alpha * e - pltpu.roll(t * e, back, 1)
        e = alpha * pltpu.roll(e, s, 1)
    inv = 1.0 / d
    r, v, w = r * inv, v * inv, w * inv
    block_o[0] = r
    block_o[1] = v
    block_o[2] = w
    packed = jnp.where((depth < 3) | (depth >= 29), r, 0.0)
    packed = jnp.where((depth >= 3) & (depth < 6), pltpu.roll(v, 3, 1), packed)
    packed = jnp.where((depth >= 26) & (depth < 29), pltpu.roll(v, CZ - 3, 1), packed)
    packed = jnp.where((depth >= 6) & (depth < 9), pltpu.roll(w, 6, 1), packed)
    packed = jnp.where((depth >= 23) & (depth < 26), pltpu.roll(w, CZ - 6, 1), packed)
    packed = jnp.where(depth == 9, pltpu.roll(edge, 9, 1), packed)
    for p in range(16):
        low_o[p] = packed


def solve_kernel(rec, block, mid_pre, mid_rhs, out, up, down):
    gz = lax.axis_index("gz")
    lane = iota((8, CZ), 1)
    depth = lane % 32

    def take(v, at):
        return pltpu.roll(v, (CZ - at) % CZ, 1) if at else v

    def parts(offset):
        p = gz + offset
        v = rec[jnp.clip(p, 0, 15)]
        low = take(v, 0), take(v, 3), take(v, 6)
        high = take(v, 31), take(v, 28), take(v, 25)
        return v, low, high, jnp.where((p >= 0) & (p <= 15), take(v, 9), 0.0)

    every = {k: parts(k) for k in range(-4, 5)}
    zero = jnp.zeros((8, CZ), jnp.float32)

    a, b = {-5: zero}, {-5: zero}
    f, g = {}, {}
    for k in range(-4, 1):
        _, (y0, v0, w0), (y1, v1, w1), e = every[k]
        left, more = e * a[k - 1], e * e * b[k - 1]
        den = 1.0 / (1.0 - v0 * more)
        f[k] = (y0 + v0 * left) * den
        g[k] = w0 * den
        a[k] = y1 + v1 * (left + more * f[k])
        b[k] = w1 + v1 * (more * g[k])
    ra, rb = {5: zero}, {5: zero}
    rf, rg = {}, {}
    e_next = zero
    for k in range(4, 0, -1):
        _, (y0, v0, w0), (y1, v1, w1), e = every[k]
        right, more = e_next * ra[k + 1], e_next * e_next * rb[k + 1]
        den = 1.0 / (1.0 - w1 * more)
        rf[k] = (y1 + w1 * right) * den
        rg[k] = v1 * den
        ra[k] = y0 + w0 * (right + more * rf[k])
        rb[k] = v0 + w0 * (more * rg[k])
        e_next = e
    e0, e1 = every[0][3], every[1][3]
    last = (a[0] + b[0] * e1 * ra[1]) / (1.0 - b[0] * e1 * e1 * rb[1])
    right = e1 * (ra[1] + rb[1] * (e1 * last))
    first = f[0] + g[0] * right
    left = e0 * (a[-1] + b[-1] * (e0 * first))
    before = f[-1] + g[-1] * (e0 * first)
    em = every[-1][3]
    left_m, right_m = em * (a[-2] + b[-2] * (em * before)), e0 * first
    after = rf[1] + rg[1] * (e1 * last)
    ep = every[2][3]
    left_p, right_p = e1 * last, ep * (ra[2] + rb[2] * (ep * after))

    ends = jnp.concatenate([left, right, left_m, right_m, left_p, right_p], 0)
    ends = jnp.where(iota((48, CZ), 1) % 32 == 0, ends, 0.0)
    copy = (iota((CZ, CZ), 1) // 32 * 32 == iota((CZ, CZ), 0)).astype(jnp.float32)
    ends = pick_lanes(ends, copy).reshape(6, 8, CZ)
    own = block[0] + block[1] * ends[0] + block[2] * ends[1]
    v = every[-1][0]
    low = v + pltpu.roll(v, 3, 1) * ends[2] + pltpu.roll(v, 6, 1) * ends[3]
    low = jnp.where((depth >= 29) & (gz > 0), low, 0.0)
    v = every[1][0]
    high = v + pltpu.roll(v, CZ - 3, 1) * ends[4] + pltpu.roll(v, CZ - 6, 1) * ends[5]
    high = jnp.where((depth < 3) & (gz < 15), high, 0.0)

    rows = []
    for y in range(4):
        part = jnp.where(lane < 32, take(own, 32 * y), 0.0)
        part = jnp.where((lane >= 32) & (lane < 64), take(high, (32 * y - 32) % CZ), part)
        part = jnp.where(lane >= 96, take(low, (32 * y + 32) % CZ), part)
        rows.append(part)
    rows = jnp.concatenate(rows, 0)
    k, m = iota((CZ, ZM), 0), iota((CZ, ZM), 1)
    spread_z = (k == jnp.where(m < 96, m // 2, m // 2 + 64)).astype(jnp.float32)
    to, frm = iota((128, 32), 0), iota((128, 32), 1)
    spread = ((to // 16 == frm % 8) & ((to % 8) // 2 == frm // 8)).astype(jnp.float32)
    mid = mid_pre[...] + pick_rows(spread, pick_lanes(rows, spread_z)).reshape(16, 8, ZM)
    out[...] = mid
    for x in range(16):
        up[6 * x : 6 * x + 5] = mid[x, 3:]
        up[6 * x + 5 : 6 * x + 6] = mid_rhs[x, 12:13]
        down[6 * x : 6 * x + 5] = mid[x, :5]
        down[6 * x + 5 : 6 * x + 6] = mid_rhs[x, 11:12]


def second_kernel(
    scale, mid, mid_p, mid_n, mid_rhs, mwx, mwy, mwz, minv, src_w, pre_w, c, wx, wy, wz, inv, se,
    adj, grad,
    mb, mva, mvb, sp, va, vb,
):
    gx = lax.axis_index("gx")
    mid_zero = jnp.zeros((YM, ZM), jnp.float32)
    none = jnp.zeros((8, ZM), jnp.float32)
    mb[...] = mid_rhs[...]
    for x in range(16):
        mb[x, 4:5] = mid_p[6 * x + 5 : 6 * x + 6]
        mb[x, 19:20] = mid_n[6 * x + 5 : 6 * x + 6]
    for ref in (mva, mvb):
        for at in (0, 1, 18, 19):
            ref[at] = mid_zero
    for x in range(16):
        mva[x + 2, 0:8] = none
        mva[x + 2, 16:24] = none
        mva[x + 2, 3:8] = mid_p[6 * x : 6 * x + 5]
        mva[x + 2, 8:16] = mid[x]
        mva[x + 2, 16:21] = mid_n[6 * x : 6 * x + 5]
    a, o = mva.at[1:19], mvb.at[1:19]
    sweep(a, o, mb, mwx, mwy, mwz, minv, 16)
    sweep(o, a, mb, mwx, mwy, mwz, minv, 16)
    sweep(a, o, mb, mwx, mwy, mwz, minv, 16)

    zero = jnp.zeros((YW, ZE), jnp.float32)
    for ref in (va, vb):
        ref[0] = zero
        ref[XW + 1] = zero
    spread_z = (iota((ZM, ZE), 1) // 2 == iota((ZM, ZE), 0)).astype(jnp.float32)
    spread_y = ((iota((YW, YM), 0) + 12) // 2 == iota((YW, YM), 1)).astype(jnp.float32)
    near = mvb[pl.ds(4 * gx, 8)]
    sp[...] = pick_lanes(near.reshape(8 * YM, ZM), spread_z).reshape(8, YM, ZE)
    for m in range(8):
        more = pick_rows(spread_y, sp[m])
        for x in (2 * m, 2 * m + 1):
            va[x + 1] = pre_w[x] + more
    sweep(va, vb, src_w, wx, wy, wz, inv, XW)
    sweep(vb, va, src_w, wx, wy, wz, inv, XW)
    sweep(va, vb, src_w, wx, wy, wz, inv, XW)

    def product(f, one, two, sone, stwo):
        return f * (one - two) * (sone - stwo)

    def half(one, two):
        return jnp.where(jnp.minimum(one, two) == 0.0, 1.0, 0.5)

    lane = iota((YW, CZ), 1)

    def terms(i, carry):
        before, acc = carry
        v, k, s = vb[i + 5], c[i + 4], se[i + 1]
        px = product(half(k, c[i + 5]), v, vb[i + 6], s, se[i + 2])
        py = product(half(k, nxt(k, 0)), v, nxt(v, 0), s, nxt(s, 0))
        pz = product(half(k, nxt(k, 1)), v, nxt(v, 1), s, nxt(s, 1))
        both = k * (px + before + py + prv(py, 0) + pz + prv(pz, 1))
        part = jnp.sum(both[:, :CZ], axis=1, keepdims=True)
        acc = jnp.where(lane == i, part, acc)
        adj[i] = pltpu.roll(v, YW - 4, 0)[:CY, :CZ]
        return px, acc

    first = product(half(c[3], c[4]), vb[4], vb[5], se[0], se[1])
    _, acc = lax.fori_loop(
        0, CX, terms, (first, jnp.zeros((YW, CZ), jnp.float32)), unroll=8
    )
    grad[...] = pltpu.roll(acc, YW - 4, 0)[:CY] * scale


def f32(*shape):
    return jax.ShapeDtypeStruct(shape, jnp.float32)


def vm(*shape):
    return pltpu.VMEM(shape, jnp.float32)


def params():
    return pltpu.CompilerParams(vmem_limit_bytes=16 << 20)


def both_ways(up, down, axis):
    count = lax.axis_size(axis)
    higher = [(i, i + 1) for i in range(count - 1)]
    lower = [(j, i) for i, j in higher]
    return lax.ppermute(up, axis, higher), lax.ppermute(down, axis, lower)


def per_device(source, state, log_coef, lateral, owners):
    block = f32(CX, CY, CZ)
    far = pl.BlockSpec(memory_space=pltpu.HBM)
    mine, down, up = pl.pallas_call(
        pack_z_kernel,
        out_shape=(f32(3 * CX + 2, CY, CZ), block, block),
        in_specs=[far] * 5,
        scratch_shapes=[
            pltpu.SMEM((1, 1, 16), jnp.int32),
            vm(CX, CY, CZ), vm(CX, CY, CZ), vm(CX, CY), vm(CX, CY, CZ),
            pltpu.SemaphoreType.DMA((5,)),
        ],
        compiler_params=params(),
        name="pack_z",
    )(*[
        pltpu.with_memory_space_constraint(v, pltpu.HBM)
        for v in (owners, source, log_coef, lateral, state)
    ])
    gz, count = lax.axis_index("gz"), lax.axis_size("gz")
    before = lax.ppermute(up, "gz", [(i, (i + 1) % count) for i in range(count)])
    after = lax.ppermute(down, "gz", [(i, (i - 1) % count) for i in range(count)])
    halo = jnp.where(gz > 0, before, 0.0) + jnp.where(gz < count - 1, after, 0.0)
    mine = lax.dynamic_update_slice(mine, halo, (2 * CX, 0, 0))
    g = lax.all_gather(mine, "gx")
    fine, fine1, fine2 = (32, YE, ZE), (33, YE, ZE), (34, YE, ZE)
    mid, mid1, mid2 = (16, YM, ZM), (17, YM, ZM), (18, YM, ZM)
    win, win1, win2 = (XW, YW, ZE), (XW + 1, YW, ZE), (XW + 2, YW, ZE)
    c_rows, s_rows = f32(440, CZ), f32(392, CZ)
    c_up, c_down, s_up, s_down = pl.pallas_call(
        pack_y_kernel,
        out_shape=(c_rows, c_rows, s_rows, s_rows),
        compiler_params=params(),
        name="pack_y",
    )(g, state)
    cp, cn = both_ways(c_up, c_down, "gy")
    yp, yn = both_ways(s_up, s_down, "gy")
    wx, wy, wz, inv, c_w, wx_w, wy_w, wz_w, inv_w, mwx, mwy, mwz, minv, low = pl.pallas_call(
        coef_kernel,
        out_shape=(
            f32(*fine1), f32(*fine), f32(*fine), f32(*fine),
            f32(*win), f32(*win1), f32(*win), f32(*win), f32(*win),
            f32(*mid1), f32(*mid), f32(*mid), f32(*mid), f32(3, 8, CZ),
        ),
        scratch_shapes=[vm(*fine2), vm(16, YM, ZE), vm(*mid2)],
        compiler_params=params(),
        name="coef",
    )(g, cp, cn)
    src_w, pre_w, se, mid_pre, mid_rhs, ends, block_s = pl.pallas_call(
        first_kernel,
        out_shape=(
            f32(*win), f32(*win), f32(CX + 2, YW, ZE),
            f32(16, 8, ZM), f32(*mid), f32(16, 8, CZ), f32(3, 8, CZ),
        ),
        scratch_shapes=[
            vm(*fine1), vm(*fine2), vm(*fine2), vm(16, YM, ZE), vm(*mid2), vm(*mid2),
        ],
        compiler_params=params(),
        name="first",
    )(g, cp, cn, yp, yn, state, wx, wy, wz, inv, mwx, mwy, mwz, minv, low)

    rec = lax.all_to_all(ends, "gz", 0, 0, tiled=True)
    tile = f32(16, 8, ZM)
    mid_init, up, down = pl.pallas_call(
        solve_kernel, out_shape=(tile, f32(96, ZM), f32(96, ZM)), compiler_params=params(), name="solve"
    )(rec, block_s, mid_pre, mid_rhs)
    mid_p, mid_n = both_ways(up, down, "gy")

    scale = -1.0 / math.sqrt(source.shape[2] * count)
    adj, grad = pl.pallas_call(
        functools.partial(second_kernel, scale),
        out_shape=(f32(CX, CY, CZ), f32(CY, CZ)),
        scratch_shapes=[
            vm(*mid), vm(20, YM, ZM), vm(20, YM, ZM), vm(8, YM, ZE), vm(*win2), vm(*win2),
        ],
        compiler_params=params(),
        name="second",
    )(mid_init, mid_p, mid_n, mid_rhs, mwx, mwy, mwz, minv,
      src_w, pre_w, c_w, wx_w, wy_w, wz_w, inv_w, se)
    sums = lax.all_to_all(grad, "gz", 0, 0, tiled=True)
    return adj, jnp.sum(sums[:, :CX], axis=0)[:, None]


def solution(mesh):
    placed = (
        P("gx", "gy", "gz"),
        P("gx", "gy", "gz"),
        P("gx", "gy", "gz"),
        P("gx", "gy"),
        P("gx", "gy", None),
    )
    return jax.shard_map(
        per_device,
        mesh=mesh,
        in_specs=placed,
        out_specs=(P("gx", "gy", "gz"), P("gx", ("gy", "gz"))),
        check_vma=False,
    )
```

```python
import functools
import math

import jax
import jax.numpy as jnp
from jax import lax
from jax.experimental import pallas as pl
from jax.experimental.pallas import tpu as pltpu
from jax.sharding import PartitionSpec as P

CX, CY, CZ = 8, 16, 128
ANISO = 200.0
OMEGA = 0.8
HC, HS = 10, 9
Y0 = 12
HZ = 18
YE = CY + 2 * Y0
ZE = 2 * CZ
TILES = 11
YM = 24
ZM = CZ
XW = CX + 8
YW = CY + 8
HIGHEST = lax.Precision.HIGHEST


def iota(shape, dim):
    return lax.broadcasted_iota(jnp.int32, shape, dim)


def mm(a, b):
    return jnp.dot(a, b, precision=HIGHEST, preferred_element_type=jnp.float32)


def split(v, axis):
    high = v.astype(jnp.bfloat16)
    v = v - high.astype(jnp.float32)
    mid = v.astype(jnp.bfloat16)
    low = (v - mid.astype(jnp.float32)).astype(jnp.bfloat16)
    return jnp.concatenate([high, mid, low], axis)


def pick_rows(sel, v):
    out = jnp.dot(sel.astype(jnp.bfloat16), split(v, 1), preferred_element_type=jnp.float32)
    n = v.shape[1]
    return out[:, :n] + (out[:, n : 2 * n] + out[:, 2 * n :])


def pick_lanes(v, sel):
    out = jnp.dot(split(v, 0), sel.astype(jnp.bfloat16), preferred_element_type=jnp.float32)
    n = v.shape[0]
    return out[:n] + (out[n : 2 * n] + out[2 * n :])


def nxt(v, axis):
    return pltpu.roll(v, v.shape[axis] - 1, axis)


def prv(v, axis):
    return pltpu.roll(v, 1, axis)


def face(a, b):
    both = a + b
    return jnp.where(jnp.minimum(a, b) == 0.0, both, 0.5 * both)


def unroll(planes):
    return 16 if planes == 16 else 8


def make_weights(c, wx, wy, wz, inv, planes, scale):
    wx[0] = scale * face(c[0], c[1])

    def step(x, carry):
        here = c[x + 1]
        fx = scale * face(here, c[x + 2])
        fy = scale * face(here, nxt(here, 0))
        fz = (scale * ANISO) * face(here, nxt(here, 1))
        wx[x + 1] = fx
        wy[x] = fy
        wz[x] = fz
        total = fx + wx[x] + fy + prv(fy, 0) + fz + prv(fz, 1)
        inv[x] = jnp.where(here > 0.0, OMEGA / total, 0.0)
        return carry

    lax.fori_loop(0, planes, step, 0, unroll=unroll(planes))


def residual(v, b, wx, wy, wz, x, before):
    here = v[x + 1]
    fx = wx[x + 1] * (here - v[x + 2])
    fy = wy[x] * (here - nxt(here, 0))
    fz = wz[x] * (here - nxt(here, 1))
    flow = (fx - before) + (fy - prv(fy, 0)) + (fz - prv(fz, 1))
    return here, b[x] - flow, fx


def sweep(v, out, b, wx, wy, wz, inv, planes):
    def step(x, before):
        here, rest, fx = residual(v, b, wx, wy, wz, x, before)
        out[x + 1] = here + inv[x] * rest
        return fx

    lax.fori_loop(0, planes, step, wx[0] * (0.0 - v[1]), unroll=unroll(planes))


def first_sweeps(out, b, wx, wy, wz, inv, planes):
    def step(x, carry):
        before, here = carry
        after = inv[jnp.minimum(x + 1, planes - 1)] * b[x + 1]
        fx = wx[x + 1] * (here - after)
        fy = wy[x] * (here - nxt(here, 0))
        fz = wz[x] * (here - nxt(here, 1))
        flow = (fx - before) + (fy - prv(fy, 0)) + (fz - prv(fz, 1))
        out[x + 1] = here + inv[x] * (b[x] - flow)
        return fx, after

    here = inv[0] * b[0]
    lax.fori_loop(0, planes, step, (wx[0] * (0.0 - here), here), unroll=unroll(planes))


def pack_z_kernel(
    line_far, src_far, log_coef_far, lateral_far, state_far, mine, down, up,
    line, src, log_coef, lateral, state, sems,
):
    copies = [
        pltpu.make_async_copy(far, near, sems.at[i])
        for i, (far, near) in enumerate(
            (
                (lateral_far, lateral), (log_coef_far, log_coef), (src_far, src),
                (state_far, state), (line_far, line),
            )
        )
    ]
    for copy in copies:
        copy.start()
    copies[0].wait()
    gz = lax.axis_index("gz")
    pick = (iota((CX * CY, CX), 0) // CY == iota((CX * CY, CX), 1)).astype(jnp.float32)
    rows = pick_rows(pick, lateral[...])
    own = iota((CX * CY, CY), 0) % CY == iota((CX * CY, CY), 1)
    rows = jnp.sum(jnp.where(own, rows, 0.0), axis=1, keepdims=True)
    rows = jnp.broadcast_to(rows, (CX * CY, CZ)).reshape(CX, CY, CZ)
    for copy in copies[1:]:
        copy.wait()
    cut = (line[0, 0, gz] != line[0, 0, jnp.minimum(gz + 1, 15)]).astype(jnp.float32)
    c = jnp.exp(log_coef[...] + rows)
    s = src[...]
    mine[0:CX] = s
    mine[CX : 2 * CX] = c
    mine[3 * CX] = state[0]
    mine[3 * CX + 1] = state[CX - 1]
    lane = iota((CX, CY, CZ), 2)
    k = pltpu.roll(c, 64, 2)
    t = pltpu.roll(state[...], 32, 2)
    zero = jnp.zeros_like(s)
    far = CZ - HZ
    coef = jnp.where((lane >= 64) & (lane < 64 + HZ), k, zero)
    down[...] = jnp.where(lane < HZ, s, jnp.where(lane == 32, t, coef))
    coef = jnp.where((lane >= far - 64) & (lane < 64), k, zero)
    coef = jnp.where(lane == 20, cut, coef)
    up[...] = jnp.where(lane >= far, s, jnp.where(lane == 31, t, coef))


def pack_y_kernel(g, state, c_up, c_down, s_up, s_down):
    lane = iota((CY, CZ), 1)
    planes = 4 * CX + TILES
    for coef, h, up, down in ((1, HC, c_up, c_down), (0, HS, s_up, s_down)):

        def put(n, plane):
            up[h * n : h * n + h] = plane[CY - h :]
            down[h * n : h * n + h] = plane[:h]

        for s in range(4):
            for i in range(CX):
                put(CX * s + i, g[s, CX * coef + i])
        for t in range(TILES):
            plane = jnp.zeros((CY, CZ), jnp.float32)
            for x in range(3 * t, min(3 * t + 3, 4 * CX)):
                off = 2 * HZ * (x % 3)
                move = off - 46 if coef else off + HZ
                halo = pltpu.roll(g[x // CX, 2 * CX + x % CX], move % CZ, 1)
                plane = jnp.where(lane >= off, halo, plane)
            put(4 * CX + t, plane)
        end = h * planes
        if coef:
            for i in range(CX):
                up[end + i : end + i + 1] = state[i, CY - 1 :]
                down[end + i : end + i + 1] = state[i, :1]
            end += CX
        none = jnp.zeros((up.shape[0] - end, CZ), jnp.float32)
        up[end:] = none
        down[end:] = none


def place(out, lanes, low, own, high):
    h = low.shape[0]
    out[Y0 - h : Y0, lanes] = low
    out[Y0 : Y0 + CY, lanes] = own
    out[Y0 + CY : Y0 + CY + h, lanes] = high


def edge_lanes(v, move):
    v = pltpu.roll(v, move % CZ, 1) if move % CZ else v
    lane = iota(v.shape, 1)
    return jnp.where((lane < HZ) | (lane >= CZ - HZ), v, 0.0)


def fill(out, g, yp, yn, x, coef):
    s, i = x // CX, x % CX
    none = jnp.zeros((8, ZE), jnp.float32)
    out[0:8] = none
    out[YE - 8 :] = none
    h = HC if coef else HS
    at = slice(h * x, h * x + h)
    place(out, LOW, yp[at], g[s, CX * coef + i], yn[at])
    n, move = 4 * CX + x // 3, CZ - HZ - 2 * HZ * (x % 3)
    at = slice(h * n, h * n + h)
    place(
        out, HIGH, edge_lanes(yp[at], move),
        edge_lanes(g[s, 2 * CX + i], 64 * coef), edge_lanes(yn[at], move),
    )


LOW, HIGH = slice(0, CZ), slice(CZ, ZE)


def window(gx, pairs, planes):
    nx = 4 * CX

    def keep(w, carry):
        for out, ref, shift, first in pairs:
            x = CX * gx - 4 + w - first
            inside = (x >= -first) & (x < nx)
            at = jnp.clip(x, -first, nx - 1) + shift
            out[w] = jnp.where(inside, ref[at, 8:32], 0.0)
        return carry

    lax.fori_loop(0, planes, keep, 0, unroll=8)


def fold_y():
    return (iota((YM, YE), 1) // 2 + 2 == iota((YM, YE), 0)).astype(jnp.float32)


def fold_z():
    return (iota((ZE, ZM), 0) // 2 == iota((ZE, ZM), 1)).astype(jnp.float32) * 0.125


def fold_low(first, count):
    shape = (8 * count, 16 * YM)
    to, frm = iota(shape, 0), iota(shape, 1)
    m, r = frm // YM, frm % YM
    return ((m // 2 == to % 8) & (r // 2 - 4 == to // 8 + first)).astype(jnp.float32) * 0.125


def squeeze():
    m, l = iota((ZM, CZ), 0), iota((ZM, CZ), 1)
    m = jnp.where(m < 96, m, m - 128)
    return ((m + 8) // 2 == l).astype(jnp.float32)


def gather(v):
    lane = iota((8, CZ), 1)
    out = pltpu.roll(v[0], CZ - 4, 1)
    for y in range(1, 4):
        out = jnp.where(lane >= 32 * y, pltpu.roll(v[y], 32 * y - 4, 1), out)
    return out


def coef_kernel(
    g, yp, yn,
    wx, wy, wz, inv, c_w, wx_w, wy_w, wz_w, inv_w, mwx, mwy, mwz, minv, low_o,
    c, t, mc,
):
    gx, gz = lax.axis_index("gx"), lax.axis_index("gz")
    zero = jnp.zeros((YE, ZE), jnp.float32)
    nx = 4 * CX
    c[0] = zero
    c[nx + 1] = zero
    for x in range(nx):
        fill(c.at[x + 1], g, yp, yn, x, 1)
    make_weights(c, wx, wy, wz, inv, nx, 1.0)
    rows = fold_y()

    def coarse(m, carry):
        t[m] = pick_rows(rows, c[2 * m + 1] + c[2 * m + 2])
        return carry

    lax.fori_loop(0, 16, coarse, 0, unroll=16)
    mid_zero = jnp.zeros((YM, ZM), jnp.float32)
    mc[0] = mid_zero
    mc[17] = mid_zero
    mc[1:17] = pick_lanes(t[...].reshape(16 * YM, ZE), fold_z()).reshape(16, YM, ZM)
    make_weights(mc, mwx, mwy, mwz, minv, 16, 0.25)
    window(gx, [(c_w, c, 1, 0), (wy_w, wy, 0, 0), (wz_w, wz, 0, 0), (inv_w, inv, 0, 0)], XW)
    window(gx, [(wx_w, wx, 1, 1)], XW + 1)

    low_c = pick_lanes(pick_rows(fold_low(-1, 6), mc[1:17].reshape(16 * YM, ZM)), squeeze())
    low_c = low_c.reshape(6, 8, CZ)
    here = low_c[1:5]
    row = iota((4, 8, CZ), 1)
    scale = 0.0625
    fx1 = scale * face(here, jnp.where(row < 7, nxt(here, 1), 0.0))
    fx0 = scale * face(here, jnp.where(row > 0, prv(here, 1), 0.0))
    fy1 = scale * face(here, low_c[2:6])
    fy0 = scale * face(here, low_c[0:4])
    fz = (scale * ANISO) * face(here, nxt(here, 2))
    lower = prv(fz, 2)
    total = fx1 + fx0 + fy1 + fy0 + fz + lower

    flag = pltpu.roll(g[3, 16, 0:8], CZ - 20, 1)
    row = iota((8, CZ), 0)
    for s in range(2, -1, -1):
        flag = jnp.where(row < 2 * s + 2, pltpu.roll(g[s, 16, 0:8], CZ - 20, 1), flag)
    flag = jnp.broadcast_to(flag[:, 0:1], (8, CZ))
    e = gather(lower)
    top = iota((8, CZ), 1) % 32 == 0
    low_o[0] = gather(total)
    low_o[1] = jnp.where(top, 0.0, e)
    low_o[2] = jnp.where(top & (flag == 0.0) & (gz > 0), e, 0.0)


def first_kernel(
    g, cp, cn, yp, yn, state, wx, wy, wz, inv, mwx, mwy, mwz, minv, low,
    src_w, pre_w, se, mid_pre_o, mb, low_o, block_o,
    b, va, vb, t, mva, mvb,
):
    gx = lax.axis_index("gx")
    zero = jnp.zeros((YE, ZE), jnp.float32)
    nx = 4 * CX
    for ref in (va, vb):
        ref[0] = zero
        ref[nx + 1] = zero
    for x in range(nx):
        fill(b.at[x], g, yp, yn, x, 0)
    b[nx] = zero
    first_sweeps(va, b, wx, wy, wz, inv, nx)
    sweep(va, vb, b, wx, wy, wz, inv, nx)

    rows = fold_y()

    def coarse(m, before):
        x = 2 * m
        _, one, fx = residual(vb, b, wx, wy, wz, x, before)
        _, two, fx = residual(vb, b, wx, wy, wz, x + 1, fx)
        t[m] = pick_rows(rows, one + two)
        return fx

    lax.fori_loop(0, 16, coarse, wx[0] * (0.0 - vb[1]), unroll=16)
    mb[...] = pick_lanes(t[...].reshape(16 * YM, ZE), fold_z()).reshape(16, YM, ZM)
    mid_zero = jnp.zeros((YM, ZM), jnp.float32)
    for ref in (mva, mvb):
        ref[0] = mid_zero
        ref[17] = mid_zero

    window(gx, [(src_w, b, 0, 0), (pre_w, vb, 1, 0)], XW)

    zero8 = jnp.zeros((8, CZ), jnp.float32)
    wide = jnp.zeros((YW, CZ), jnp.float32)
    row = iota((YW, CZ), 0)
    lane = iota((YW, CZ), 1)
    left = g[jnp.maximum(gx - 1, 0), 25]
    right = g[jnp.minimum(gx + 1, 3), 24]
    left = jnp.where(gx > 0, left, 0.0)
    right = jnp.where(gx < 3, right, 0.0)
    for at, plane in ((0, left), (9, right)):
        mid = pltpu.roll(jnp.concatenate([plane, zero8], 0), 4, 0)
        se[at] = jnp.concatenate([mid, wide], 1)
    for i in range(CX):
        mid = pltpu.roll(jnp.concatenate([state[i], zero8], 0), 4, 0)
        n = HC * (4 * CX + TILES) + i
        under, over = cp[n : n + 1], cn[n : n + 1]
        mid = jnp.where(row == 3, under, jnp.where(row == 20, over, mid))
        halo = pltpu.roll(jnp.concatenate([g[gx, 16 + i], zero8], 0), 4, 0)
        halo = pltpu.roll(halo, CZ - 32, 1)
        halo = jnp.where((lane == 0) | (lane == CZ - 1), halo, 0.0)
        se[i + 1] = jnp.concatenate([mid, halo], 1)

    mva[1:17] = minv[...] * mb[...]
    sweep(mva, mvb, mb, mwx, mwy, mwz, minv, 16)
    sweep(mvb, mva, mb, mwx, mwy, mwz, minv, 16)

    def rest(x, before):
        _, r, fx = residual(mva, mb, mwx, mwy, mwz, x, before)
        mvb[x + 1] = r
        mid_pre_o[x] = mva[x + 1, 8:16]
        return fx

    lax.fori_loop(0, 16, rest, mwx[0] * (0.0 - mva[1]), unroll=16)

    rhs = pick_lanes(pick_rows(fold_low(0, 4), mvb[1:17].reshape(16 * YM, ZM)), squeeze()).reshape(4, 8, CZ)
    depth = iota((8, CZ), 1) % 32
    top = depth == 0
    r, d, e, edge = gather(rhs), low[0], low[1], low[2]
    v = jnp.where(top, 1.0, 0.0)
    w = jnp.where(depth == 31, 1.0, 0.0)
    for k in range(5):
        s = 1 << k
        back = CZ - s
        inv = 1.0 / d
        t = e * inv
        alpha = e * pltpu.roll(inv, s, 1)
        r, v, w = [
            q + alpha * pltpu.roll(q, s, 1) + pltpu.roll(t * q, back, 1) for q in (r, v, w)
        ]
        d = d - alpha * e - pltpu.roll(t * e, back, 1)
        e = alpha * pltpu.roll(e, s, 1)
    inv = 1.0 / d
    r, v, w = r * inv, v * inv, w * inv
    block_o[0] = r
    block_o[1] = v
    block_o[2] = w
    packed = jnp.where((depth < 3) | (depth >= 29), r, 0.0)
    packed = jnp.where((depth >= 3) & (depth < 6), pltpu.roll(v, 3, 1), packed)
    packed = jnp.where((depth >= 26) & (depth < 29), pltpu.roll(v, CZ - 3, 1), packed)
    packed = jnp.where((depth >= 6) & (depth < 9), pltpu.roll(w, 6, 1), packed)
    packed = jnp.where((depth >= 23) & (depth < 26), pltpu.roll(w, CZ - 6, 1), packed)
    packed = jnp.where(depth == 9, pltpu.roll(edge, 9, 1), packed)
    for p in range(16):
        low_o[p] = packed


def solve_kernel(rec, block, mid_pre, mid_rhs, out, up, down):
    gz = lax.axis_index("gz")
    lane = iota((8, CZ), 1)
    depth = lane % 32

    def take(v, at):
        return pltpu.roll(v, (CZ - at) % CZ, 1) if at else v

    def parts(offset):
        p = gz + offset
        v = rec[jnp.clip(p, 0, 15)]
        low = take(v, 0), take(v, 3), take(v, 6)
        high = take(v, 31), take(v, 28), take(v, 25)
        return v, low, high, jnp.where((p >= 0) & (p <= 15), take(v, 9), 0.0)

    every = {k: parts(k) for k in range(-4, 5)}
    zero = jnp.zeros((8, CZ), jnp.float32)

    a, b = {-5: zero}, {-5: zero}
    f, g = {}, {}
    for k in range(-4, 1):
        _, (y0, v0, w0), (y1, v1, w1), e = every[k]
        left, more = e * a[k - 1], e * e * b[k - 1]
        den = 1.0 / (1.0 - v0 * more)
        f[k] = (y0 + v0 * left) * den
        g[k] = w0 * den
        a[k] = y1 + v1 * (left + more * f[k])
        b[k] = w1 + v1 * (more * g[k])
    ra, rb = {5: zero}, {5: zero}
    rf, rg = {}, {}
    e_next = zero
    for k in range(4, 0, -1):
        _, (y0, v0, w0), (y1, v1, w1), e = every[k]
        right, more = e_next * ra[k + 1], e_next * e_next * rb[k + 1]
        den = 1.0 / (1.0 - w1 * more)
        rf[k] = (y1 + w1 * right) * den
        rg[k] = v1 * den
        ra[k] = y0 + w0 * (right + more * rf[k])
        rb[k] = v0 + w0 * (more * rg[k])
        e_next = e
    e0, e1 = every[0][3], every[1][3]
    last = (a[0] + b[0] * e1 * ra[1]) / (1.0 - b[0] * e1 * e1 * rb[1])
    right = e1 * (ra[1] + rb[1] * (e1 * last))
    first = f[0] + g[0] * right
    left = e0 * (a[-1] + b[-1] * (e0 * first))
    before = f[-1] + g[-1] * (e0 * first)
    em = every[-1][3]
    left_m, right_m = em * (a[-2] + b[-2] * (em * before)), e0 * first
    after = rf[1] + rg[1] * (e1 * last)
    ep = every[2][3]
    left_p, right_p = e1 * last, ep * (ra[2] + rb[2] * (ep * after))

    ends = jnp.concatenate([left, right, left_m, right_m, left_p, right_p], 0)
    ends = jnp.where(iota((48, CZ), 1) % 32 == 0, ends, 0.0)
    copy = (iota((CZ, CZ), 1) // 32 * 32 == iota((CZ, CZ), 0)).astype(jnp.float32)
    ends = pick_lanes(ends, copy).reshape(6, 8, CZ)
    own = block[0] + block[1] * ends[0] + block[2] * ends[1]
    v = every[-1][0]
    low = v + pltpu.roll(v, 3, 1) * ends[2] + pltpu.roll(v, 6, 1) * ends[3]
    low = jnp.where((depth >= 29) & (gz > 0), low, 0.0)
    v = every[1][0]
    high = v + pltpu.roll(v, CZ - 3, 1) * ends[4] + pltpu.roll(v, CZ - 6, 1) * ends[5]
    high = jnp.where((depth < 3) & (gz < 15), high, 0.0)

    rows = []
    for y in range(4):
        part = jnp.where(lane < 32, take(own, 32 * y), 0.0)
        part = jnp.where((lane >= 32) & (lane < 64), take(high, (32 * y - 32) % CZ), part)
        part = jnp.where(lane >= 96, take(low, (32 * y + 32) % CZ), part)
        rows.append(part)
    rows = jnp.concatenate(rows, 0)
    k, m = iota((CZ, ZM), 0), iota((CZ, ZM), 1)
    spread_z = (k == jnp.where(m < 96, m // 2, m // 2 + 64)).astype(jnp.float32)
    to, frm = iota((128, 32), 0), iota((128, 32), 1)
    spread = ((to // 16 == frm % 8) & ((to % 8) // 2 == frm // 8)).astype(jnp.float32)
    mid = mid_pre[...] + pick_rows(spread, pick_lanes(rows, spread_z)).reshape(16, 8, ZM)
    out[...] = mid
    for x in range(16):
        up[6 * x : 6 * x + 5] = mid[x, 3:]
        up[6 * x + 5 : 6 * x + 6] = mid_rhs[x, 12:13]
        down[6 * x : 6 * x + 5] = mid[x, :5]
        down[6 * x + 5 : 6 * x + 6] = mid_rhs[x, 11:12]


def second_kernel(
    scale, mid, mid_p, mid_n, mid_rhs, mwx, mwy, mwz, minv, src_w, pre_w, c, wx, wy, wz, inv, se,
    adj, grad,
    mb, mva, mvb, sp, va, vb,
):
    gx = lax.axis_index("gx")
    mid_zero = jnp.zeros((YM, ZM), jnp.float32)
    none = jnp.zeros((8, ZM), jnp.float32)
    mb[...] = mid_rhs[...]
    for x in range(16):
        mb[x, 4:5] = mid_p[6 * x + 5 : 6 * x + 6]
        mb[x, 19:20] = mid_n[6 * x + 5 : 6 * x + 6]
    for ref in (mva, mvb):
        for at in (0, 1, 18, 19):
            ref[at] = mid_zero
    for x in range(16):
        mva[x + 2, 0:8] = none
        mva[x + 2, 16:24] = none
        mva[x + 2, 3:8] = mid_p[6 * x : 6 * x + 5]
        mva[x + 2, 8:16] = mid[x]
        mva[x + 2, 16:21] = mid_n[6 * x : 6 * x + 5]
    a, o = mva.at[1:19], mvb.at[1:19]
    sweep(a, o, mb, mwx, mwy, mwz, minv, 16)
    sweep(o, a, mb, mwx, mwy, mwz, minv, 16)
    sweep(a, o, mb, mwx, mwy, mwz, minv, 16)

    zero = jnp.zeros((YW, ZE), jnp.float32)
    for ref in (va, vb):
        ref[0] = zero
        ref[XW + 1] = zero
    spread_z = (iota((ZM, ZE), 1) // 2 == iota((ZM, ZE), 0)).astype(jnp.float32)
    spread_y = ((iota((YW, YM), 0) + 12) // 2 == iota((YW, YM), 1)).astype(jnp.float32)
    near = mvb[pl.ds(4 * gx, 8)]
    sp[...] = pick_lanes(near.reshape(8 * YM, ZM), spread_z).reshape(8, YM, ZE)
    for m in range(8):
        more = pick_rows(spread_y, sp[m])
        for x in (2 * m, 2 * m + 1):
            va[x + 1] = pre_w[x] + more
    sweep(va, vb, src_w, wx, wy, wz, inv, XW)
    sweep(vb, va, src_w, wx, wy, wz, inv, XW)
    sweep(va, vb, src_w, wx, wy, wz, inv, XW)

    def product(f, one, two, sone, stwo):
        return f * (one - two) * (sone - stwo)

    def half(one, two):
        return jnp.where(jnp.minimum(one, two) == 0.0, 1.0, 0.5)

    lane = iota((YW, CZ), 1)

    def terms(i, carry):
        before, acc = carry
        v, k, s = vb[i + 5], c[i + 4], se[i + 1]
        px = product(half(k, c[i + 5]), v, vb[i + 6], s, se[i + 2])
        py = product(half(k, nxt(k, 0)), v, nxt(v, 0), s, nxt(s, 0))
        pz = product(half(k, nxt(k, 1)), v, nxt(v, 1), s, nxt(s, 1))
        both = k * (px + before + py + prv(py, 0) + pz + prv(pz, 1))
        part = jnp.sum(both[:, :CZ], axis=1, keepdims=True)
        acc = jnp.where(lane == i, part, acc)
        adj[i] = pltpu.roll(v, YW - 4, 0)[:CY, :CZ]
        return px, acc

    first = product(half(c[3], c[4]), vb[4], vb[5], se[0], se[1])
    _, acc = lax.fori_loop(
        0, CX, terms, (first, jnp.zeros((YW, CZ), jnp.float32)), unroll=8
    )
    grad[...] = pltpu.roll(acc, YW - 4, 0)[:CY] * scale


def f32(*shape):
    return jax.ShapeDtypeStruct(shape, jnp.float32)


def vm(*shape):
    return pltpu.VMEM(shape, jnp.float32)


def params():
    return pltpu.CompilerParams(vmem_limit_bytes=16 << 20)


def both_ways(up, down, axis):
    count = lax.axis_size(axis)
    higher = [(i, i + 1) for i in range(count - 1)]
    lower = [(j, i) for i, j in higher]
    return lax.ppermute(up, axis, higher), lax.ppermute(down, axis, lower)


def per_device(source, state, log_coef, lateral, owners):
    block = f32(CX, CY, CZ)
    far = pl.BlockSpec(memory_space=pltpu.HBM)
    mine, down, up = pl.pallas_call(
        pack_z_kernel,
        out_shape=(f32(3 * CX + 2, CY, CZ), block, block),
        in_specs=[far] * 5,
        scratch_shapes=[
            pltpu.SMEM((1, 1, 16), jnp.int32),
            vm(CX, CY, CZ), vm(CX, CY, CZ), vm(CX, CY), vm(CX, CY, CZ),
            pltpu.SemaphoreType.DMA((5,)),
        ],
        compiler_params=params(),
        name="pack_z",
    )(*[
        pltpu.with_memory_space_constraint(v, pltpu.HBM)
        for v in (owners, source, log_coef, lateral, state)
    ])
    gz, count = lax.axis_index("gz"), lax.axis_size("gz")
    before = lax.ppermute(up, "gz", [(i, (i + 1) % count) for i in range(count)])
    after = lax.ppermute(down, "gz", [(i, (i - 1) % count) for i in range(count)])
    halo = jnp.where(gz > 0, before, 0.0) + jnp.where(gz < count - 1, after, 0.0)
    mine = lax.dynamic_update_slice(mine, halo, (2 * CX, 0, 0))
    g = lax.all_gather(mine, "gx")
    fine, fine1, fine2 = (32, YE, ZE), (33, YE, ZE), (34, YE, ZE)
    mid, mid1, mid2 = (16, YM, ZM), (17, YM, ZM), (18, YM, ZM)
    win, win1, win2 = (XW, YW, ZE), (XW + 1, YW, ZE), (XW + 2, YW, ZE)
    c_rows, s_rows = f32(440, CZ), f32(392, CZ)
    c_up, c_down, s_up, s_down = pl.pallas_call(
        pack_y_kernel,
        out_shape=(c_rows, c_rows, s_rows, s_rows),
        compiler_params=params(),
        name="pack_y",
    )(g, state)
    cp, cn = both_ways(c_up, c_down, "gy")
    yp, yn = both_ways(s_up, s_down, "gy")
    wx, wy, wz, inv, c_w, wx_w, wy_w, wz_w, inv_w, mwx, mwy, mwz, minv, low = pl.pallas_call(
        coef_kernel,
        out_shape=(
            f32(*fine1), f32(*fine), f32(*fine), f32(*fine),
            f32(*win), f32(*win1), f32(*win), f32(*win), f32(*win),
            f32(*mid1), f32(*mid), f32(*mid), f32(*mid), f32(3, 8, CZ),
        ),
        scratch_shapes=[vm(*fine2), vm(16, YM, ZE), vm(*mid2)],
        compiler_params=params(),
        name="coef",
    )(g, cp, cn)
    src_w, pre_w, se, mid_pre, mid_rhs, ends, block_s = pl.pallas_call(
        first_kernel,
        out_shape=(
            f32(*win), f32(*win), f32(CX + 2, YW, ZE),
            f32(16, 8, ZM), f32(*mid), f32(16, 8, CZ), f32(3, 8, CZ),
        ),
        scratch_shapes=[
            vm(*fine1), vm(*fine2), vm(*fine2), vm(16, YM, ZE), vm(*mid2), vm(*mid2),
        ],
        compiler_params=params(),
        name="first",
    )(g, cp, cn, yp, yn, state, wx, wy, wz, inv, mwx, mwy, mwz, minv, low)

    rec = lax.all_to_all(ends, "gz", 0, 0, tiled=True)
    tile = f32(16, 8, ZM)
    mid_init, up, down = pl.pallas_call(
        solve_kernel, out_shape=(tile, f32(96, ZM), f32(96, ZM)), compiler_params=params(), name="solve"
    )(rec, block_s, mid_pre, mid_rhs)
    mid_p, mid_n = both_ways(up, down, "gy")

    scale = -1.0 / math.sqrt(source.shape[2] * count)
    adj, grad = pl.pallas_call(
        functools.partial(second_kernel, scale),
        out_shape=(f32(CX, CY, CZ), f32(CY, CZ)),
        scratch_shapes=[
            vm(*mid), vm(20, YM, ZM), vm(20, YM, ZM), vm(8, YM, ZE), vm(*win2), vm(*win2),
        ],
        compiler_params=params(),
        name="second",
    )(mid_init, mid_p, mid_n, mid_rhs, mwx, mwy, mwz, minv,
      src_w, pre_w, c_w, wx_w, wy_w, wz_w, inv_w, se)
    sums = lax.all_to_all(grad, "gz", 0, 0, tiled=True)
    return adj, jnp.sum(sums[:, :CX], axis=0)[:, None]


def solution(mesh):
    placed = (
        P("gx", "gy", "gz"),
        P("gx", "gy", "gz"),
        P("gx", "gy", "gz"),
        P("gx", "gy"),
        P("gx", "gy", None),
    )
    return jax.shard_map(
        per_device,
        mesh=mesh,
        in_specs=placed,
        out_specs=(P("gx", "gy", "gz"), P("gx", ("gy", "gz"))),
        check_vma=False,
    )
```
